512 devices in a mesh: kv: 4 (over x), blk: 128 (over z, y, core).
Axes of the slice: x: 4, y: 8, z: 8, core: 2. Of those that a mesh axis runs over, the one named last changes fastest.
Arguments:
- prefix_pool: bfloat16 [4, 3072, 64, 512], P('kv', 'blk'), may hold values from -6 to 6
- slot_page: int32 [3072], P('blk'), may hold values from 0 to 3071, as said below
- prompt_len: int32 [48], replicated, may hold values from 1 to 32768, 193536 in all
- request_ids: int32 [768], replicated, may hold values from 0 to 767, each once
- tail_len: int32 [768], P('blk'), may hold values from 1 to 128, 49152 in all
- tail_cache: bfloat16 [4, 768, 128, 512], P('kv', 'blk'), may hold values from -6 to 6
- queries: bfloat16 [768, 2, 2048], P('blk', None, 'kv'), may hold values from -120 to 120
- new_kv: bfloat16 [4, 768, 2, 512], P('kv', 'blk'), may hold values from -5.1 to 5.1
- hidden: bfloat16 [768, 2, 2048], P('blk'), may hold values from -4 to 4
- out_weight: bfloat16 [2048, 2048], P('kv'), may hold values from -0.125 to 0.125
- norm_gain: float32 [2048], replicated, may hold values from 0.1 to 1.9
- score_weight: float32 [2048], replicated, may hold values from -0.125 to 0.125
Outputs:
- hidden_out: bfloat16 [768, 2, 2048], P('blk')
- scores_out: float32 [768], P('blk')
The draws below stay inside these ranges and needn't reach their ends.
Inputs may be any that keep to these rules, and one draw needn't show every extreme that they name: `slot_page`: the pages of all prompts fit the pool; every logical page number appears once. Request slot r serves sample request_ids[r] % 16 of prompt request_ids[r] // 16; every pair once.
All inputs are finite; a program needn't handle non-finite values. No bound on the sum of `tail_len` on one device may be relied on, other than what follows from the above.
Results may differ from the reference program's by a relative error of at most 0.02.
Values may be sent and summed in bfloat16 or wider, within the bound.
A program may use at most 64 MiB of HBM per device.

```python
import math
import jax
import jax.numpy as jnp
import numpy as np
from jax import lax

D = 2048
HEAD = 256
KVHEADS = 4
GROUP = 2
QHEADS = 8
SAMPLES = 16
DRAFT = 2
PAGE = 64
TAIL = 128
REQS = 768
PROMPTS = 48
PAGES = 3072
PREFIX_TOTAL = 193536
PROMPT_MOST = 32768
TAIL_TOTAL = 49152


def draw_slot_page(key, part):
    base = jax.random.fold_in(key, 57)
    key_move, key_dest = jax.random.split(base, 2)
    order = jnp.arange(PAGES, dtype=jnp.int32)
    mover = (jax.random.randint(key_move, (PAGES,), 0, 8) == 0).astype(jnp.int32)
    target = jax.random.randint(key_dest, (PAGES,), 0, PAGES)
    place = jnp.where(mover == 1, target, order)
    score = (place * 2 + mover) * PAGES + order
    return jnp.argsort(score, stable=True).astype(jnp.int32)


def draw_joint(key):
    base = jax.random.fold_in(key, 31)
    key_query, key_pairs = jax.random.split(base, 2)
    queries = jnp.clip(jax.random.normal(key_query, (REQS, DRAFT, QHEADS * HEAD), jnp.float32), -5.0, 5.0)
    fresh = jnp.clip(jax.random.normal(key_pairs, (KVHEADS, REQS, DRAFT, 2 * HEAD), jnp.float32), -5.0, 5.0)
    return (queries, fresh)


def draw_queries(key, part):
    return draw_joint(key)[0].astype(jnp.bfloat16)


def draw_new_kv(key, part):
    return draw_joint(key)[1].astype(jnp.bfloat16)


def shard_levels(rng, extent, cuts, least, high):
    level = 1.0
    for dim, parts in cuts:
        steps = jax.random.uniform(jax.random.fold_in(jax.random.fold_in(rng, 6), dim), (parts,), jnp.float32, least / len(cuts), high / len(cuts))
        level = level * jnp.repeat(jnp.exp(steps), extent[dim] // parts).reshape((-1,) + (1,) * (len(extent) - 1 - dim))
    return level


def length_profile(amount, total, bound, slope):
    portions = [(1 << 20) // math.isqrt(standing ** slope) + 1 for standing in range(2, amount + 1)]
    rest, given = total - bound - (amount - 1), [1] * (amount - 1)
    while rest > 0:
        candidates = [i for i in range(amount - 1) if given[i] < bound]
        mass, remaining = sum([portions[i] for i in candidates]), rest
        for i in candidates:
            extra = min(bound - given[i], max(1, remaining * portions[i] // mass), rest)
            given[i] = given[i] + extra
            rest = rest - extra
    return np.array([bound] + given)


def ragged_sizes(own_key, number_of, total, most, lean):
    if number_of == 2:
        one = jax.random.randint(own_key, (), max(1, total - most), min(most, total - 1) + 1)
        return jnp.stack([one, total - one])
    tallies = jnp.asarray(length_profile(number_of, total, most, lean), jnp.int32)
    pairs = (number_of - 1) // 2
    donor, sink = tallies[1:1 + 2 * pairs:2], tallies[2:2 + 2 * pairs:2]
    slack = jnp.minimum(donor - 1, most - sink)
    shifted = jax.random.randint(jax.random.fold_in(own_key, 1), (pairs,), 0, 1 << 20) % (slack + 1)
    tallies = tallies.at[1:1 + 2 * pairs:2].set(donor - shifted).at[2:2 + 2 * pairs:2].set(sink + shifted)
    return tallies[jax.random.permutation(jax.random.fold_in(own_key, 2), number_of)]


def centred(own_key, shape, scale, reach, cuts=(), kind=jnp.bfloat16):
    result = scale * jax.random.normal(own_key, shape, jnp.float32)
    if cuts:
        result = result * shard_levels(own_key, shape, cuts, -0.22, 0.18)
    return jnp.clip(result, -reach, reach).astype(kind)


def setup_inputs(seed: int = 0) -> dict:
    key_list = jax.random.split(jax.random.key(seed), 13)
    return {
        "prefix_pool": centred(key_list[0], (KVHEADS, PAGES, PAGE, 2 * HEAD), 1.0, 6.0, ((0, 4), (1, 128))),
        "slot_page": draw_slot_page(jax.random.fold_in(key_list[12], 71), 0),
        "prompt_len": ragged_sizes(key_list[2], PROMPTS, PREFIX_TOTAL, PROMPT_MOST, 2).astype(jnp.int32),
        "request_ids": jax.random.permutation(key_list[3], REQS).astype(jnp.int32),
        "tail_len": ragged_sizes(key_list[4], REQS, TAIL_TOTAL, TAIL, 2).astype(jnp.int32),
        "tail_cache": centred(key_list[5], (KVHEADS, REQS, TAIL, 2 * HEAD), 1.0, 6.0, ((0, 4), (1, 128))),
        "queries": draw_queries(jax.random.fold_in(key_list[12], 71), 0),
        "new_kv": draw_new_kv(jax.random.fold_in(key_list[12], 71), 0),
        "hidden": centred(key_list[8], (REQS, DRAFT, D), 0.5, 4.0, ((0, 128),)),
        "out_weight": centred(key_list[9], (QHEADS * HEAD, D), (QHEADS * HEAD) ** -0.5, 0.125, ((0, 4),)),
        "norm_gain": jnp.clip(1.0 + 0.18 * jax.random.normal(key_list[10], (D,), jnp.float32), 0.1, 1.9),
        "score_weight": centred(key_list[11], (D,), D ** -0.5, 0.125, (), jnp.float32),
    }


NEG_FLOOR = -1e+30

def page_layout(slot_page, prompt_len, page_tokens):
    needed = (prompt_len + page_tokens - 1) // page_tokens
    page_ends = jnp.cumsum(needed).astype(jnp.int32)
    page_starts = page_ends - needed
    page_owner = lax.optimization_barrier(jnp.sum((slot_page[:, None] >= page_ends[None, :]).astype(jnp.int32), axis=1))
    in_use = page_owner < prompt_len.shape[0]
    page_owner = jnp.minimum(page_owner, prompt_len.shape[0] - 1)
    offset = slot_page - page_starts[page_owner]
    position = offset[:, None] * page_tokens + jnp.arange(page_tokens, dtype=jnp.int32)[None, :]
    live_keys = in_use[:, None] & (position < prompt_len[page_owner][:, None])
    return (page_owner, live_keys)

def home_slots(request_ids):
    total_count = request_ids.shape[0]
    return jnp.zeros((total_count,), jnp.int32).at[request_ids].set(jnp.arange(total_count, dtype=jnp.int32))

def prefix_sums(all_queries, page_pool, slot_rows, live_keys, total_count):
    page_count = page_pool.shape[0]
    score_scale = HEAD ** (-0.5)
    row_count = DRAFT * GROUP
    picked = all_queries[slot_rows].reshape(page_count, -1, HEAD).astype(jnp.float32)
    logits = jnp.einsum('prh,pkh->prk', picked, page_pool[:, :, :HEAD].astype(jnp.float32)) * score_scale
    logits = jnp.where(live_keys[:, None, :], logits, NEG_FLOOR)
    flat_rows = slot_rows.reshape(-1)
    slot_peak = lax.optimization_barrier(jnp.max(logits, axis=2)).reshape(-1, row_count)
    prefix_peak = jnp.full((total_count, row_count), NEG_FLOOR, jnp.float32).at[flat_rows].max(slot_peak)
    ref_peak = prefix_peak[slot_rows].reshape(page_count, -1)
    weights = jnp.where(live_keys[:, None, :], jnp.exp(logits - ref_peak[:, :, None]), 0.0)
    slot_den = lax.optimization_barrier(jnp.sum(weights, axis=2)).reshape(-1, row_count)
    rounded = lax.optimization_barrier(weights.astype(jnp.bfloat16)).astype(jnp.float32)
    slot_num = jnp.einsum('prk,pkh->prh', rounded, page_pool[:, :, HEAD:].astype(jnp.float32)).reshape(-1, row_count, HEAD)
    prefix_num = jnp.zeros((total_count, row_count, HEAD), jnp.float32).at[flat_rows].add(slot_num)
    prefix_den = jnp.zeros((total_count, row_count), jnp.float32).at[flat_rows].add(slot_den)
    return (prefix_peak, prefix_num, prefix_den)

def own_attention(own_queries, tail_block, fresh_block, tail_len, prefix_peak, prefix_num, prefix_den):
    req_count = own_queries.shape[0]
    row_count = DRAFT * GROUP
    score_scale = HEAD ** (-0.5)
    flat_queries = own_queries.reshape(req_count, row_count, HEAD).astype(jnp.float32)
    tail_logits = jnp.einsum('rqh,rkh->rqk', flat_queries, tail_block[:, :, :HEAD].astype(jnp.float32)) * score_scale
    tail_live = (jnp.arange(tail_block.shape[1], dtype=jnp.int32)[None, :] < tail_len[:, None])[:, None, :]
    tail_logits = jnp.where(tail_live, tail_logits, NEG_FLOOR)
    fresh_logits = jnp.einsum('rqh,rkh->rqk', flat_queries, fresh_block[:, :, :HEAD].astype(jnp.float32)) * score_scale
    fresh_live = (jnp.arange(DRAFT, dtype=jnp.int32)[None, :] <= (jnp.arange(row_count, dtype=jnp.int32) // GROUP)[:, None])[None]
    fresh_logits = jnp.where(fresh_live, fresh_logits, NEG_FLOOR)
    own_peak = jnp.maximum(lax.optimization_barrier(jnp.max(tail_logits, axis=2)), lax.optimization_barrier(jnp.max(fresh_logits, axis=2)))
    top_peak = jnp.maximum(prefix_peak, own_peak)
    tail_weights = jnp.where(tail_live, jnp.exp(tail_logits - top_peak[:, :, None]), 0.0)
    fresh_weights = jnp.where(fresh_live, jnp.exp(fresh_logits - top_peak[:, :, None]), 0.0)
    carried = jnp.exp(prefix_peak - top_peak)
    tail_round = lax.optimization_barrier(tail_weights.astype(jnp.bfloat16)).astype(jnp.float32)
    fresh_round = lax.optimization_barrier(fresh_weights.astype(jnp.bfloat16)).astype(jnp.float32)
    numer = prefix_num * carried[:, :, None]
    numer = numer + jnp.einsum('rqk,rkh->rqh', tail_round, tail_block[:, :, HEAD:].astype(jnp.float32))
    numer = numer + jnp.einsum('rqk,rkh->rqh', fresh_round, fresh_block[:, :, HEAD:].astype(jnp.float32))
    denom = prefix_den * carried + lax.optimization_barrier(jnp.sum(tail_weights, axis=2)) + lax.optimization_barrier(jnp.sum(fresh_weights, axis=2))
    return (numer / denom[:, :, None]).astype(jnp.bfloat16).reshape(req_count, DRAFT, GROUP * HEAD)

def reference(prefix_pool, slot_page, prompt_len, request_ids, tail_len, tail_cache, queries, new_kv, hidden, out_weight, norm_gain, score_weight):
    page_owner, live_keys = page_layout(slot_page, prompt_len, PAGE)
    home_rows = home_slots(request_ids)
    slot_rows = home_rows[page_owner[:, None] * SAMPLES + jnp.arange(SAMPLES, dtype=jnp.int32)[None, :]]
    head_width = GROUP * HEAD
    heads_out = []
    for head_index in range(KVHEADS):
        head_queries = queries[:, :, head_index * head_width:(head_index + 1) * head_width]
        prefix_peak, prefix_num, prefix_den = prefix_sums(head_queries, prefix_pool[head_index], slot_rows, live_keys, REQS)
        heads_out.append(own_attention(head_queries, tail_cache[head_index], new_kv[head_index], tail_len, prefix_peak, prefix_num, prefix_den))
    attention = jnp.concatenate(heads_out, axis=2)
    projected = jnp.dot(attention.reshape(-1, QHEADS * HEAD), out_weight, preferred_element_type=jnp.float32)
    hidden_out = (hidden.astype(jnp.float32) + projected.reshape(hidden.shape)).astype(jnp.bfloat16)
    last_hidden = hidden_out[:, -1, :].astype(jnp.float32)
    normed = last_hidden * lax.rsqrt(lax.optimization_barrier(jnp.mean(last_hidden * last_hidden, axis=-1, keepdims=True)) + 1e-06) * norm_gain
    scores_out = lax.optimization_barrier(jnp.sum(normed * score_weight, axis=-1))
    return (hidden_out, scores_out)
```

```python
import functools

import jax
import jax.numpy as jnp
from jax import lax
from jax.experimental import pallas as pl
from jax.experimental.pallas import tpu as pltpu
from jax.sharding import PartitionSpec as P

MESH = pl.DeviceIdType.MESH
SAMPLES = 16
HEAD = 256
PAGE = 64
NEG = -1e30
F32 = jnp.float32
BF16 = jnp.bfloat16


def iota(shape, dim):
    return lax.broadcasted_iota(jnp.int32, shape, dim)


def dot(a, b, ca=1, cb=0):
    return lax.dot_general(a, b, (((ca,), (cb,)), ((), ())), preferred_element_type=F32)


def split3(x):
    a = x.astype(BF16).astype(F32)
    b = (x - a).astype(BF16).astype(F32)
    return a, b, x - a - b


def kernel(
    n, nx, reqs, pages,
    slot_ref, plen_ref, tlen_ref, ids_ref, q_ref, nk_ref, hid_ref, gain_ref, score_ref,
    pool_hbm, tail_hbm, w_hbm,
    out_ref, sc_ref,
    poolv, tailv, wv, s1, agm, ago, gm, go, gtm, gto, pick, accb, stb,
    xo_acc, xo_st, rx_acc, rx_st, tx_acc, tx_ml, rs_acc, rs_ml, t2, r2,
    own_acc, own_st, part, ar,
    local_sem, s1_send, s1_recv, ag_send, ag_recv, fw_send, fw_recv,
    xo_send, xo_recv, xs_send, xs_recv, rs_send, rs_recv, rm_send, rm_recv,
    t2_send, t2_recv, ar_send, ar_recv,
):
    chunk = n * 2 * reqs
    rows = pages * SAMPLES
    prompts = plen_ref.shape[0]
    scale = HEAD ** (-0.5)
    x = lax.axis_index("kv")
    b = lax.axis_index("blk")
    k = lax.rem(b, 2)
    y = lax.rem(lax.div(b, 2), n)
    z = lax.div(b, 2 * n)
    p1 = y + k * (z - y)
    p2 = z + k * (y - z)
    other = 1 - k

    def at(zz, yy, kk):
        return (x, (zz * n + yy) * 2 + kk)

    def ring1(pos, h, kk):
        if h == 0:
            return at(z, pos, kk)
        return at(pos, y, kk)

    def mine1(pos, kk):
        return at(z + k * (pos - z), pos + k * (y - pos), kk)

    def mine2(pos):
        return at(pos + k * (z - pos), y + k * (pos - y), k)

    partner = at(z, y, other)

    def remote(src, dst, send, recv, to):
        return pltpu.make_async_remote_copy(
            src_ref=src, dst_ref=dst, send_sem=send, recv_sem=recv, device_id=to, device_id_type=MESH
        )

    barrier = pltpu.get_barrier_semaphore()

    def greet(to):
        pl.semaphore_signal(barrier, inc=1, device_id=to, device_id_type=MESH)

    greet(partner)
    for d in range(1, n):
        for kk in range(2):
            greet(at(z, lax.rem(y + d, n), kk))
            greet(at(lax.rem(z + d, n), y, kk))
    for d in range(1, nx):
        greet((lax.rem(x + d, nx), b))

    loads = [
        pltpu.make_async_copy(pool_hbm, poolv, local_sem.at[0]),
        pltpu.make_async_copy(tail_hbm, tailv, local_sem.at[1]),
        pltpu.make_async_copy(w_hbm, wv, local_sem.at[2]),
    ]
    for load in loads:
        load.start()
    s1[p1 * 2 + k] = q_ref[k]

    pl.semaphore_wait(barrier, 1 + 4 * (n - 1) + (nx - 1))

    def first(h, d):
        mypos = (y, z)[h]
        pos = lax.rem(mypos + d, n)
        slot = mypos * 2 + k
        return remote(
            q_ref.at[h], s1.at[slot], s1_send.at[h * n + d], s1_recv.at[slot], ring1(pos, h, h)
        )

    for d in range(1, n):
        for h in range(2):
            first(h, d).start()
    remote(q_ref.at[other], s1.at[remote_slot(n, y, z, k)], s1_send.at[other * n],
           s1_recv.at[remote_slot(n, y, z, k)], partner).start()

    lane = iota((1, 128), 1)
    lens = jnp.zeros((1, 128), jnp.int32)
    for p in range(prompts):
        lens = jnp.where(lane == p, plen_ref[p], lens)
    need = lax.div(lens + (PAGE - 1), PAGE).astype(F32)
    grid_r, grid_c = iota((128, 128), 0), iota((128, 128), 1)
    need_t = jnp.transpose(jnp.broadcast_to(need, (128, 128)))
    ends = jnp.sum(jnp.where(grid_r <= grid_c, need_t, 0.0), axis=0, keepdims=True)
    starts = ends - need
    page_r = iota((pages, 128), 0)
    slots = jnp.zeros((pages, 128), jnp.int32)
    for j in range(pages):
        slots = jnp.where(page_r == j, slot_ref[j], slots)
    slots = slots.astype(F32)
    plane = iota((pages, 128), 1)
    owner = jnp.sum(
        jnp.where((plane < prompts) & (slots >= ends), 1.0, 0.0), axis=1, keepdims=True
    )
    used = owner < prompts
    owner = jnp.minimum(owner, prompts - 1.0)
    mine = plane.astype(F32) == owner
    start = jnp.sum(jnp.where(mine, starts, 0.0), axis=1, keepdims=True)
    length = jnp.sum(jnp.where(mine, lens.astype(F32), 0.0), axis=1, keepdims=True)
    live = jnp.where(used, length - (slots - start) * PAGE, 0.0)

    sample = lax.rem(iota((rows, 128), 0), SAMPLES).astype(F32)
    target = (
        jnp.broadcast_to((owner * SAMPLES + jnp.zeros_like(slots))[:, None, :], (pages, SAMPLES, 128))
        .reshape(rows, 128) + sample
    )
    live_c = jnp.broadcast_to(live[:, None, :], (pages, SAMPLES, 128)).reshape(rows, 128)
    target_row = jnp.concatenate(
        [jnp.transpose(target[i * 128:(i + 1) * 128])[0:1] for i in range(rows // 128)], axis=1
    )
    live_row = jnp.concatenate(
        [jnp.transpose(live_c[i * 128:(i + 1) * 128])[0:1] for i in range(rows // 128)], axis=1
    )
    for half, g, gt in ((k, gm, gtm), (other, go, gto)):
        ids = ids_ref[half]
        padded = jnp.concatenate([ids, jnp.zeros((128 - n, 128), F32)], axis=0)
        ids_t = jnp.transpose(padded)
        for p in range(n):
            g[p] = jnp.where(
                target[:, :chunk] == ids[p:p + 1, :chunk], 1.0, 0.0
            ).astype(BF16)
            gt[pl.ds(p * chunk, chunk), :] = jnp.where(
                ids_t[:chunk, p:p + 1] == target_row, 1.0, 0.0
            ).astype(BF16)

    loads[1].wait()
    qown = jnp.concatenate([q_ref[0], q_ref[1]], axis=0)
    tails = tailv[...].reshape(reqs * 128, 2 * HEAD)
    news = nk_ref[...]
    row32 = lax.rem(iota((32, reqs * 128), 0), 8)
    col32 = iota((32, reqs * 128), 1)
    tl = jnp.concatenate([jnp.full((1, 128), tlen_ref[r], jnp.int32) for r in range(reqs)], axis=1)
    tlive = (row32 == lax.div(col32, 128)) & (lax.rem(col32, 128) < tl)
    ts = jnp.where(tlive, dot(qown, tails[:, :HEAD], 1, 1) * scale, NEG)
    nrow, ncol = iota((32, 16), 0), iota((32, 16), 1)
    nlive = (lax.rem(nrow, 8) == lax.rem(ncol, 8)) & (lax.div(ncol, 8) <= lax.div(nrow, 16))
    ns = jnp.where(nlive, dot(qown, news[:, :HEAD], 1, 1) * scale, NEG)
    peak = jnp.maximum(jnp.max(ts, axis=1, keepdims=True), jnp.max(ns, axis=1, keepdims=True))
    tw = jnp.where(tlive, jnp.exp(ts - peak), 0.0)
    nw = jnp.where(nlive, jnp.exp(ns - peak), 0.0)
    own_acc[...] = dot(tw.astype(BF16), tails[:, HEAD:]) + dot(nw.astype(BF16), news[:, HEAD:])
    own_den = jnp.sum(tw, axis=1, keepdims=True) + jnp.sum(nw, axis=1, keepdims=True)
    own_st[...] = jnp.where(iota((32, 128), 1) == 0, peak, own_den)

    for d in range(n):
        for kk in range(2):
            slot = lax.rem(p1 + d, n) * 2 + lax.rem(k + kk, 2)
            if d or kk:
                remote(q_ref.at[0], s1.at[slot], s1_send.at[0], s1_recv.at[slot], partner).wait_recv()
    s1v = s1[...].reshape(2 * n * 16, HEAD)
    pr, pc = iota((chunk, 2 * n * 16), 0), iota((chunk, 2 * n * 16), 1)
    want = lax.div(pr, reqs) * 16 + lax.rem(pr, reqs)
    packed = [
        dot(jnp.where(pc == want + c * 8, 1.0, 0.0).astype(BF16), s1v) for c in range(2)
    ]
    agm[p2] = jnp.concatenate(packed, axis=1).astype(BF16)

    def second(pos, src):
        return remote(agm.at[src], agm.at[src], ag_send.at[pos], ag_recv.at[src], mine2(pos))

    def forward(src):
        return remote(agm.at[src], ago.at[src], fw_send.at[src], fw_recv.at[src], partner)

    far = [d for i in range(1, n // 2 + 1) for d in ((i, n - i) if 2 * i != n else (i,))]
    for d in far:
        pos = lax.rem(p2 + d, n)
        second(pos, p2).start()
    forward(p2).start()
    pick[0] = dot(gm[p2], agm[p2])
    for d in far:
        src = lax.rem(p2 + n - d, n)
        second(src, src).wait_recv()
        forward(src).start()
        pick[0] += dot(gm[src], agm[src])
    q2 = p1
    for i, d in enumerate([0] + far):
        src = lax.rem(q2 + n - d, n)
        forward(src).wait_recv()
        got = dot(go[src], ago[src])
        pick[1] = got if i == 0 else pick[1] + got

    loads[0].wait()
    blocks = pages // 8
    scores, peaks = [], []
    for blk in range(blocks):
        keys = poolv[blk * 8:(blk + 1) * 8].reshape(8 * PAGE, 2 * HEAD)[:, :HEAD]
        qb = jnp.concatenate(
            [
                pick[h, blk * 128:(blk + 1) * 128, c * HEAD:(c + 1) * HEAD].astype(BF16)
                for h in range(2) for c in range(2)
            ],
            axis=0,
        )
        full = dot(keys, qb, 1, 1)
        page_l = lax.div(lax.rem(iota((PAGE, 512), 1), 128), SAMPLES)
        s = jnp.zeros((PAGE, 512), F32)
        for j in range(8):
            s = jnp.where(page_l == j, full[j * PAGE:(j + 1) * PAGE], s)
        lv = jnp.concatenate([live_row[:, blk * 128:(blk + 1) * 128]] * 4, axis=1)
        alive = iota((PAGE, 512), 0).astype(F32) < lv
        s = jnp.where(alive, s * scale, NEG)
        scores.append((s, alive))
        m = jnp.max(s, axis=0, keepdims=True)
        peaks.append(jnp.concatenate([m[:, i * 128:(i + 1) * 128] for i in range(4)], axis=0))
    local = jnp.concatenate(peaks, axis=1)
    local = jnp.concatenate([local, local], axis=0)
    tgt8 = jnp.broadcast_to(target_row, (8, rows))
    lane8 = iota((8, rows), 1)
    top = local
    lead = jnp.ones((8, rows), F32)
    for d in range(1, pages):
        same = pltpu.roll(tgt8, d * SAMPLES, 1) == tgt8
        top = jnp.where(same, jnp.maximum(top, pltpu.roll(local, d * SAMPLES, 1)), top)
        lead = jnp.where(same & (lane8 >= d * SAMPLES), 0.0, lead)
    dens = []
    for blk in range(blocks):
        s, alive = scores[blk]
        tb = top[:, blk * 128:(blk + 1) * 128]
        tb = jnp.concatenate([tb[i:i + 1] for i in range(4)], axis=1)
        w = jnp.where(alive, jnp.exp(s - tb), 0.0)
        dsum = jnp.sum(w, axis=0, keepdims=True)
        dens.append(jnp.concatenate([dsum[:, i * 128:(i + 1) * 128] for i in range(4)], axis=0))
        page_l = lax.div(lax.rem(iota((PAGE, 512), 1), 128), SAMPLES)
        wide = jnp.concatenate([jnp.where(page_l == j, w, 0.0) for j in range(8)], axis=0)
        values = poolv[blk * 8:(blk + 1) * 8].reshape(8 * PAGE, 2 * HEAD)[:, HEAD:]
        acc = dot(jnp.transpose(wide).astype(BF16), values)
        for h in range(2):
            for c in range(2):
                i = h * 2 + c
                accb[h, blk * 128:(blk + 1) * 128, c * HEAD:(c + 1) * HEAD] = (
                    acc[i * 128:(i + 1) * 128].astype(BF16)
                )
    den = jnp.concatenate(dens, axis=1)
    for h in range(2):
        ms = jnp.where(lead[0:2] > 0.5, top[2 * h:2 * h + 2], 0.0)
        st = jnp.concatenate(
            [ms, den[2 * h:2 * h + 2], lead[0:1], jnp.zeros((123, rows), F32)], axis=0
        )
        st = jnp.concatenate(
            [jnp.transpose(st[:, i * 128:(i + 1) * 128]) for i in range(rows // 128)], axis=0
        )
        stb[h] = jnp.concatenate([t.astype(BF16) for t in split3(st)], axis=1)

    lane_c = iota((chunk, 128), 1)

    def column_stats(g, h):
        st = dot(g, stb[h])
        st = st[:, :128] + st[:, 128:256] + st[:, 256:]
        return jnp.where((lane_c < 2) & (st[:, 4:5] < 0.5), NEG, st)

    for p in range(n):
        g = gto[pl.ds(p * chunk, chunk), :]
        xo_acc[p] = dot(g, accb[1]).astype(BF16)
        xo_st[p] = column_stats(g, 1)
        remote(xo_acc.at[p], rx_acc.at[p], xo_send.at[p], xo_recv.at[p], partner).start()
        remote(xo_st.at[p], rx_st.at[p], xs_send.at[p], xs_recv.at[p], partner).start()

    def spread(col):
        return jnp.broadcast_to(col, (chunk, HEAD))

    def to_ring_acc(p):
        return remote(tx_acc.at[p], rs_acc.at[p2], rs_send.at[p], rs_recv.at[p2], mine2(p))

    def to_ring_ml(p):
        return remote(tx_ml.at[p], rs_ml.at[p2], rm_send.at[p], rm_recv.at[p2], mine2(p))

    for d in far[::-1] + [0]:
        p = lax.rem(p2 + d, n)
        g = gtm[pl.ds(pl.multiple_of(p * chunk, chunk), chunk), :]
        acc = dot(g, accb[0])
        st = column_stats(g, 0)
        remote(xo_acc.at[p], rx_acc.at[p], xo_send.at[p], xo_recv.at[p], partner).wait_recv()
        remote(xo_st.at[p], rx_st.at[p], xs_send.at[p], xs_recv.at[p], partner).wait_recv()
        st2 = rx_st[p]
        both = jnp.maximum(st, st2)
        a, c2 = jnp.exp(st - both), jnp.exp(st2 - both)
        acc2 = rx_acc[p].astype(F32)
        outs, dn = [], []
        for c in range(2):
            sl = slice(c * HEAD, (c + 1) * HEAD)
            wa, wb = a[:, c:c + 1], c2[:, c:c + 1]
            outs.append(acc[:, sl] * spread(wa) + acc2[:, sl] * spread(wb))
            dn.append(st[:, 2 + c:3 + c] * wa + st2[:, 2 + c:3 + c] * wb)
        ml = jnp.where(lane_c < 2, both, jnp.where(lane_c == 2, dn[0], dn[1]))
        if chunk < 128:
            ml = jnp.concatenate([ml, jnp.zeros((128 - chunk, 128), F32)], axis=0)
        ml = jnp.transpose(ml)[0:8]
        outs = jnp.concatenate(outs, axis=1).astype(BF16)
        if d:
            tx_acc[p] = outs
            tx_ml[p] = ml
            to_ring_acc(p).start()
            to_ring_ml(p).start()
        else:
            rs_acc[p] = outs
            rs_ml[p] = ml

    for d in far:
        src = lax.rem(p2 + n - d, n)
        remote(tx_acc.at[src], rs_acc.at[src], rs_send.at[src], rs_recv.at[src], partner).wait_recv()
        remote(tx_ml.at[src], rs_ml.at[src], rm_send.at[src], rm_recv.at[src], partner).wait_recv()
    stats = []
    for c in range(2):
        m = jnp.concatenate([rs_ml[i, c:c + 1, :] for i in range(n)], axis=0)
        den_c = jnp.concatenate([rs_ml[i, 2 + c:3 + c, :] for i in range(n)], axis=0)
        mx = jnp.max(m, axis=0, keepdims=True)
        w = jnp.exp(m - mx)
        stats.append((w, mx, jnp.sum(w * den_c, axis=0, keepdims=True)))
    table = jnp.concatenate(
        [stats[0][0], stats[1][0], stats[0][1], stats[1][1], stats[0][2], stats[1][2],
         jnp.zeros((124 - 2 * n, 128), F32)],
        axis=0,
    )
    table = jnp.transpose(table)[:chunk]
    t2v = jnp.zeros((2 * n * 16, HEAD + 128), F32)
    sr, sc = iota((2 * n * 16, chunk), 0), iota((2 * n * 16, chunk), 1)
    for c in range(2):
        acc = jnp.zeros((chunk, HEAD), F32)
        for i in range(n):
            acc += rs_acc[i, :, c * HEAD:(c + 1) * HEAD].astype(F32) * spread(
                table[:, c * n + i:c * n + i + 1]
            )
        cols = split3(table[:, 2 * n + c:2 * n + c + 1]) + split3(table[:, 2 * n + 2 + c:2 * n + 3 + c])
        tile = jnp.zeros((chunk, 128), F32)
        for i, col in enumerate(cols):
            tile = jnp.where(lane_c == i, col, tile)
        rowsrc = jnp.concatenate([acc, tile], axis=1).astype(BF16)
        inner = lax.rem(sr, 16) - c * 8
        pick_rows = (inner >= 0) & (inner < reqs) & (lax.div(sr, 16) * reqs + inner == sc)
        t2v += dot(jnp.where(pick_rows, 1.0, 0.0).astype(BF16), rowsrc)
    t2[...] = t2v.astype(BF16).reshape(2 * n, 16, HEAD + 128)

    def home(pos, kk):
        return remote(
            t2.at[pos * 2 + kk], r2.at[k, p1], t2_send.at[pos * 2 + kk], t2_recv.at[k, p1],
            mine1(pos, kk),
        )

    for d in far[::-1]:
        pos = lax.rem(p1 + d, n)
        for kk in range(2):
            home(pos, kk).start()
    home(p1, other).start()
    r2[k, p1] = t2[p1 * 2 + k]
    loads[2].wait()
    for d in range(1, n):
        for h in range(2):
            src = lax.rem((y, z)[h] + d, n)
            remote(t2.at[0], r2.at[h, src], t2_send.at[0], t2_recv.at[h, src], partner).wait_recv()
    src = y + other * (z - y)
    remote(t2.at[0], r2.at[other, src], t2_send.at[0], t2_recv.at[other, src], partner).wait_recv()

    heads = []
    for h in range(2):
        cells = [r2[h, i].astype(F32) for i in range(n)]
        ms = [t[:, HEAD:HEAD + 1] + t[:, HEAD + 1:HEAD + 2] + t[:, HEAD + 2:HEAD + 3] for t in cells]
        ds = [t[:, HEAD + 3:HEAD + 4] + t[:, HEAD + 4:HEAD + 5] + t[:, HEAD + 5:HEAD + 6] for t in cells]
        ms.append(own_st[h * 16:(h + 1) * 16, 0:1])
        ds.append(own_st[h * 16:(h + 1) * 16, 1:2])
        accs = [t[:, :HEAD] for t in cells] + [own_acc[h * 16:(h + 1) * 16]]
        mx = functools.reduce(jnp.maximum, ms)
        num = jnp.zeros((16, HEAD), F32)
        dn = jnp.zeros((16, 1), F32)
        for m, dd, acc in zip(ms, ds, accs):
            w = jnp.exp(m - mx)
            num += acc * w
            dn += dd * w
        heads.append(num / dn)
    att = jnp.concatenate(
        [jnp.concatenate([a[0:8], a[8:16]], axis=1) for a in heads], axis=0
    ).astype(BF16)

    ar[x] = dot(att, wv[...]).astype(BF16)

    def share(d):
        return remote(
            ar.at[x], ar.at[x], ar_send.at[d], ar_recv.at[x], (lax.rem(x + d, nx), b)
        )

    for d in range(1, nx):
        share(d).start()
    for d in range(1, nx):
        src = lax.rem(x + nx - d, nx)
        remote(ar.at[src], ar.at[src], ar_send.at[d], ar_recv.at[src], partner).wait_recv()
    total = ar[0].astype(F32)
    for i in range(1, nx):
        total += ar[i].astype(F32)
    hid = (hid_ref[...].astype(F32) + total).astype(BF16)
    out_ref[...] = hid
    last = hid[8:16].astype(F32)
    normed = last * lax.rsqrt(jnp.mean(last * last, axis=1, keepdims=True) + 1e-06) * gain_ref[...]
    sc_ref[...] = jnp.broadcast_to(jnp.sum(normed * score_ref[...], axis=1, keepdims=True), (8, 128))

    for h in range(2):
        for d in range(1, n):
            first(h, d).wait_send()
    remote(q_ref.at[other], s1.at[remote_slot(n, y, z, k)], s1_send.at[other * n],
           s1_recv.at[remote_slot(n, y, z, k)], partner).wait_send()
    for d in far:
        second(lax.rem(p2 + d, n), p2).wait_send()
    for p in range(n):
        forward(p).wait_send()
        remote(xo_acc.at[p], rx_acc.at[p], xo_send.at[p], xo_recv.at[p], partner).wait_send()
        remote(xo_st.at[p], rx_st.at[p], xs_send.at[p], xs_recv.at[p], partner).wait_send()
    for d in far:
        to_ring_acc(lax.rem(p2 + d, n)).wait_send()
        to_ring_ml(lax.rem(p2 + d, n)).wait_send()
    for d in range(1, n):
        for kk in range(2):
            home(lax.rem(p1 + d, n), kk).wait_send()
    home(p1, other).wait_send()
    for d in range(1, nx):
        share(d).wait_send()


def remote_slot(n, y, z, k):
    return (z + k * (y - z)) * 2 + k


def rows_of(a):
    r = a.shape[0]
    a = a.reshape(r, 2, 2, HEAD).transpose(1, 2, 0, 3)
    return jnp.pad(a, ((0, 0), (0, 0), (0, 8 - r), (0, 0))).reshape(2, 16, HEAD)


def body(n, nx, prefix_pool, slot_page, prompt_len, request_ids, tail_len, tail_cache, queries,
         new_kv, hidden, out_weight, norm_gain, score_weight):
    pages = prefix_pool.shape[1]
    reqs, width = hidden.shape[0], hidden.shape[2]
    chunk = n * 2 * reqs
    rows = pages * SAMPLES
    total = n * chunk
    grid = request_ids.astype(F32).reshape(n, n, 2 * reqs)
    ids = jnp.stack([grid.reshape(n, chunk), grid.transpose(1, 0, 2).reshape(n, chunk)])
    ids = jnp.pad(ids, ((0, 0), (0, 0), (0, 128 - chunk)), constant_values=-1.0)
    q = rows_of(queries)
    nk = jnp.pad(new_kv[0].transpose(1, 0, 2), ((0, 0), (0, 8 - reqs), (0, 0))).reshape(16, 2 * HEAD)
    hid = jnp.pad(hidden.transpose(1, 0, 2), ((0, 0), (0, 8 - reqs), (0, 0))).reshape(16, width)
    vm = pl.BlockSpec(memory_space=pltpu.VMEM)
    sm = pl.BlockSpec(memory_space=pltpu.SMEM)
    hbm = pl.BlockSpec(memory_space=pl.ANY)
    dma = pltpu.SemaphoreType.DMA
    out, sc = pl.pallas_call(
        functools.partial(kernel, n, nx, reqs, pages),
        out_shape=(
            jax.ShapeDtypeStruct((16, width), BF16),
            jax.ShapeDtypeStruct((8, 128), F32),
        ),
        in_specs=[sm, sm, sm, vm, vm, vm, vm, vm, vm, hbm, hbm, hbm],
        out_specs=(vm, vm),
        scratch_shapes=[
            pltpu.VMEM((pages, PAGE, 2 * HEAD), BF16),
            pltpu.VMEM((reqs, 128, 2 * HEAD), BF16),
            pltpu.VMEM((2 * HEAD, width), BF16),
            pltpu.VMEM((2 * n, 16, HEAD), BF16),
            pltpu.VMEM((n, chunk, 512), BF16),
            pltpu.VMEM((n, chunk, 512), BF16),
            pltpu.VMEM((n, rows, chunk), BF16),
            pltpu.VMEM((n, rows, chunk), BF16),
            pltpu.VMEM((total, rows), BF16),
            pltpu.VMEM((total, rows), BF16),
            pltpu.VMEM((2, rows, 512), F32),
            pltpu.VMEM((2, rows, 512), BF16),
            pltpu.VMEM((2, rows, 384), BF16),
            pltpu.VMEM((n, chunk, 512), BF16),
            pltpu.VMEM((n, chunk, 128), F32),
            pltpu.VMEM((n, chunk, 512), BF16),
            pltpu.VMEM((n, chunk, 128), F32),
            pltpu.VMEM((n, chunk, 512), BF16),
            pltpu.VMEM((n, 8, 128), F32),
            pltpu.VMEM((n, chunk, 512), BF16),
            pltpu.VMEM((n, 8, 128), F32),
            pltpu.VMEM((2 * n, 16, HEAD + 128), BF16),
            pltpu.VMEM((2, n, 16, HEAD + 128), BF16),
            pltpu.VMEM((32, HEAD), F32),
            pltpu.VMEM((32, 128), F32),
            pltpu.VMEM((8, 128), F32),
            pltpu.VMEM((nx, 16, width), BF16),
            dma((3,)), dma((2 * n,)), dma((2 * n,)),
            dma((n,)), dma((n,)), dma((n,)), dma((n,)),
            dma((n,)), dma((n,)), dma((n,)), dma((n,)),
            dma((n,)), dma((n,)), dma((n,)), dma((n,)),
            dma((2 * n,)), dma((2, n)), dma((nx,)), dma((nx,)),
        ],
        compiler_params=pltpu.CompilerParams(collective_id=0, has_side_effects=True),
    )(
        slot_page, prompt_len, tail_len, ids, q, nk, hid, norm_gain.reshape(1, -1),
        score_weight.reshape(1, -1), prefix_pool[0], tail_cache[0], out_weight,
    )
    hidden_out = out.reshape(2, 8, width)[:, :reqs].transpose(1, 0, 2)
    return hidden_out, sc[:reqs, 0]


def solution(mesh):
    nx = mesh.shape["kv"]
    n = int(round((mesh.shape["blk"] // 2) ** 0.5))
    in_specs = (
        P("kv", "blk", None, None),
        P("blk"),
        P(),
        P(),
        P("blk"),
        P("kv", "blk", None, None),
        P("blk", None, "kv"),
        P("kv", "blk", None, None),
        P("blk", None, None),
        P("kv", None),
        P(),
        P(),
    )
    out_specs = (P("blk", None, None), P("blk"))
    return jax.shard_map(
        functools.partial(body, n, nx), mesh=mesh, in_specs=in_specs, out_specs=out_specs, check_vma=False
    )
```

```python
import functools

import jax
import jax.numpy as jnp
from jax import lax
from jax.experimental import pallas as pl
from jax.experimental.pallas import tpu as pltpu
from jax.sharding import PartitionSpec as P

MESH = pl.DeviceIdType.MESH
SAMPLES = 16
HEAD = 256
PAGE = 64
NEG = -1e30
F32 = jnp.float32
BF16 = jnp.bfloat16


def iota(shape, dim):
    return lax.broadcasted_iota(jnp.int32, shape, dim)


def dot(a, b, ca=1, cb=0):
    return lax.dot_general(a, b, (((ca,), (cb,)), ((), ())), preferred_element_type=F32)


def floor_div(a, c):
    return jnp.floor((a.astype(F32) + 0.5) * (1.0 / c))


def split3(x):
    a = x.astype(BF16).astype(F32)
    b = (x - a).astype(BF16).astype(F32)
    return a, b, x - a - b


def kernel(
    n, nx, reqs, pages,
    slot_ref, plen_ref, tlen_ref, ids_ref, q_in, nk_ref, hid_ref, gain_ref, score_ref,
    pool_hbm, tail_hbm, w_hbm,
    out_ref, sc_ref,
    q_ref, poolv, tailv, wv, s1, agm, ago, gm, go, gt, pick, accm, acco, stats, ptgt, peak_tx, peak_rx, den_tx, den_rx,
    tx_acc, tx_ml, a3_acc, a4_acc, b_acc, rx_ml, t2, r2, own_acc, own_st, ar,
    local_sem, s1_send, s1_recv, ag_send, ag_recv, fw_send, fw_recv,
    cx_send, cx_recv, rs_send, rs_recv, rm_send, rm_recv,
    t2_send, t2_recv, ar_send, ar_recv,
):
    chunk = n * 2 * reqs
    half = chunk // 2
    rows = pages * SAMPLES
    prompts = plen_ref.shape[0]
    scale = HEAD ** (-0.5)
    x = lax.axis_index("kv")
    b = lax.axis_index("blk")
    k = lax.rem(b, 2)
    y = lax.rem(lax.div(b, 2), n)
    z = lax.div(b, 2 * n)
    p1 = y + k * (z - y)
    p2 = z + k * (y - z)
    other = 1 - k

    def at(zz, yy, kk):
        return (x, (zz * n + yy) * 2 + kk)

    def ring1(pos, h, kk):
        if h == 0:
            return at(z, pos, kk)
        return at(pos, y, kk)

    def mine1(pos, kk):
        return at(z + k * (pos - z), pos + k * (y - pos), kk)

    def mine2(d):
        pos = lax.rem(p2 + (d + n), n)
        return at(pos + k * (z - pos), y + k * (pos - y), k)

    def near(d):
        return lax.rem(p2 + (d + n), n)

    partner = at(z, y, other)

    def remote(src, dst, send, recv, to):
        return pltpu.make_async_remote_copy(
            src_ref=src, dst_ref=dst, send_sem=send, recv_sem=recv, device_id=to, device_id_type=MESH
        )

    pending = []

    def start(copy):
        copy.start()
        pending.append(copy)

    barrier = pltpu.get_barrier_semaphore()

    def greet(to):
        pl.semaphore_signal(barrier, inc=1, device_id=to, device_id_type=MESH)

    for d in [i for j in range(1, n // 2 + 1) for i in ((j, n - j) if 2 * j != n else (j,))]:
        for kk in range(2):
            greet(at(z, lax.rem(y + d, n), kk))
            greet(at(lax.rem(z + d, n), y, kk))
    greet(partner)
    for d in range(1, nx):
        greet((lax.rem(x + d, nx), b))

    loads = [
        pltpu.make_async_copy(pool_hbm, poolv, local_sem.at[0]),
        pltpu.make_async_copy(tail_hbm, tailv, local_sem.at[1]),
        pltpu.make_async_copy(w_hbm, wv, local_sem.at[2]),
    ]
    for load in loads:
        load.start()

    raw = q_in[...].astype(F32)
    gap = jnp.zeros((8 - reqs, HEAD), F32)
    for i in range(2):
        q_ref[i] = jnp.concatenate(
            [raw[:, i, 0:HEAD], gap, raw[:, i, HEAD:2 * HEAD], gap], axis=0
        ).astype(BF16)
    s1[p1 * 2 + k] = q_ref[k]

    pl.semaphore_wait(barrier, 1 + 4 * (n - 1) + (nx - 1))

    def first(h, d):
        mypos = (y, z)[h]
        pos = lax.rem(mypos + d, n)
        slot = mypos * 2 + k
        return remote(
            q_ref.at[h], s1.at[slot], s1_send.at[h * n + d], s1_recv.at[slot], ring1(pos, h, h)
        )

    order = [d for i in range(n // 2, 0, -1) for d in ((i, n - i) if 2 * i != n else (i,))]
    for d in order:
        for h in range(2):
            start(first(h, d))
    slot = p1_of(y, z, other) * 2 + k
    start(remote(q_ref.at[other], s1.at[slot], s1_send.at[other * n], s1_recv.at[slot], partner))

    lane = iota((1, 128), 1)
    lens = jnp.zeros((1, 128), jnp.int32)
    for p in range(prompts):
        lens = jnp.where(lane == p, plen_ref[p], lens)
    need = lax.shift_right_logical(lens + (PAGE - 1), 6).astype(F32)
    grid_r, grid_c = iota((128, 128), 0), iota((128, 128), 1)
    need_t = jnp.transpose(jnp.broadcast_to(need, (128, 128)))
    ends = jnp.sum(jnp.where(grid_r <= grid_c, need_t, 0.0), axis=0, keepdims=True)
    starts = ends - need
    page_r = iota((pages, 128), 0)
    slots = jnp.zeros((pages, 128), jnp.int32)
    for j in range(pages):
        slots = jnp.where(page_r == j, slot_ref[j], slots)
    slots = slots.astype(F32)
    plane = iota((pages, 128), 1)
    owner = jnp.sum(
        jnp.where((plane < prompts) & (slots >= ends), 1.0, 0.0), axis=1, keepdims=True
    )
    used = owner < prompts
    owner = jnp.minimum(owner, prompts - 1.0)
    mine = plane.astype(F32) == owner
    begin = jnp.sum(jnp.where(mine, starts, 0.0), axis=1, keepdims=True)
    length = jnp.sum(jnp.where(mine, lens.astype(F32), 0.0), axis=1, keepdims=True)
    live = jnp.where(used, length - (slots - begin) * PAGE, 0.0)
    sample = (iota((rows, 128), 0) & (SAMPLES - 1)).astype(F32)
    target = (
        jnp.broadcast_to((owner * SAMPLES + jnp.zeros_like(slots))[:, None, :], (pages, SAMPLES, 128))
        .reshape(rows, 128) + sample
    )
    live_c = jnp.broadcast_to(live[:, None, :], (pages, SAMPLES, 128)).reshape(rows, 128)
    target_row = jnp.concatenate(
        [jnp.transpose(target[i * 128:(i + 1) * 128])[0:8] for i in range(rows // 128)], axis=1
    )
    live_row = jnp.concatenate(
        [jnp.transpose(live_c[i * 128:(i + 1) * 128])[0:1] for i in range(rows // 128)], axis=1
    )
    ptgt[0] = target_row

    pr, pc = iota((chunk, 2 * n * 16), 0), iota((chunk, 2 * n * 16), 1).astype(F32)
    cell = floor_div(pr, reqs)
    want = cell * 16.0 + (pr.astype(F32) - cell * reqs)
    for d in range(n):
        for kk in range(2):
            slot = lax.rem(p1 + d, n) * 2 + lax.rem(k + kk, 2)
            if d or kk:
                remote(q_ref.at[0], s1.at[slot], s1_send.at[0], s1_recv.at[slot], partner).wait_recv()
    s1v = s1[...].reshape(2 * n * 16, HEAD)
    packed = [
        dot(jnp.where(pc == want + c * 8.0, 1.0, 0.0).astype(BF16), s1v) for c in range(2)
    ]
    agm[p2] = jnp.concatenate(packed, axis=1).astype(BF16)
    start(remote(ptgt.at[0], ptgt.at[1], cx_send.at[0], cx_recv.at[0], partner))

    def part(src, piece):
        return agm.at[src, pl.ds(piece * half, half)]

    def second(src, s, hop, kind, piece):
        return remote(
            part(src, piece), part(src, piece), ag_send.at[s, kind, piece], ag_recv.at[s, kind, piece],
            mine2((1, -1)[s] * hop),
        )

    def arrived(s, kind, piece):
        src = near(-(1, -1)[s] * (kind + 1))
        second(src, s, 1, kind, piece).wait_recv()
        return src

    def forward(src, piece):
        return remote(
            part(src, piece), ago.at[src, pl.ds(piece * half, half)], fw_send.at[src, piece],
            fw_recv.at[src, piece], partner,
        )

    for i in range(2):
        for s in range(2):
            start(second(p2, s, 2, 1, i ^ s))
    for i in range(2):
        for s in range(2):
            start(second(p2, s, 1, 0, i ^ s))
    for i in range(2):
        start(forward(p2, i))

    total = n * chunk
    ids = ids_ref[...]
    grid_u = iota((n * n, total), 0).astype(F32)
    grid_e = iota((n * n, total), 1)
    on = floor_div(grid_e, 2 * reqs) == grid_u
    e_in = iota((total, 128), 0)
    e_mod = e_in.astype(F32) - floor_div(e_in, 2 * reqs) * (2 * reqs)
    l_in = iota((1, 128), 1)
    l_div = floor_div(l_in, 2 * reqs)
    l_mod = l_in.astype(F32) - l_div * (2 * reqs)
    spread_e = jnp.where(e_mod == l_mod, 1.0, 0.0).astype(BF16)
    hi = jnp.where(on, lax.shift_right_logical(ids, 5).astype(F32), 0.0).astype(BF16)
    lo = jnp.where(on, (ids & 31).astype(F32), 0.0).astype(BF16)
    table = dot(hi, spread_e) * 32.0 + dot(lo, spread_e)
    nat = jnp.concatenate(
        [
            jnp.sum(
                jnp.where(iota((n, 128), 0).astype(F32) == l_div, table[i * n:(i + 1) * n], 0.0),
                axis=0, keepdims=True,
            )
            for i in range(n)
        ],
        axis=0,
    )
    perm = jnp.zeros((n, 128), F32)
    for i in range(n):
        perm = jnp.where(l_div == float(i), table[i * n:(i + 1) * n], perm)
    ids_m = jnp.where(k == 0, nat, perm)
    ids_o = jnp.where(k == 0, perm, nat)
    for p in range(n):
        gm[p] = jnp.where(target[:, :chunk] == ids_m[p:p + 1, :chunk], 1.0, 0.0).astype(BF16)

    for i in range(2):
        for s in range(2):
            piece = i ^ s
            src = arrived(s, 1, piece)
            if i == 0:
                start(second(src, s, 2, 3, piece))
            start(second(src, s, 1, 2, piece))
            start(forward(src, piece))
    pick[0] = dot(gm[p2], agm[p2])
    for i in range(2):
        for s in range(2):
            piece = i ^ s
            start(forward(arrived(s, 0, piece), piece))
    for p in range(n):
        go[p] = jnp.where(target[:, :chunk] == ids_o[p:p + 1, :chunk], 1.0, 0.0).astype(BF16)
    for s in range(2):
        for dd in (2, 1):
            src = near(-(1, -1)[s] * dd)
            pick[0] += dot(gm[src], agm[src])

    def from_core(pos, first_one=False):
        for piece in range(2):
            forward(pos, piece).wait_recv()
        got = dot(go[pos], ago[pos])
        pick[1] = got if first_one else pick[1] + got

    from_core(p1, True)
    for dd in (2, -2, 1, -1):
        from_core(lax.rem(p1 + dd + n, n))
    for i in range(2):
        for s in range(2):
            piece = i ^ s
            start(forward(arrived(s, 2, piece), piece))
    for s in range(2):
        src = near(-(1, -1)[s] * 3)
        pick[0] += dot(gm[src], agm[src])
    for s in range(2):
        start(forward(arrived(s, 3, s), s))
    src = near(4)
    pick[0] += dot(gm[src], agm[src])
    for dd in (3, -3, 4):
        from_core(lax.rem(p1 + dd + n, n))

    loads[0].wait()
    blocks = pages // 8
    scores, peaks = [], []
    page_l = lax.shift_right_logical(iota((PAGE, 512), 1) & 127, 4)
    for blk in range(blocks):
        keys = poolv[blk * 8:(blk + 1) * 8].reshape(8 * PAGE, 2 * HEAD)[:, :HEAD]
        qb = jnp.concatenate(
            [
                pick[h, blk * 128:(blk + 1) * 128, c * HEAD:(c + 1) * HEAD].astype(BF16)
                for h in range(2) for c in range(2)
            ],
            axis=0,
        )
        full = dot(keys, qb, 1, 1)
        s = jnp.zeros((PAGE, 512), F32)
        for j in range(8):
            s = jnp.where(page_l == j, full[j * PAGE:(j + 1) * PAGE], s)
        lv = jnp.concatenate([live_row[:, blk * 128:(blk + 1) * 128]] * 4, axis=1)
        alive = iota((PAGE, 512), 0).astype(F32) < lv
        s = jnp.where(alive, s * scale, NEG)
        scores.append((s, alive))
        m = jnp.max(s, axis=0, keepdims=True)
        peaks.append(jnp.concatenate([m[:, i * 128:(i + 1) * 128] for i in range(4)], axis=0))
    local = jnp.concatenate(peaks, axis=1)
    peak_tx[...] = jnp.concatenate([local[2:4], local[0:2], local], axis=0)
    start(remote(peak_tx, peak_rx, cx_send.at[1], cx_recv.at[1], partner))

    remote(ptgt.at[0], ptgt.at[1], cx_send.at[0], cx_recv.at[0], partner).wait_recv()
    tgt_p = ptgt[1]
    both_t = jnp.concatenate([target_row[0:4], tgt_p[0:4]], axis=0)
    swap_t = jnp.concatenate([tgt_p[0:4], target_row[0:4]], axis=0)
    lane8 = iota((8, rows), 1)
    lower = iota((8, rows), 0) >= 4
    lead = jnp.where(lower & (swap_t == both_t), 0.0, 1.0)
    for d in range(1, pages):
        same = pltpu.roll(both_t, d * SAMPLES, 1) == both_t
        cross = pltpu.roll(swap_t, d * SAMPLES, 1) == both_t
        lead = jnp.where((same & (lane8 >= d * SAMPLES)) | (cross & lower), 0.0, lead)
    remote(peak_tx, peak_rx, cx_send.at[1], cx_recv.at[1], partner).wait_recv()
    peer = peak_rx[...]
    both_m = jnp.concatenate([local, peer[0:4]], axis=0)
    swap_m = jnp.concatenate([peer[0:4], local], axis=0)
    top = jnp.where(swap_t == both_t, jnp.maximum(both_m, swap_m), both_m)
    for d in range(1, pages):
        same = pltpu.roll(both_t, d * SAMPLES, 1) == both_t
        cross = pltpu.roll(swap_t, d * SAMPLES, 1) == both_t
        top = jnp.where(same, jnp.maximum(top, pltpu.roll(both_m, d * SAMPLES, 1)), top)
        top = jnp.where(cross, jnp.maximum(top, pltpu.roll(swap_m, d * SAMPLES, 1)), top)

    def give(blk):
        sl = pl.ds(blk * 128, 128)
        return remote(
            acco.at[sl], accm.at[pl.ds(rows + blk * 128, 128)], cx_send.at[3 + blk], cx_recv.at[3 + blk],
            partner,
        )

    dens = []
    for blk in range(blocks):
        s, alive = scores[blk]
        tb = top[:, blk * 128:(blk + 1) * 128]
        tb = jnp.concatenate([tb[i:i + 1] for i in range(4)], axis=1)
        w = jnp.where(alive, jnp.exp(s - tb), 0.0)
        dsum = jnp.sum(w, axis=0, keepdims=True)
        dens.append(jnp.concatenate([dsum[:, i * 128:(i + 1) * 128] for i in range(4)], axis=0))
        wide = jnp.concatenate([jnp.where(page_l == j, w, 0.0) for j in range(8)], axis=0)
        values = poolv[blk * 8:(blk + 1) * 8].reshape(8 * PAGE, 2 * HEAD)[:, HEAD:]
        acc = dot(jnp.transpose(wide).astype(BF16), values)
        for c in range(2):
            acco[blk * 128:(blk + 1) * 128, c * HEAD:(c + 1) * HEAD] = (
                acc[(2 + c) * 128:(3 + c) * 128].astype(BF16)
            )
        start(give(blk))
        for c in range(2):
            accm[blk * 128:(blk + 1) * 128, c * HEAD:(c + 1) * HEAD] = (
                acc[c * 128:(c + 1) * 128].astype(BF16)
            )
    den = jnp.concatenate(dens, axis=1)
    den_tx[...] = jnp.concatenate([den[2:4], den[2:4], den], axis=0)
    start(remote(den_tx, den_rx, cx_send.at[2], cx_recv.at[2], partner))
    for p in range(n):
        if p == 0:
            ids_t = jnp.transpose(jnp.concatenate([ids_m, jnp.zeros((128 - n, 128), F32)], axis=0))
            all_t = jnp.concatenate([target_row[0:1], tgt_p[0:1]], axis=1)
        gt[pl.ds(p * chunk, chunk), :] = jnp.where(ids_t[:chunk, p:p + 1] == all_t, 1.0, 0.0).astype(BF16)
    remote(den_tx, den_rx, cx_send.at[2], cx_recv.at[2], partner).wait_recv()
    den_p = den_rx[...]
    st = jnp.concatenate(
        [
            jnp.concatenate([jnp.where(lead[0:2] > 0.5, top[0:2], 0.0),
                             jnp.where(lead[4:6] > 0.5, top[4:6], 0.0)], axis=1),
            jnp.concatenate([den[0:2], den_p[0:2]], axis=1),
            jnp.concatenate([lead[0:1], lead[4:5]], axis=1),
            jnp.zeros((3, 2 * rows), F32),
        ],
        axis=0,
    )
    stats[...] = jnp.concatenate(split3(st), axis=0).astype(BF16)
    for blk in range(blocks):
        give(blk).wait_recv()

    sub8 = iota((8, 128), 0)

    def sums(d):
        g = gt[pl.ds(pl.multiple_of(near(d) * chunk, chunk), chunk), :]
        acc = dot(g, accm[...])
        ml = dot(stats[...], g, 1, 1)
        ml = ml[0:8] + ml[8:16] + ml[16:24]
        ml = jnp.concatenate([ml, jnp.zeros((8, 128 - chunk), F32)], axis=1)
        return acc, jnp.where((sub8 < 2) & (ml[4:5] < 0.5), NEG, ml)

    def ring(s, kind, src, dst, hop):
        to = mine2((1, -1)[s] * hop)
        return (
            remote(src[0], dst, rs_send.at[s, kind], rs_recv.at[s, kind], to),
            remote(src[1], rx_ml.at[s, kind], rm_send.at[s, kind], rm_recv.at[s, kind], to),
        )

    def landed(s, kind, dst):
        for copy in ring(s, kind, (dst, rx_ml.at[s, kind]), dst, 1):
            copy.wait_recv()

    def store(i, d):
        acc, ml = sums(d)
        tx_acc[i] = acc.astype(BF16)
        tx_ml[i] = ml

    store(2, 4)
    for s in range(2):
        for copy in ring(s, 1, (tx_acc.at[2, pl.ds(s * half, half)], tx_ml.at[2]), a4_acc.at[s], 2):
            start(copy)
    for s in range(2):
        store(s, (3, -3)[s])
        for copy in ring(s, 0, (tx_acc.at[s], tx_ml.at[s]), a3_acc.at[s], 1):
            start(copy)
    for s in range(2):
        store(3 + s, (1, -1)[s])
        for copy in ring(s, 2, (tx_acc.at[3 + s], tx_ml.at[3 + s]), b_acc.at[s, 0], 1):
            start(copy)

    def weigh(mls):
        out = []
        for c in range(2):
            mx = functools.reduce(jnp.maximum, [m[c:c + 1] for m in mls])
            w = [jnp.exp(m[c:c + 1] - mx) for m in mls]
            dn = functools.reduce(jnp.add, [a * m[2 + c:3 + c] for a, m in zip(w, mls)])
            out.append((w, mx, dn))
        return out

    def columns(items):
        return jnp.transpose(
            jnp.concatenate(items + [jnp.zeros((128 - len(items), 128), F32)], axis=0)
        )

    lane128 = iota((8, 128), 1)
    for s in range(2):
        acc, ml = sums((2, -2)[s])
        landed(s, 0, a3_acc.at[s])
        landed(s, 1, a4_acc.at[s])
        inside = (lane128 < half) if s == 0 else (lane128 >= half)
        ml4 = jnp.where((sub8 < 2) & jnp.logical_not(inside), NEG, rx_ml[s, 1])
        mls = [ml, rx_ml[s, 0], ml4]
        st = weigh(mls)
        cols = columns(st[0][0] + st[1][0])
        outs = []
        for c in range(2):
            sl = slice(c * HEAD, (c + 1) * HEAD)
            a3 = a3_acc[s, :, sl].astype(F32)
            a4 = a4_acc[s, :, sl].astype(F32)
            v = acc[:, sl] * cols[:chunk, 3 * c:3 * c + 1] + a3 * cols[:chunk, 3 * c + 1:3 * c + 2]
            add = a4 * cols[s * half:(s + 1) * half, 3 * c + 2:3 * c + 3]
            if s == 0:
                v = jnp.concatenate([v[:half] + add, v[half:]], axis=0)
            else:
                v = jnp.concatenate([v[:half], v[half:] + add], axis=0)
            outs.append(v)
        tx_acc[5 + s] = jnp.concatenate(outs, axis=1).astype(BF16)
        tx_ml[5 + s] = jnp.concatenate(
            [st[0][1], st[1][1], st[0][2], st[1][2], jnp.zeros((4, 128), F32)], axis=0
        )
        for copy in ring(s, 3, (tx_acc.at[5 + s], tx_ml.at[5 + s]), b_acc.at[s, 1], 2):
            start(copy)
    home_acc, home_ml = sums(0)

    loads[1].wait()
    qown = jnp.concatenate([q_ref[0], q_ref[1]], axis=0)
    tails = tailv[...].reshape(reqs * 128, 2 * HEAD)
    row32 = iota((32, 128), 0) & 7
    ts, tl = [], []
    for r in range(reqs):
        ok = (row32 == r) & (iota((32, 128), 1) < tlen_ref[r])
        tl.append(ok)
        ts.append(jnp.where(ok, dot(qown, tails[r * 128:(r + 1) * 128, :HEAD], 1, 1) * scale, NEG))
    fresh = nk_ref[...].astype(F32)
    pad = jnp.zeros((8 - reqs, 2 * HEAD), F32)
    news = jnp.concatenate([fresh[:, 0, :], pad, fresh[:, 1, :], pad], axis=0).astype(BF16)
    nrow, ncol = iota((32, 16), 0), iota((32, 16), 1)
    nlive = ((nrow & 7) == (ncol & 7)) & (lax.shift_right_logical(ncol, 3) <= lax.shift_right_logical(nrow, 4))
    ns = jnp.where(nlive, dot(qown, news[:, :HEAD], 1, 1) * scale, NEG)
    peak = jnp.max(ns, axis=1, keepdims=True)
    peak = jnp.maximum(peak, jnp.max(functools.reduce(jnp.maximum, ts), axis=1, keepdims=True))
    nw = jnp.where(nlive, jnp.exp(ns - peak), 0.0)
    tw = [jnp.where(ok, jnp.exp(t - peak), 0.0) for t, ok in zip(ts, tl)]
    own_den = jnp.sum(nw, axis=1, keepdims=True)
    own_den += jnp.sum(functools.reduce(jnp.add, tw), axis=1, keepdims=True)
    own_acc[...] = dot(nw.astype(BF16), news[:, HEAD:]) + dot(
        jnp.concatenate(tw, axis=1).astype(BF16), tails[:, HEAD:]
    )
    own_st[...] = jnp.where(iota((32, 128), 1) == 0, peak, own_den)

    for s in range(2):
        landed(s, 2, b_acc.at[s, 0])
    for s in range(2):
        landed(s, 3, b_acc.at[s, 1])
    st = weigh([home_ml] + [rx_ml[s, kind] for s in range(2) for kind in (2, 3)])
    cols = columns(st[0][0] + st[1][0] + [st[0][1], st[1][1], st[0][2], st[1][2]])[:chunk]
    lane_c = iota((chunk, 128), 1)
    t2v = jnp.zeros((2 * n * 16, HEAD + 128), F32)
    sr, sc = iota((2 * n * 16, chunk), 0), iota((2 * n * 16, chunk), 1)
    for c in range(2):
        sl = slice(c * HEAD, (c + 1) * HEAD)
        acc = home_acc[:, sl] * cols[:, 5 * c:5 * c + 1]
        for i in range(4):
            acc += b_acc[i // 2, i % 2, :, sl].astype(F32) * cols[:, 5 * c + 1 + i:5 * c + 2 + i]
        parts = split3(cols[:, 10 + c:11 + c]) + split3(cols[:, 12 + c:13 + c])
        tile = jnp.zeros((chunk, 128), F32)
        for i, col in enumerate(parts):
            tile = jnp.where(lane_c == i, col, tile)
        rowsrc = jnp.concatenate([acc, tile], axis=1).astype(BF16)
        inner = (sr & 15) - c * 8
        pick_rows = (inner >= 0) & (inner < reqs) & (lax.shift_right_logical(sr, 4) * reqs + inner == sc)
        t2v += dot(jnp.where(pick_rows, 1.0, 0.0).astype(BF16), rowsrc)
    t2[...] = t2v.astype(BF16).reshape(2 * n, 16, HEAD + 128)

    def home(pos, kk):
        return remote(
            t2.at[pos * 2 + kk], r2.at[k, p1], t2_send.at[pos * 2 + kk], t2_recv.at[k, p1],
            mine1(pos, kk),
        )

    for d in order:
        pos = lax.rem(p1 + d, n)
        for kk in range(2):
            start(home(pos, kk))
    start(home(p1, other))
    r2[k, p1] = t2[p1 * 2 + k]
    loads[2].wait()
    for d in range(1, n):
        for h in range(2):
            src = lax.rem((y, z)[h] + d, n)
            remote(t2.at[0], r2.at[h, src], t2_send.at[0], t2_recv.at[h, src], partner).wait_recv()
    src = p1_of(y, z, other)
    remote(t2.at[0], r2.at[other, src], t2_send.at[0], t2_recv.at[other, src], partner).wait_recv()

    heads = []
    for h in range(2):
        cells = [r2[h, i].astype(F32) for i in range(n)]
        ms = [t[:, HEAD:HEAD + 1] + t[:, HEAD + 1:HEAD + 2] + t[:, HEAD + 2:HEAD + 3] for t in cells]
        ds = [t[:, HEAD + 3:HEAD + 4] + t[:, HEAD + 4:HEAD + 5] + t[:, HEAD + 5:HEAD + 6] for t in cells]
        ms.append(own_st[h * 16:(h + 1) * 16, 0:1])
        ds.append(own_st[h * 16:(h + 1) * 16, 1:2])
        accs = [t[:, :HEAD] for t in cells] + [own_acc[h * 16:(h + 1) * 16]]
        mx = functools.reduce(jnp.maximum, ms)
        num = jnp.zeros((16, HEAD), F32)
        dn = jnp.zeros((16, 1), F32)
        for m, dd, acc in zip(ms, ds, accs):
            w = jnp.exp(m - mx)
            num += acc * w
            dn += dd * w
        heads.append(num / dn)
    att = jnp.concatenate(
        [jnp.concatenate([a[0:8], a[8:16]], axis=1) for a in heads], axis=0
    ).astype(BF16)

    ar[x] = dot(att, wv[...]).astype(BF16)

    def share(d):
        return remote(
            ar.at[x], ar.at[x], ar_send.at[d], ar_recv.at[x], (lax.rem(x + d, nx), b)
        )

    for d in range(1, nx):
        start(share(d))
    raw_h = hid_ref[...].astype(F32)
    for d in range(1, nx):
        src = lax.rem(x + nx - d, nx)
        remote(ar.at[src], ar.at[src], ar_send.at[d], ar_recv.at[src], partner).wait_recv()
    total_h = ar[0].astype(F32)
    for i in range(1, nx):
        total_h += ar[i].astype(F32)
    hid = [(raw_h[:, i, :] + total_h[8 * i:8 * i + reqs]).astype(BF16).astype(F32) for i in range(2)]
    out_ref[...] = jnp.stack(hid, axis=1).astype(BF16)
    last = hid[1]
    normed = last * lax.rsqrt(jnp.mean(last * last, axis=1, keepdims=True) + 1e-06) * gain_ref[...]
    sc_ref[...] = jnp.broadcast_to(jnp.sum(normed * score_ref[...], axis=1, keepdims=True), (reqs, 128))
    for copy in pending:
        copy.wait_send()


def p1_of(y, z, h):
    return y + h * (z - y)


def body(n, nx, prefix_pool, slot_page, prompt_len, request_ids, tail_len, tail_cache, queries,
         new_kv, hidden, out_weight, norm_gain, score_weight):
    pages = prefix_pool.shape[1]
    reqs, width = hidden.shape[0], hidden.shape[2]
    chunk = n * 2 * reqs
    rows = pages * SAMPLES
    total = n * chunk
    vm = pl.BlockSpec(memory_space=pltpu.VMEM)
    sm = pl.BlockSpec(memory_space=pltpu.SMEM)
    hbm = pl.BlockSpec(memory_space=pl.ANY)
    dma = pltpu.SemaphoreType.DMA
    out, sc = pl.pallas_call(
        functools.partial(kernel, n, nx, reqs, pages),
        out_shape=(
            jax.ShapeDtypeStruct((reqs, 2, width), BF16),
            jax.ShapeDtypeStruct((reqs, 128), F32),
        ),
        in_specs=[sm, sm, sm, vm, vm, vm, vm, vm, vm, hbm, hbm, hbm],
        out_specs=(vm, vm),
        scratch_shapes=[
            pltpu.VMEM((2, 16, HEAD), BF16),
            pltpu.VMEM((pages, PAGE, 2 * HEAD), BF16),
            pltpu.VMEM((reqs, 128, 2 * HEAD), BF16),
            pltpu.VMEM((2 * HEAD, width), BF16),
            pltpu.VMEM((2 * n, 16, HEAD), BF16),
            pltpu.VMEM((n, chunk, 512), BF16),
            pltpu.VMEM((n, chunk, 512), BF16),
            pltpu.VMEM((n, rows, chunk), BF16),
            pltpu.VMEM((n, rows, chunk), BF16),
            pltpu.VMEM((total, 2 * rows), BF16),
            pltpu.VMEM((2, rows, 512), F32),
            pltpu.VMEM((2 * rows, 512), BF16),
            pltpu.VMEM((rows, 512), BF16),
            pltpu.VMEM((24, 2 * rows), BF16),
            pltpu.VMEM((2, 8, rows), F32),
            pltpu.VMEM((8, rows), F32),
            pltpu.VMEM((8, rows), F32),
            pltpu.VMEM((8, rows), F32),
            pltpu.VMEM((8, rows), F32),
            pltpu.VMEM((7, chunk, 512), BF16),
            pltpu.VMEM((7, 8, 128), F32),
            pltpu.VMEM((2, chunk, 512), BF16),
            pltpu.VMEM((2, chunk // 2, 512), BF16),
            pltpu.VMEM((2, 2, chunk, 512), BF16),
            pltpu.VMEM((2, 4, 8, 128), F32),
            pltpu.VMEM((2 * n, 16, HEAD + 128), BF16),
            pltpu.VMEM((2, n, 16, HEAD + 128), BF16),
            pltpu.VMEM((32, HEAD), F32),
            pltpu.VMEM((32, 128), F32),
            pltpu.VMEM((nx, 16, width), BF16),
            dma((3,)), dma((2 * n,)), dma((2 * n,)),
            dma((2, 4, 2)), dma((2, 4, 2)), dma((n, 2)), dma((n, 2)),
            dma((3 + pages // 8,)), dma((3 + pages // 8,)),
            dma((2, 4)), dma((2, 4)), dma((2, 4)), dma((2, 4)),
            dma((2 * n,)), dma((2, n)), dma((nx,)), dma((nx,)),
        ],
        compiler_params=pltpu.CompilerParams(collective_id=0, has_side_effects=True),
    )(
        slot_page, prompt_len, tail_len, request_ids.reshape(1, -1), queries, new_kv[0], hidden,
        norm_gain.reshape(1, -1), score_weight.reshape(1, -1), prefix_pool[0], tail_cache[0], out_weight,
    )
    return out, sc[:, 0]


def solution(mesh):
    nx = mesh.shape["kv"]
    n = int(round((mesh.shape["blk"] // 2) ** 0.5))
    in_specs = (
        P("kv", "blk", None, None),
        P("blk"),
        P(),
        P(),
        P("blk"),
        P("kv", "blk", None, None),
        P("blk", None, "kv"),
        P("kv", "blk", None, None),
        P("blk", None, None),
        P("kv", None),
        P(),
        P(),
    )
    out_specs = (P("blk", None, None), P("blk"))
    return jax.shard_map(
        functools.partial(body, n, nx), mesh=mesh, in_specs=in_specs, out_specs=out_specs, check_vma=False
    )
```

```python
import functools

import jax
import jax.numpy as jnp
from jax import lax
from jax.experimental import pallas as pl
from jax.experimental.pallas import tpu as pltpu
from jax.sharding import PartitionSpec as P

MESH = pl.DeviceIdType.MESH
SAMPLES = 16
HEAD = 256
PAGE = 64
NEG = -1e30
F32 = jnp.float32
BF16 = jnp.bfloat16


def iota(shape, dim):
    return lax.broadcasted_iota(jnp.int32, shape, dim)


def dot(a, b, ca=1, cb=0):
    return lax.dot_general(a, b, (((ca,), (cb,)), ((), ())), preferred_element_type=F32)


def floor_div(a, c):
    return jnp.floor((a.astype(F32) + 0.5) * (1.0 / c))


def split3(x):
    a = x.astype(BF16).astype(F32)
    b = (x - a).astype(BF16).astype(F32)
    return a, b, x - a - b


def kernel(
    n, nx, reqs, pages,
    slot_hbm, plen_hbm, tlen_hbm, ids_hbm, q_hbm, nk_hbm, pool_hbm, tail_hbm, w_hbm,
    out_ref,
    slot_ref, plen_ref, tlen_ref, ids_ref, q_in, nk_ref,
    q_ref, poolv, tailv, wv, s1, agm, gm, gt, pick, accm, stats, info_tx, info_rx,
    tx_acc, tx_ml, a3_acc, a4_acc, b_acc, rx_ml, t2, r2, own_acc, own_st, ar, ar_rx,
    local_sem, s1_send, s1_recv, ag_send, ag_recv,
    cx_send, cx_recv, rs_send, rs_recv, rm_send, rm_recv,
    t2_send, t2_recv, ar_send, ar_recv,
):
    chunk = n * 2 * reqs
    half = chunk // 2
    rows = pages * SAMPLES
    prompts = plen_ref.shape[0]
    scale = HEAD ** (-0.5)
    x = lax.axis_index("kv")
    b = lax.axis_index("blk")
    k = lax.rem(b, 2)
    y = lax.rem(lax.div(b, 2), n)
    z = lax.div(b, 2 * n)
    p1 = y + k * (z - y)
    p2 = z + k * (y - z)
    other = 1 - k

    def at(zz, yy, kk):
        return (x, (zz * n + yy) * 2 + kk)

    def ring1(pos, h, kk):
        if h == 0:
            return at(z, pos, kk)
        return at(pos, y, kk)

    def mine1(pos, kk):
        return at(z + k * (pos - z), pos + k * (y - pos), kk)

    def mine2(d):
        pos = lax.rem(p2 + (d + n), n)
        return at(pos + k * (z - pos), y + k * (pos - y), k)

    def near(d):
        return lax.rem(p2 + (d + n), n)

    partner = at(z, y, other)

    def remote(src, dst, send, recv, to):
        return pltpu.make_async_remote_copy(
            src_ref=src, dst_ref=dst, send_sem=send, recv_sem=recv, device_id=to, device_id_type=MESH
        )

    pending = []

    def start(copy):
        copy.start()
        pending.append(copy)

    barrier = pltpu.get_barrier_semaphore()

    def greet(to):
        pl.semaphore_signal(barrier, inc=1, device_id=to, device_id_type=MESH)

    for d in [i for j in range(1, n // 2 + 1) for i in ((j, n - j) if 2 * j != n else (j,))]:
        for kk in range(2):
            greet(at(z, lax.rem(y + d, n), kk))
            greet(at(lax.rem(z + d, n), y, kk))
    greet(partner)
    if nx > 1:
        greet((x + 1 - 2 * lax.rem(x, 2), b))
    if nx > 2:
        greet((nx - 1 - x, b))

    loads = [
        pltpu.make_async_copy(src, dst, local_sem.at[i])
        for i, (src, dst) in enumerate([
            (q_hbm, q_in), (plen_hbm, plen_ref), (slot_hbm, slot_ref), (ids_hbm, ids_ref),
            (pool_hbm, poolv.at[pl.ds(0, pages)]), (tlen_hbm, tlen_ref), (nk_hbm, nk_ref),
            (tail_hbm, tailv), (w_hbm, wv),
        ])
    ]
    for load in loads:
        load.start()
    loads[0].wait()

    raw = q_in[...].astype(F32)
    gap = jnp.zeros((8 - reqs, HEAD), F32)
    for i in range(2):
        q_ref[i] = jnp.concatenate(
            [raw[:, i, 0:HEAD], gap, raw[:, i, HEAD:2 * HEAD], gap], axis=0
        ).astype(BF16)
    s1[p1 * 2 + k] = q_ref[k]

    pl.semaphore_wait(barrier, 1 + 4 * (n - 1) + min(nx - 1, 2))

    def first(h, d):
        mypos = (y, z)[h]
        pos = lax.rem(mypos + d, n)
        slot = mypos * 2 + k
        return remote(
            q_ref.at[h], s1.at[slot], s1_send.at[h * n + d], s1_recv.at[slot], ring1(pos, h, h)
        )

    order = [d for i in range(n // 2, 0, -1) for d in ((i, n - i) if 2 * i != n else (i,))]
    for d in order:
        for h in range(2):
            start(first(h, d))
    slot = p1_of(y, z, other) * 2 + k
    start(remote(q_ref.at[other], s1.at[slot], s1_send.at[other * n], s1_recv.at[slot], partner))

    swap = remote(pool_hbm, poolv.at[pl.ds(pages, pages)], cx_send.at[0], cx_recv.at[0], partner)
    start(swap)

    loads[1].wait()
    loads[2].wait()
    lane = iota((1, 128), 1)
    lens = jnp.zeros((1, 128), jnp.int32)
    for p in range(prompts):
        lens = jnp.where(lane == p, plen_ref[p], lens)
    need = lax.shift_right_logical(lens + (PAGE - 1), 6).astype(F32)
    grid_r, grid_c = iota((128, 128), 0), iota((128, 128), 1)
    need_t = jnp.transpose(jnp.broadcast_to(need, (128, 128)))
    ends = jnp.sum(jnp.where(grid_r <= grid_c, need_t, 0.0), axis=0, keepdims=True)
    starts = ends - need
    page_r = iota((pages, 128), 0)
    slots = jnp.zeros((pages, 128), jnp.int32)
    for j in range(pages):
        slots = jnp.where(page_r == j, slot_ref[j], slots)
    slots = slots.astype(F32)
    plane = iota((pages, 128), 1)
    owner = jnp.sum(
        jnp.where((plane < prompts) & (slots >= ends), 1.0, 0.0), axis=1, keepdims=True
    )
    used = owner < prompts
    owner = jnp.minimum(owner, prompts - 1.0)
    mine = plane.astype(F32) == owner
    begin = jnp.sum(jnp.where(mine, starts, 0.0), axis=1, keepdims=True)
    length = jnp.sum(jnp.where(mine, lens.astype(F32), 0.0), axis=1, keepdims=True)
    live = jnp.where(used, length - (slots - begin) * PAGE, 0.0)
    info_tx[0] = owner * SAMPLES + jnp.zeros_like(slots)
    info_tx[1] = live + jnp.zeros_like(slots)
    info = remote(info_tx, info_rx, cx_send.at[1], cx_recv.at[1], partner)
    start(info)

    pr, pc = iota((chunk, 2 * n * 16), 0), iota((chunk, 2 * n * 16), 1).astype(F32)
    cell = floor_div(pr, reqs)
    want = cell * 16.0 + (pr.astype(F32) - cell * reqs)
    for d in range(n):
        for kk in range(2):
            slot = lax.rem(p1 + d, n) * 2 + lax.rem(k + kk, 2)
            if d or kk:
                remote(q_ref.at[0], s1.at[slot], s1_send.at[0], s1_recv.at[slot], partner).wait_recv()
    s1v = s1[...].reshape(2 * n * 16, HEAD)
    packed = [
        dot(jnp.where(pc == want + c * 8.0, 1.0, 0.0).astype(BF16), s1v) for c in range(2)
    ]
    agm[p2] = jnp.concatenate(packed, axis=1).astype(BF16)

    def part(src, piece):
        return agm.at[src, pl.ds(piece * half, half)]

    def second(src, s, hop, kind, piece):
        return remote(
            part(src, piece), part(src, piece), ag_send.at[s, kind, piece], ag_recv.at[s, kind, piece],
            mine2((1, -1)[s] * hop),
        )

    def arrived(s, kind, piece):
        src = near(-(1, -1)[s] * (kind + 1))
        second(src, s, 1, kind, piece).wait_recv()
        return src

    for i in range(2):
        for s in range(2):
            start(second(p2, s, 2, 1, i ^ s))
    for i in range(2):
        for s in range(2):
            start(second(p2, s, 1, 0, i ^ s))

    total = n * chunk
    loads[3].wait()
    ids = ids_ref[...].reshape(1, total)
    grid_u = iota((n * n, total), 0).astype(F32)
    grid_e = iota((n * n, total), 1)
    on = floor_div(grid_e, 2 * reqs) == grid_u
    e_in = iota((total, 128), 0)
    e_mod = e_in.astype(F32) - floor_div(e_in, 2 * reqs) * (2 * reqs)
    l_in = iota((1, 128), 1)
    l_div = floor_div(l_in, 2 * reqs)
    l_mod = l_in.astype(F32) - l_div * (2 * reqs)
    spread_e = jnp.where(e_mod == l_mod, 1.0, 0.0).astype(BF16)
    hi = jnp.where(on, lax.shift_right_logical(ids, 5).astype(F32), 0.0).astype(BF16)
    lo = jnp.where(on, (ids & 31).astype(F32), 0.0).astype(BF16)
    table = dot(hi, spread_e) * 32.0 + dot(lo, spread_e)
    nat = jnp.concatenate(
        [
            jnp.sum(
                jnp.where(iota((n, 128), 0).astype(F32) == l_div, table[i * n:(i + 1) * n], 0.0),
                axis=0, keepdims=True,
            )
            for i in range(n)
        ],
        axis=0,
    )
    perm = jnp.zeros((n, 128), F32)
    for i in range(n):
        perm = jnp.where(l_div == float(i), table[i * n:(i + 1) * n], perm)
    ids_m = jnp.where(k == 0, nat, perm)
    info.wait_recv()
    pair = 2 * pages
    sample = (iota((2 * rows, 128), 0) & (SAMPLES - 1)).astype(F32)

    def per_row(i):
        v = jnp.concatenate([info_tx[i], info_rx[i]], axis=0)
        return jnp.broadcast_to(v[:, None, :], (pair, SAMPLES, 128)).reshape(2 * rows, 128)

    target = per_row(0) + sample
    live_c = per_row(1)
    for p in range(n):
        gm[p] = jnp.where(target[:, :chunk] == ids_m[p:p + 1, :chunk], 1.0, 0.0).astype(BF16)

    for i in range(2):
        for s in range(2):
            piece = i ^ s
            src = arrived(s, 1, piece)
            if i == 0:
                start(second(src, s, 2, 3, piece))
            start(second(src, s, 1, 2, piece))
    pick[...] = dot(gm[p2], agm[p2])

    def take(d):
        src = near(d)
        pick[...] += dot(gm[src], agm[src])

    for s in range(2):
        take((-2, 2)[s])
    target_row = jnp.concatenate(
        [jnp.transpose(target[i * 128:(i + 1) * 128])[0:8] for i in range(2 * rows // 128)], axis=1
    )
    live_row = jnp.concatenate(
        [jnp.transpose(live_c[i * 128:(i + 1) * 128])[0:1] for i in range(2 * rows // 128)], axis=1
    )
    both_t = jnp.concatenate([target_row[0:4, :rows], target_row[0:4, rows:]], axis=0)
    swap_t = jnp.concatenate([target_row[0:4, rows:], target_row[0:4, :rows]], axis=0)
    lane8 = iota((8, rows), 1)
    lower = iota((8, rows), 0) >= 4
    lead = jnp.where(lower & (swap_t == both_t), 0.0, 1.0)
    for d in range(1, pages):
        same = pltpu.roll(both_t, d * SAMPLES, 1) == both_t
        cross = pltpu.roll(swap_t, d * SAMPLES, 1) == both_t
        lead = jnp.where((same & (lane8 >= d * SAMPLES)) | (cross & lower), 0.0, lead)
    ids_t = jnp.transpose(jnp.concatenate([ids_m, jnp.zeros((128 - n, 128), F32)], axis=0))
    for p in range(n):
        gt[pl.ds(p * chunk, chunk), :] = jnp.where(
            ids_t[:chunk, p:p + 1] == target_row[0:1], 1.0, 0.0
        ).astype(BF16)
    for i in range(2):
        for s in range(2):
            arrived(s, 0, i ^ s)
    for s in range(2):
        take((-1, 1)[s])
    for i in range(2):
        for s in range(2):
            arrived(s, 2, i ^ s)
    for s in range(2):
        take((-3, 3)[s])
    for s in range(2):
        arrived(s, 3, s)
    take(4)

    loads[4].wait()
    swap.wait_recv()
    blocks = pair // 8
    scores, peaks = [], []
    page_l = lax.shift_right_logical(iota((PAGE, 256), 1) & 127, 4)
    for blk in range(blocks):
        keys = poolv[blk * 8:(blk + 1) * 8].reshape(8 * PAGE, 2 * HEAD)[:, :HEAD]
        sl = slice(blk * 128, (blk + 1) * 128)
        qb = jnp.concatenate([pick[sl, :HEAD], pick[sl, HEAD:]], axis=0).astype(BF16)
        full = dot(keys, qb, 1, 1)
        s = jnp.zeros((PAGE, 256), F32)
        for j in range(8):
            s = jnp.where(page_l == j, full[j * PAGE:(j + 1) * PAGE], s)
        lv = jnp.concatenate([live_row[:, sl]] * 2, axis=1)
        alive = iota((PAGE, 256), 0).astype(F32) < lv
        s = jnp.where(alive, s * scale, NEG)
        scores.append((s, alive))
        m = jnp.max(s, axis=0, keepdims=True)
        peaks.append(jnp.concatenate([m[:, :128], m[:, 128:]], axis=0))
    hb = blocks // 2
    low, high = jnp.concatenate(peaks[:hb], axis=1), jnp.concatenate(peaks[hb:], axis=1)

    both_m = jnp.concatenate([low, low, high, high], axis=0)
    swap_m = jnp.concatenate([high, high, low, low], axis=0)
    top = jnp.where(swap_t == both_t, jnp.maximum(both_m, swap_m), both_m)
    for d in range(1, pages):
        same = pltpu.roll(both_t, d * SAMPLES, 1) == both_t
        cross = pltpu.roll(swap_t, d * SAMPLES, 1) == both_t
        top = jnp.where(same, jnp.maximum(top, pltpu.roll(both_m, d * SAMPLES, 1)), top)
        top = jnp.where(cross, jnp.maximum(top, pltpu.roll(swap_m, d * SAMPLES, 1)), top)

    dens = []
    page_r8 = lax.shift_right_logical(iota((256, 8 * PAGE), 0) & 127, 4)
    own_page = page_r8 == lax.shift_right_logical(iota((256, 8 * PAGE), 1), 6)
    for blk in range(blocks):
        s, alive = scores[blk]
        base = 4 * (blk // hb)
        tb = top[base:base + 2, (blk % hb) * 128:(blk % hb + 1) * 128]
        tb = jnp.concatenate([tb[0:1], tb[1:2]], axis=1)
        w = jnp.where(alive, jnp.exp(s - tb), 0.0)
        dsum = jnp.sum(w, axis=0, keepdims=True)
        dens.append(jnp.concatenate([dsum[:, :128], dsum[:, 128:]], axis=0))
        wt = jnp.transpose(w)
        wt = jnp.concatenate([wt, wt], axis=1)
        wide = jnp.where(own_page, jnp.concatenate([wt] * 4, axis=1), 0.0).astype(BF16)
        values = poolv[blk * 8:(blk + 1) * 8].reshape(8 * PAGE, 2 * HEAD)[:, HEAD:]
        acc = dot(wide, values).astype(BF16)
        accm[blk * 128:(blk + 1) * 128, :HEAD] = acc[:128]
        accm[blk * 128:(blk + 1) * 128, HEAD:] = acc[128:]
    st = jnp.concatenate(
        [
            jnp.concatenate([jnp.where(lead[0:2] > 0.5, top[0:2], 0.0),
                             jnp.where(lead[4:6] > 0.5, top[4:6], 0.0)], axis=1),
            jnp.concatenate(dens, axis=1),
            jnp.concatenate([lead[0:1], lead[4:5]], axis=1),
            jnp.zeros((3, 2 * rows), F32),
        ],
        axis=0,
    )
    stats[...] = jnp.concatenate(split3(st), axis=0).astype(BF16)

    sub8 = iota((8, 128), 0)

    def sums(d):
        g = gt[pl.ds(pl.multiple_of(near(d) * chunk, chunk), chunk), :]
        acc = dot(g, accm[...])
        ml = dot(stats[...], g, 1, 1)
        ml = ml[0:8] + ml[8:16] + ml[16:24]
        ml = jnp.concatenate([ml, jnp.zeros((8, 128 - chunk), F32)], axis=1)
        return acc, jnp.where((sub8 < 2) & (ml[4:5] < 0.5), NEG, ml)

    def ring(s, kind, src, dst, hop):
        to = mine2((1, -1)[s] * hop)
        return (
            remote(src[0], dst, rs_send.at[s, kind], rs_recv.at[s, kind], to),
            remote(src[1], rx_ml.at[s, kind], rm_send.at[s, kind], rm_recv.at[s, kind], to),
        )

    def landed(s, kind, dst):
        for copy in ring(s, kind, (dst, rx_ml.at[s, kind]), dst, 1):
            copy.wait_recv()

    def store(i, d):
        acc, ml = sums(d)
        tx_acc[i] = acc.astype(BF16)
        tx_ml[i] = ml

    store(2, 4)
    for s in range(2):
        for copy in ring(s, 1, (tx_acc.at[2, pl.ds(s * half, half)], tx_ml.at[2]), a4_acc.at[s], 2):
            start(copy)
    for s in range(2):
        store(s, (3, -3)[s])
        for copy in ring(s, 0, (tx_acc.at[s], tx_ml.at[s]), a3_acc.at[s], 1):
            start(copy)
    for s in range(2):
        store(3 + s, (1, -1)[s])
        for copy in ring(s, 2, (tx_acc.at[3 + s], tx_ml.at[3 + s]), b_acc.at[s, 0], 1):
            start(copy)

    def weigh(mls):
        out = []
        for c in range(2):
            mx = functools.reduce(jnp.maximum, [m[c:c + 1] for m in mls])
            w = [jnp.exp(m[c:c + 1] - mx) for m in mls]
            dn = functools.reduce(jnp.add, [a * m[2 + c:3 + c] for a, m in zip(w, mls)])
            out.append((w, mx, dn))
        return out

    def columns(items):
        return jnp.transpose(
            jnp.concatenate(items + [jnp.zeros((128 - len(items), 128), F32)], axis=0)
        )

    lane128 = iota((8, 128), 1)
    for s in range(2):
        acc, ml = sums((2, -2)[s])
        landed(s, 0, a3_acc.at[s])
        landed(s, 1, a4_acc.at[s])
        inside = (lane128 < half) if s == 0 else (lane128 >= half)
        ml4 = jnp.where((sub8 < 2) & jnp.logical_not(inside), NEG, rx_ml[s, 1])
        mls = [ml, rx_ml[s, 0], ml4]
        st = weigh(mls)
        cols = columns(st[0][0] + st[1][0])
        outs = []
        for c in range(2):
            sl = slice(c * HEAD, (c + 1) * HEAD)
            a3 = a3_acc[s, :, sl].astype(F32)
            a4 = a4_acc[s, :, sl].astype(F32)
            v = acc[:, sl] * cols[:chunk, 3 * c:3 * c + 1] + a3 * cols[:chunk, 3 * c + 1:3 * c + 2]
            add = a4 * cols[s * half:(s + 1) * half, 3 * c + 2:3 * c + 3]
            if s == 0:
                v = jnp.concatenate([v[:half] + add, v[half:]], axis=0)
            else:
                v = jnp.concatenate([v[:half], v[half:] + add], axis=0)
            outs.append(v)
        tx_acc[5 + s] = jnp.concatenate(outs, axis=1).astype(BF16)
        tx_ml[5 + s] = jnp.concatenate(
            [st[0][1], st[1][1], st[0][2], st[1][2], jnp.zeros((4, 128), F32)], axis=0
        )
        for copy in ring(s, 3, (tx_acc.at[5 + s], tx_ml.at[5 + s]), b_acc.at[s, 1], 2):
            start(copy)
    home_acc, home_ml = sums(0)

    loads[5].wait()
    loads[6].wait()
    loads[7].wait()
    qown = jnp.concatenate([q_ref[0], q_ref[1]], axis=0)
    tails = tailv[...].reshape(reqs * 128, 2 * HEAD)
    row32 = iota((32, 128), 0) & 7
    ts, tl = [], []
    for r in range(reqs):
        ok = (row32 == r) & (iota((32, 128), 1) < tlen_ref[r])
        tl.append(ok)
        ts.append(jnp.where(ok, dot(qown, tails[r * 128:(r + 1) * 128, :HEAD], 1, 1) * scale, NEG))
    fresh = nk_ref[...].astype(F32)
    pad = jnp.zeros((8 - reqs, 2 * HEAD), F32)
    news = jnp.concatenate([fresh[:, 0, :], pad, fresh[:, 1, :], pad], axis=0).astype(BF16)
    nrow, ncol = iota((32, 16), 0), iota((32, 16), 1)
    nlive = ((nrow & 7) == (ncol & 7)) & (lax.shift_right_logical(ncol, 3) <= lax.shift_right_logical(nrow, 4))
    ns = jnp.where(nlive, dot(qown, news[:, :HEAD], 1, 1) * scale, NEG)
    peak = jnp.max(ns, axis=1, keepdims=True)
    peak = jnp.maximum(peak, jnp.max(functools.reduce(jnp.maximum, ts), axis=1, keepdims=True))
    nw = jnp.where(nlive, jnp.exp(ns - peak), 0.0)
    tw = [jnp.where(ok, jnp.exp(t - peak), 0.0) for t, ok in zip(ts, tl)]
    own_den = jnp.sum(nw, axis=1, keepdims=True)
    own_den += jnp.sum(functools.reduce(jnp.add, tw), axis=1, keepdims=True)
    own_acc[...] = dot(nw.astype(BF16), news[:, HEAD:]) + dot(
        jnp.concatenate(tw, axis=1).astype(BF16), tails[:, HEAD:]
    )
    own_st[...] = jnp.where(iota((32, 128), 1) == 0, peak, own_den)

    for s in range(2):
        landed(s, 2, b_acc.at[s, 0])
    for s in range(2):
        landed(s, 3, b_acc.at[s, 1])
    st = weigh([home_ml] + [rx_ml[s, kind] for s in range(2) for kind in (2, 3)])
    cols = columns(st[0][0] + st[1][0] + [st[0][1], st[1][1], st[0][2], st[1][2]])[:chunk]
    lane_c = iota((chunk, 128), 1)
    t2v = jnp.zeros((2 * n * 16, HEAD + 128), F32)
    sr, sc = iota((2 * n * 16, chunk), 0), iota((2 * n * 16, chunk), 1)
    for c in range(2):
        sl = slice(c * HEAD, (c + 1) * HEAD)
        acc = home_acc[:, sl] * cols[:, 5 * c:5 * c + 1]
        for i in range(4):
            acc += b_acc[i // 2, i % 2, :, sl].astype(F32) * cols[:, 5 * c + 1 + i:5 * c + 2 + i]
        parts = split3(cols[:, 10 + c:11 + c]) + split3(cols[:, 12 + c:13 + c])
        tile = jnp.zeros((chunk, 128), F32)
        for i, col in enumerate(parts):
            tile = jnp.where(lane_c == i, col, tile)
        rowsrc = jnp.concatenate([acc, tile], axis=1).astype(BF16)
        inner = (sr & 15) - c * 8
        pick_rows = (inner >= 0) & (inner < reqs) & (lax.shift_right_logical(sr, 4) * reqs + inner == sc)
        t2v += dot(jnp.where(pick_rows, 1.0, 0.0).astype(BF16), rowsrc)
    t2[...] = t2v.astype(BF16).reshape(2 * n, 16, HEAD + 128)

    def home(pos, kk):
        return remote(
            t2.at[pos * 2 + kk], r2.at[k, p1], t2_send.at[pos * 2 + kk], t2_recv.at[k, p1],
            mine1(pos, kk),
        )

    for d in order:
        pos = lax.rem(p1 + d, n)
        for kk in range(2):
            start(home(pos, kk))
    start(home(p1, other))
    r2[k, p1] = t2[p1 * 2 + k]
    loads[8].wait()
    for d in range(1, n):
        for h in range(2):
            src = lax.rem((y, z)[h] + d, n)
            remote(t2.at[0], r2.at[h, src], t2_send.at[0], t2_recv.at[h, src], partner).wait_recv()
    src = p1_of(y, z, other)
    remote(t2.at[0], r2.at[other, src], t2_send.at[0], t2_recv.at[other, src], partner).wait_recv()

    heads = []
    for h in range(2):
        cells = [r2[h, i].astype(F32) for i in range(n)]
        ms = [t[:, HEAD:HEAD + 1] + t[:, HEAD + 1:HEAD + 2] + t[:, HEAD + 2:HEAD + 3] for t in cells]
        ds = [t[:, HEAD + 3:HEAD + 4] + t[:, HEAD + 4:HEAD + 5] + t[:, HEAD + 5:HEAD + 6] for t in cells]
        ms.append(own_st[h * 16:(h + 1) * 16, 0:1])
        ds.append(own_st[h * 16:(h + 1) * 16, 1:2])
        accs = [t[:, :HEAD] for t in cells] + [own_acc[h * 16:(h + 1) * 16]]
        mx = functools.reduce(jnp.maximum, ms)
        num = jnp.zeros((16, HEAD), F32)
        dn = jnp.zeros((16, 1), F32)
        for m, dd, acc in zip(ms, ds, accs):
            w = jnp.exp(m - mx)
            num += acc * w
            dn += dd * w
        heads.append(num / dn)
    att = jnp.concatenate(
        [jnp.concatenate([a[0:8], a[8:16]], axis=1) for a in heads], axis=0
    ).astype(BF16)

    hw = wv.shape[1] // 2
    even = x + 1 - 2 * lax.rem(x, 2)
    odd = nx - 1 - x
    if nx == 1:
        for i in range(2):
            out_ref[0, i] = dot(att, wv[:, i * hw:(i + 1) * hw]).astype(BF16)
            out_ref[1, i] = jnp.zeros((16, hw), BF16)
    else:
        def trade(i, turn):
            src = ar.at[i] if turn == 0 else out_ref.at[0, i]
            dst = ar_rx.at[i] if turn == 0 else out_ref.at[1, i]
            to = even if (i + turn) % 2 == 0 else odd
            return remote(src, dst, ar_send.at[turn, i], ar_recv.at[turn, i], (to, b))

        for i in range(2):
            ar[i] = dot(att, wv[:, i * hw:(i + 1) * hw]).astype(BF16)
            start(trade(i, 0))
        for i in range(2):
            trade(i, 0).wait_recv()
            out_ref[0, i] = (ar[i].astype(F32) + ar_rx[i].astype(F32)).astype(BF16)
            if nx > 2:
                start(trade(i, 1))
            else:
                out_ref[1, i] = jnp.zeros((16, hw), BF16)
        for i in range(2):
            if nx > 2:
                trade(i, 1).wait_recv()
    for copy in pending:
        copy.wait_send()


def finish(sum_ref, hid_ref, gain_ref, score_ref, out_ref, sc_ref):
    reqs = hid_ref.shape[0]
    raw = hid_ref[...].astype(F32)
    total = jnp.concatenate(
        [sum_ref[0, i].astype(F32) + sum_ref[1, i].astype(F32) for i in range(2)], axis=1
    )
    hid = [(raw[:, i, :] + total[8 * i:8 * i + reqs]).astype(BF16).astype(F32) for i in range(2)]
    out_ref[...] = jnp.stack(hid, axis=1).astype(BF16)
    last = hid[1]
    normed = last * lax.rsqrt(jnp.mean(last * last, axis=1, keepdims=True) + 1e-06) * gain_ref[...]
    score = jnp.sum(normed * score_ref[...], axis=1, keepdims=True)
    tile = jnp.concatenate([jnp.broadcast_to(score, (reqs, 128)), jnp.zeros((128 - reqs, 128), F32)], axis=0)
    sc_ref[...] = jnp.transpose(tile)[0, :reqs]


def p1_of(y, z, h):
    return y + h * (z - y)


def body(n, nx, prefix_pool, slot_page, prompt_len, request_ids, tail_len, tail_cache, queries,
         new_kv, hidden, out_weight, norm_gain, score_weight):
    pages = prefix_pool.shape[1]
    reqs, width = hidden.shape[0], hidden.shape[2]
    chunk = n * 2 * reqs
    rows = pages * SAMPLES
    total = n * chunk
    vm = pl.BlockSpec(memory_space=pltpu.VMEM)
    hbm = pl.BlockSpec(memory_space=pl.ANY)
    dma = pltpu.SemaphoreType.DMA
    sums = pl.pallas_call(
        functools.partial(kernel, n, nx, reqs, pages),
        out_shape=jax.ShapeDtypeStruct((2, 2, 16, width // 2), BF16),
        in_specs=[hbm] * 9,
        out_specs=vm,
        scratch_shapes=[
            pltpu.SMEM(slot_page.shape, jnp.int32),
            pltpu.SMEM(prompt_len.shape, jnp.int32),
            pltpu.SMEM(tail_len.shape, jnp.int32),
            pltpu.VMEM(request_ids.shape, jnp.int32),
            pltpu.VMEM(queries.shape, BF16),
            pltpu.VMEM(new_kv.shape[1:], BF16),
            pltpu.VMEM((2, 16, HEAD), BF16),
            pltpu.VMEM((2 * pages, PAGE, 2 * HEAD), BF16),
            pltpu.VMEM((reqs, 128, 2 * HEAD), BF16),
            pltpu.VMEM((2 * HEAD, width), BF16),
            pltpu.VMEM((2 * n, 16, HEAD), BF16),
            pltpu.VMEM((n, chunk, 512), BF16),
            pltpu.VMEM((n, 2 * rows, chunk), BF16),
            pltpu.VMEM((total, 2 * rows), BF16),
            pltpu.VMEM((2 * rows, 512), F32),
            pltpu.VMEM((2 * rows, 512), BF16),
            pltpu.VMEM((24, 2 * rows), BF16),
            pltpu.VMEM((2, pages, 128), F32),
            pltpu.VMEM((2, pages, 128), F32),
            pltpu.VMEM((7, chunk, 512), BF16),
            pltpu.VMEM((7, 8, 128), F32),
            pltpu.VMEM((2, chunk, 512), BF16),
            pltpu.VMEM((2, chunk // 2, 512), BF16),
            pltpu.VMEM((2, 2, chunk, 512), BF16),
            pltpu.VMEM((2, 4, 8, 128), F32),
            pltpu.VMEM((2 * n, 16, HEAD + 128), BF16),
            pltpu.VMEM((2, n, 16, HEAD + 128), BF16),
            pltpu.VMEM((32, HEAD), F32),
            pltpu.VMEM((32, 128), F32),
            pltpu.VMEM((2, 16, width // 2), BF16),
            pltpu.VMEM((2, 16, width // 2), BF16),
            dma((9,)), dma((2 * n,)), dma((2 * n,)),
            dma((2, 4, 2)), dma((2, 4, 2)),
            dma((2,)), dma((2,)),
            dma((2, 4)), dma((2, 4)), dma((2, 4)), dma((2, 4)),
            dma((2 * n,)), dma((2, n)), dma((2, 2)), dma((2, 2)),
        ],
        compiler_params=pltpu.CompilerParams(collective_id=0, has_side_effects=True),
    )(
        slot_page, prompt_len, tail_len, request_ids, queries, new_kv[0],
        prefix_pool[0], tail_cache[0], out_weight,
    )
    return pl.pallas_call(
        finish,
        out_shape=(jax.ShapeDtypeStruct(hidden.shape, BF16), jax.ShapeDtypeStruct((reqs,), F32)),
        in_specs=[vm] * 4,
        out_specs=(vm, vm),
    )(sums, hidden, norm_gain.reshape(1, -1), score_weight.reshape(1, -1))


def solution(mesh):
    nx = mesh.shape["kv"]
    n = int(round((mesh.shape["blk"] // 2) ** 0.5))
    in_specs = (
        P("kv", "blk", None, None),
        P("blk"),
        P(),
        P(),
        P("blk"),
        P("kv", "blk", None, None),
        P("blk", None, "kv"),
        P("kv", "blk", None, None),
        P("blk", None, None),
        P("kv", None),
        P(),
        P(),
    )
    out_specs = (P("blk", None, None), P("blk"))
    return jax.shard_map(
        functools.partial(body, n, nx), mesh=mesh, in_specs=in_specs, out_specs=out_specs, check_vma=False
    )
```

```python
import functools

import jax
import jax.numpy as jnp
from jax import lax
from jax.experimental import pallas as pl
from jax.experimental.pallas import tpu as pltpu
from jax.sharding import PartitionSpec as P

MESH = pl.DeviceIdType.MESH
SAMPLES = 16
HEAD = 256
PAGE = 64
NEG = -1e30
F32 = jnp.float32
BF16 = jnp.bfloat16


def iota(shape, dim):
    return lax.broadcasted_iota(jnp.int32, shape, dim)


def dot(a, b, ca=1, cb=0):
    return lax.dot_general(a, b, (((ca,), (cb,)), ((), ())), preferred_element_type=F32)


def floor_div(a, c):
    return jnp.floor((a.astype(F32) + 0.5) * (1.0 / c))


def split3(x):
    a = x.astype(BF16).astype(F32)
    b = (x - a).astype(BF16).astype(F32)
    return a, b, x - a - b


def kernel(
    n, nx, reqs, pages,
    slot_hbm, plen_hbm, tlen_hbm, ids_hbm, q_hbm, nk_hbm, pool_hbm, tail_hbm, w_hbm,
    out_ref,
    slot_ref, plen_ref, tlen_ref, ids_ref, q_in, nk_ref,
    q_ref, poolv, tailv, wv, s1, agm, gm, gt, pick, accm, stats, info_tx, info_rx,
    tx_acc, tx_ml, a3_acc, a4_acc, b_acc, rx_ml, t2, r2, own_acc, own_st, ar, ar_rx,
    local_sem, s1_send, s1_recv, ag_send, ag_recv,
    cx_send, cx_recv, rs_send, rs_recv, rm_send, rm_recv,
    t2_send, t2_recv, ar_send, ar_recv,
):
    chunk = n * 2 * reqs
    half = chunk // 2
    rows = pages * SAMPLES
    prompts = plen_ref.shape[0]
    scale = HEAD ** (-0.5)
    x = lax.axis_index("kv")
    b = lax.axis_index("blk")
    k = lax.rem(b, 2)
    y = lax.rem(lax.div(b, 2), n)
    z = lax.div(b, 2 * n)
    p1 = y + k * (z - y)
    p2 = z + k * (y - z)
    other = 1 - k

    def at(zz, yy, kk):
        return (x, (zz * n + yy) * 2 + kk)

    def ring1(pos, h, kk):
        if h == 0:
            return at(z, pos, kk)
        return at(pos, y, kk)

    def mine1(pos, kk):
        return at(z + k * (pos - z), pos + k * (y - pos), kk)

    def mine2(d):
        pos = lax.rem(p2 + (d + n), n)
        return at(pos + k * (z - pos), y + k * (pos - y), k)

    def near(d):
        return lax.rem(p2 + (d + n), n)

    partner = at(z, y, other)

    def remote(src, dst, send, recv, to):
        return pltpu.make_async_remote_copy(
            src_ref=src, dst_ref=dst, send_sem=send, recv_sem=recv, device_id=to, device_id_type=MESH
        )

    pending = []

    def start(copy):
        copy.start()
        pending.append(copy)

    barrier = pltpu.get_barrier_semaphore()

    def greet(to):
        pl.semaphore_signal(barrier, inc=1, device_id=to, device_id_type=MESH)

    for d in [i for j in range(1, n // 2 + 1) for i in ((j, n - j) if 2 * j != n else (j,))]:
        for kk in range(2):
            greet(at(z, lax.rem(y + d, n), kk))
            greet(at(lax.rem(z + d, n), y, kk))
    greet(partner)
    if nx > 1:
        greet((x + 1 - 2 * lax.rem(x, 2), b))
    if nx > 2:
        greet((nx - 1 - x, b))

    loads = [
        pltpu.make_async_copy(src, dst, local_sem.at[i])
        for i, (src, dst) in enumerate([
            (q_hbm, q_in), (plen_hbm, plen_ref), (slot_hbm, slot_ref), (ids_hbm, ids_ref),
            (pool_hbm, poolv.at[pl.ds(0, pages)]), (tlen_hbm, tlen_ref), (nk_hbm, nk_ref),
            (tail_hbm, tailv), (w_hbm, wv),
        ])
    ]
    for load in loads:
        load.start()
    loads[0].wait()

    raw = q_in[...].astype(F32)
    gap = jnp.zeros((8 - reqs, HEAD), F32)
    for i in range(2):
        q_ref[i] = jnp.concatenate(
            [raw[:, i, 0:HEAD], gap, raw[:, i, HEAD:2 * HEAD], gap], axis=0
        ).astype(BF16)
    s1[p1 * 2 + k] = q_ref[k]

    pl.semaphore_wait(barrier, 1 + 4 * (n - 1) + min(nx - 1, 2))

    def first(h, d):
        mypos = (y, z)[h]
        pos = lax.rem(mypos + d, n)
        slot = mypos * 2 + k
        return remote(
            q_ref.at[h], s1.at[slot], s1_send.at[h * n + d], s1_recv.at[slot], ring1(pos, h, h)
        )

    order = [d for i in range(n // 2, 0, -1) for d in ((i, n - i) if 2 * i != n else (i,))]
    for d in order:
        for h in range(2):
            start(first(h, d))
    slot = p1_of(y, z, other) * 2 + k
    start(remote(q_ref.at[other], s1.at[slot], s1_send.at[other * n], s1_recv.at[slot], partner))

    swap = remote(pool_hbm, poolv.at[pl.ds(pages, pages)], cx_send.at[0], cx_recv.at[0], partner)
    start(swap)

    loads[1].wait()
    loads[2].wait()
    lane = iota((1, 128), 1)
    lens = jnp.zeros((1, 128), jnp.int32)
    for p in range(prompts):
        lens = jnp.where(lane == p, plen_ref[p], lens)
    need = lax.shift_right_logical(lens + (PAGE - 1), 6).astype(F32)
    grid_r, grid_c = iota((128, 128), 0), iota((128, 128), 1)
    need_t = jnp.transpose(jnp.broadcast_to(need, (128, 128)))
    ends = jnp.sum(jnp.where(grid_r <= grid_c, need_t, 0.0), axis=0, keepdims=True)
    starts = ends - need
    page_r = iota((pages, 128), 0)
    slots = jnp.zeros((pages, 128), jnp.int32)
    for j in range(pages):
        slots = jnp.where(page_r == j, slot_ref[j], slots)
    slots = slots.astype(F32)
    plane = iota((pages, 128), 1)
    owner = jnp.sum(
        jnp.where((plane < prompts) & (slots >= ends), 1.0, 0.0), axis=1, keepdims=True
    )
    used = owner < prompts
    owner = jnp.minimum(owner, prompts - 1.0)
    mine = plane.astype(F32) == owner
    begin = jnp.sum(jnp.where(mine, starts, 0.0), axis=1, keepdims=True)
    length = jnp.sum(jnp.where(mine, lens.astype(F32), 0.0), axis=1, keepdims=True)
    live = jnp.where(used, length - (slots - begin) * PAGE, 0.0)
    info_tx[0] = owner * SAMPLES + jnp.zeros_like(slots)
    info_tx[1] = live + jnp.zeros_like(slots)
    info = remote(info_tx, info_rx, cx_send.at[1], cx_recv.at[1], partner)
    start(info)

    pr, pc = iota((chunk, 2 * n * 16), 0), iota((chunk, 2 * n * 16), 1).astype(F32)
    cell = floor_div(pr, reqs)
    want = cell * 16.0 + (pr.astype(F32) - cell * reqs)
    for d in range(n):
        for kk in range(2):
            slot = lax.rem(p1 + d, n) * 2 + lax.rem(k + kk, 2)
            if d or kk:
                remote(q_ref.at[0], s1.at[slot], s1_send.at[0], s1_recv.at[slot], partner).wait_recv()
    s1v = s1[...].reshape(2 * n * 16, HEAD)
    packed = [
        dot(jnp.where(pc == want + c * 8.0, 1.0, 0.0).astype(BF16), s1v) for c in range(2)
    ]
    agm[p2] = jnp.concatenate(packed, axis=1).astype(BF16)

    def part(src, piece):
        return agm.at[src, pl.ds(piece * half, half)]

    def second(src, s, hop, kind, piece):
        return remote(
            part(src, piece), part(src, piece), ag_send.at[s, kind, piece], ag_recv.at[s, kind, piece],
            mine2((1, -1)[s] * hop),
        )

    def arrived(s, kind, piece):
        src = near(-(1, -1)[s] * (kind + 1))
        second(src, s, 1, kind, piece).wait_recv()
        return src

    for i in range(2):
        for s in range(2):
            start(second(p2, s, 2, 1, i ^ s))
    for i in range(2):
        for s in range(2):
            start(second(p2, s, 1, 0, i ^ s))

    total = n * chunk
    loads[3].wait()
    ids = ids_ref[...].reshape(1, total)
    grid_u = iota((n * n, total), 0).astype(F32)
    grid_e = iota((n * n, total), 1)
    on = floor_div(grid_e, 2 * reqs) == grid_u
    e_in = iota((total, 128), 0)
    e_mod = e_in.astype(F32) - floor_div(e_in, 2 * reqs) * (2 * reqs)
    l_in = iota((1, 128), 1)
    l_div = floor_div(l_in, 2 * reqs)
    l_mod = l_in.astype(F32) - l_div * (2 * reqs)
    spread_e = jnp.where(e_mod == l_mod, 1.0, 0.0).astype(BF16)
    hi = jnp.where(on, lax.shift_right_logical(ids, 5).astype(F32), 0.0).astype(BF16)
    lo = jnp.where(on, (ids & 31).astype(F32), 0.0).astype(BF16)
    table = dot(hi, spread_e) * 32.0 + dot(lo, spread_e)
    nat = jnp.concatenate(
        [
            jnp.sum(
                jnp.where(iota((n, 128), 0).astype(F32) == l_div, table[i * n:(i + 1) * n], 0.0),
                axis=0, keepdims=True,
            )
            for i in range(n)
        ],
        axis=0,
    )
    perm = jnp.zeros((n, 128), F32)
    for i in range(n):
        perm = jnp.where(l_div == float(i), table[i * n:(i + 1) * n], perm)
    ids_m = jnp.where(k == 0, nat, perm)
    info.wait_recv()
    pair = 2 * pages
    sample = (iota((2 * rows, 128), 0) & (SAMPLES - 1)).astype(F32)

    def per_row(i):
        v = jnp.concatenate([info_tx[i], info_rx[i]], axis=0)
        return jnp.broadcast_to(v[:, None, :], (pair, SAMPLES, 128)).reshape(2 * rows, 128)

    target = per_row(0) + sample
    live_c = per_row(1)
    for p in range(n):
        gm[p] = jnp.where(target[:, :chunk] == ids_m[p:p + 1, :chunk], 1.0, 0.0).astype(BF16)

    for i in range(2):
        for s in range(2):
            piece = i ^ s
            src = arrived(s, 1, piece)
            if i == 0:
                start(second(src, s, 2, 3, piece))
            start(second(src, s, 1, 2, piece))
    pick[...] = dot(gm[p2], agm[p2])

    def take(d):
        src = near(d)
        pick[...] += dot(gm[src], agm[src])

    for s in range(2):
        take((-2, 2)[s])
    target_row = jnp.concatenate(
        [jnp.transpose(target[i * 128:(i + 1) * 128])[0:8] for i in range(2 * rows // 128)], axis=1
    )
    live_row = jnp.concatenate(
        [jnp.transpose(live_c[i * 128:(i + 1) * 128])[0:1] for i in range(2 * rows // 128)], axis=1
    )
    both_t = jnp.concatenate([target_row[0:4, :rows], target_row[0:4, rows:]], axis=0)
    swap_t = jnp.concatenate([target_row[0:4, rows:], target_row[0:4, :rows]], axis=0)
    lane8 = iota((8, rows), 1)
    lower = iota((8, rows), 0) >= 4
    lead = jnp.where(lower & (swap_t == both_t), 0.0, 1.0)
    for d in range(1, pages):
        same = pltpu.roll(both_t, d * SAMPLES, 1) == both_t
        cross = pltpu.roll(swap_t, d * SAMPLES, 1) == both_t
        lead = jnp.where((same & (lane8 >= d * SAMPLES)) | (cross & lower), 0.0, lead)
    ids_t = jnp.transpose(jnp.concatenate([ids_m, jnp.zeros((128 - n, 128), F32)], axis=0))
    for p in range(n):
        gt[pl.ds(p * chunk, chunk), :] = jnp.where(
            ids_t[:chunk, p:p + 1] == target_row[0:1], 1.0, 0.0
        ).astype(BF16)
    for i in range(2):
        for s in range(2):
            arrived(s, 0, i ^ s)
    for s in range(2):
        take((-1, 1)[s])
    for i in range(2):
        for s in range(2):
            arrived(s, 2, i ^ s)
    for s in range(2):
        take((-3, 3)[s])
    for s in range(2):
        arrived(s, 3, s)
    take(4)

    loads[4].wait()
    swap.wait_recv()
    blocks = pair // 8
    scores, peaks = [], []
    page_l = lax.shift_right_logical(iota((PAGE, 256), 1) & 127, 4)
    for blk in range(blocks):
        keys = poolv[blk * 8:(blk + 1) * 8].reshape(8 * PAGE, 2 * HEAD)[:, :HEAD]
        sl = slice(blk * 128, (blk + 1) * 128)
        qb = jnp.concatenate([pick[sl, :HEAD], pick[sl, HEAD:]], axis=0).astype(BF16)
        full = dot(keys, qb, 1, 1)
        s = jnp.zeros((PAGE, 256), F32)
        for j in range(8):
            s = jnp.where(page_l == j, full[j * PAGE:(j + 1) * PAGE], s)
        lv = jnp.concatenate([live_row[:, sl]] * 2, axis=1)
        alive = iota((PAGE, 256), 0).astype(F32) < lv
        s = jnp.where(alive, s * scale, NEG)
        scores.append((s, alive))
        m = jnp.max(s, axis=0, keepdims=True)
        peaks.append(jnp.concatenate([m[:, :128], m[:, 128:]], axis=0))
    hb = blocks // 2
    low, high = jnp.concatenate(peaks[:hb], axis=1), jnp.concatenate(peaks[hb:], axis=1)

    both_m = jnp.concatenate([low, low, high, high], axis=0)
    swap_m = jnp.concatenate([high, high, low, low], axis=0)
    top = jnp.where(swap_t == both_t, jnp.maximum(both_m, swap_m), both_m)
    for d in range(1, pages):
        same = pltpu.roll(both_t, d * SAMPLES, 1) == both_t
        cross = pltpu.roll(swap_t, d * SAMPLES, 1) == both_t
        top = jnp.where(same, jnp.maximum(top, pltpu.roll(both_m, d * SAMPLES, 1)), top)
        top = jnp.where(cross, jnp.maximum(top, pltpu.roll(swap_m, d * SAMPLES, 1)), top)

    dens = []
    page_r8 = lax.shift_right_logical(iota((256, 8 * PAGE), 0) & 127, 4)
    own_page = page_r8 == lax.shift_right_logical(iota((256, 8 * PAGE), 1), 6)
    for blk in range(blocks):
        s, alive = scores[blk]
        base = 4 * (blk // hb)
        tb = top[base:base + 2, (blk % hb) * 128:(blk % hb + 1) * 128]
        tb = jnp.concatenate([tb[0:1], tb[1:2]], axis=1)
        w = jnp.where(alive, jnp.exp(s - tb), 0.0)
        dsum = jnp.sum(w, axis=0, keepdims=True)
        dens.append(jnp.concatenate([dsum[:, :128], dsum[:, 128:]], axis=0))
        wt = jnp.transpose(w)
        wt = jnp.concatenate([wt, wt], axis=1)
        wide = jnp.where(own_page, jnp.concatenate([wt] * 4, axis=1), 0.0).astype(BF16)
        values = poolv[blk * 8:(blk + 1) * 8].reshape(8 * PAGE, 2 * HEAD)[:, HEAD:]
        acc = dot(wide, values).astype(BF16)
        accm[blk * 128:(blk + 1) * 128, :HEAD] = acc[:128]
        accm[blk * 128:(blk + 1) * 128, HEAD:] = acc[128:]
    st = jnp.concatenate(
        [
            jnp.concatenate([jnp.where(lead[0:2] > 0.5, top[0:2], 0.0),
                             jnp.where(lead[4:6] > 0.5, top[4:6], 0.0)], axis=1),
            jnp.concatenate(dens, axis=1),
            jnp.concatenate([lead[0:1], lead[4:5]], axis=1),
            jnp.zeros((3, 2 * rows), F32),
        ],
        axis=0,
    )
    stats[...] = jnp.concatenate(split3(st), axis=0).astype(BF16)

    sub8 = iota((8, 128), 0)

    def sums(d):
        g = gt[pl.ds(pl.multiple_of(near(d) * chunk, chunk), chunk), :]
        acc = dot(g, accm[...])
        ml = dot(stats[...], g, 1, 1)
        ml = ml[0:8] + ml[8:16] + ml[16:24]
        ml = jnp.concatenate([ml, jnp.zeros((8, 128 - chunk), F32)], axis=1)
        return acc, jnp.where((sub8 < 2) & (ml[4:5] < 0.5), NEG, ml)

    def ring(s, kind, src, dst, hop):
        to = mine2((1, -1)[s] * hop)
        return (
            remote(src[0], dst, rs_send.at[s, kind], rs_recv.at[s, kind], to),
            remote(src[1], rx_ml.at[s, kind], rm_send.at[s, kind], rm_recv.at[s, kind], to),
        )

    def landed(s, kind, dst):
        for copy in ring(s, kind, (dst, rx_ml.at[s, kind]), dst, 1):
            copy.wait_recv()

    def store(i, d):
        acc, ml = sums(d)
        tx_acc[i] = acc.astype(BF16)
        tx_ml[i] = ml

    store(2, 4)
    for s in range(2):
        for copy in ring(s, 1, (tx_acc.at[2, pl.ds(s * half, half)], tx_ml.at[2]), a4_acc.at[s], 2):
            start(copy)
    for s in range(2):
        store(s, (3, -3)[s])
        for copy in ring(s, 0, (tx_acc.at[s], tx_ml.at[s]), a3_acc.at[s], 1):
            start(copy)
    for s in range(2):
        store(3 + s, (1, -1)[s])
        for copy in ring(s, 2, (tx_acc.at[3 + s], tx_ml.at[3 + s]), b_acc.at[s, 0], 1):
            start(copy)

    def weigh(mls):
        out = []
        for c in range(2):
            mx = functools.reduce(jnp.maximum, [m[c:c + 1] for m in mls])
            w = [jnp.exp(m[c:c + 1] - mx) for m in mls]
            dn = functools.reduce(jnp.add, [a * m[2 + c:3 + c] for a, m in zip(w, mls)])
            out.append((w, mx, dn))
        return out

    def columns(items):
        return jnp.transpose(
            jnp.concatenate(items + [jnp.zeros((128 - len(items), 128), F32)], axis=0)
        )

    lane128 = iota((8, 128), 1)
    for s in range(2):
        acc, ml = sums((2, -2)[s])
        landed(s, 0, a3_acc.at[s])
        landed(s, 1, a4_acc.at[s])
        inside = (lane128 < half) if s == 0 else (lane128 >= half)
        ml4 = jnp.where((sub8 < 2) & jnp.logical_not(inside), NEG, rx_ml[s, 1])
        mls = [ml, rx_ml[s, 0], ml4]
        st = weigh(mls)
        cols = columns(st[0][0] + st[1][0])
        outs = []
        for c in range(2):
            sl = slice(c * HEAD, (c + 1) * HEAD)
            a3 = a3_acc[s, :, sl].astype(F32)
            a4 = a4_acc[s, :, sl].astype(F32)
            v = acc[:, sl] * cols[:chunk, 3 * c:3 * c + 1] + a3 * cols[:chunk, 3 * c + 1:3 * c + 2]
            add = a4 * cols[s * half:(s + 1) * half, 3 * c + 2:3 * c + 3]
            if s == 0:
                v = jnp.concatenate([v[:half] + add, v[half:]], axis=0)
            else:
                v = jnp.concatenate([v[:half], v[half:] + add], axis=0)
            outs.append(v)
        tx_acc[5 + s] = jnp.concatenate(outs, axis=1).astype(BF16)
        tx_ml[5 + s] = jnp.concatenate(
            [st[0][1], st[1][1], st[0][2], st[1][2], jnp.zeros((4, 128), F32)], axis=0
        )
        for copy in ring(s, 3, (tx_acc.at[5 + s], tx_ml.at[5 + s]), b_acc.at[s, 1], 2):
            start(copy)
    home_acc, home_ml = sums(0)

    loads[5].wait()
    loads[6].wait()
    loads[7].wait()
    qown = jnp.concatenate([q_ref[0], q_ref[1]], axis=0)
    tails = tailv[...].reshape(reqs * 128, 2 * HEAD)
    row32 = iota((32, 128), 0) & 7
    ts, tl = [], []
    for r in range(reqs):
        ok = (row32 == r) & (iota((32, 128), 1) < tlen_ref[r])
        tl.append(ok)
        ts.append(jnp.where(ok, dot(qown, tails[r * 128:(r + 1) * 128, :HEAD], 1, 1) * scale, NEG))
    fresh = nk_ref[...].astype(F32)
    pad = jnp.zeros((8 - reqs, 2 * HEAD), F32)
    news = jnp.concatenate([fresh[:, 0, :], pad, fresh[:, 1, :], pad], axis=0).astype(BF16)
    nrow, ncol = iota((32, 16), 0), iota((32, 16), 1)
    nlive = ((nrow & 7) == (ncol & 7)) & (lax.shift_right_logical(ncol, 3) <= lax.shift_right_logical(nrow, 4))
    ns = jnp.where(nlive, dot(qown, news[:, :HEAD], 1, 1) * scale, NEG)
    peak = jnp.max(ns, axis=1, keepdims=True)
    peak = jnp.maximum(peak, jnp.max(functools.reduce(jnp.maximum, ts), axis=1, keepdims=True))
    nw = jnp.where(nlive, jnp.exp(ns - peak), 0.0)
    tw = [jnp.where(ok, jnp.exp(t - peak), 0.0) for t, ok in zip(ts, tl)]
    own_den = jnp.sum(nw, axis=1, keepdims=True)
    own_den += jnp.sum(functools.reduce(jnp.add, tw), axis=1, keepdims=True)
    own_acc[...] = dot(nw.astype(BF16), news[:, HEAD:]) + dot(
        jnp.concatenate(tw, axis=1).astype(BF16), tails[:, HEAD:]
    )
    own_st[...] = jnp.where(iota((32, 128), 1) == 0, peak, own_den)

    for s in range(2):
        landed(s, 2, b_acc.at[s, 0])
    for s in range(2):
        landed(s, 3, b_acc.at[s, 1])
    st = weigh([home_ml] + [rx_ml[s, kind] for s in range(2) for kind in (2, 3)])
    cols = columns(st[0][0] + st[1][0] + [st[0][1], st[1][1], st[0][2], st[1][2]])[:chunk]
    lane_c = iota((chunk, 128), 1)
    t2v = jnp.zeros((2 * n * 16, HEAD + 128), F32)
    sr, sc = iota((2 * n * 16, chunk), 0), iota((2 * n * 16, chunk), 1)
    for c in range(2):
        sl = slice(c * HEAD, (c + 1) * HEAD)
        acc = home_acc[:, sl] * cols[:, 5 * c:5 * c + 1]
        for i in range(4):
            acc += b_acc[i // 2, i % 2, :, sl].astype(F32) * cols[:, 5 * c + 1 + i:5 * c + 2 + i]
        parts = split3(cols[:, 10 + c:11 + c]) + split3(cols[:, 12 + c:13 + c])
        tile = jnp.zeros((chunk, 128), F32)
        for i, col in enumerate(parts):
            tile = jnp.where(lane_c == i, col, tile)
        rowsrc = jnp.concatenate([acc, tile], axis=1).astype(BF16)
        inner = (sr & 15) - c * 8
        pick_rows = (inner >= 0) & (inner < reqs) & (lax.shift_right_logical(sr, 4) * reqs + inner == sc)
        t2v += dot(jnp.where(pick_rows, 1.0, 0.0).astype(BF16), rowsrc)
    t2[...] = t2v.astype(BF16).reshape(2 * n, 16, HEAD + 128)

    def home(pos, kk):
        return remote(
            t2.at[pos * 2 + kk], r2.at[k, p1], t2_send.at[pos * 2 + kk], t2_recv.at[k, p1],
            mine1(pos, kk),
        )

    for d in order:
        pos = lax.rem(p1 + d, n)
        for kk in range(2):
            start(home(pos, kk))
    start(home(p1, other))
    r2[k, p1] = t2[p1 * 2 + k]
    loads[8].wait()
    for d in range(1, n):
        for h in range(2):
            src = lax.rem((y, z)[h] + d, n)
            remote(t2.at[0], r2.at[h, src], t2_send.at[0], t2_recv.at[h, src], partner).wait_recv()
    src = p1_of(y, z, other)
    remote(t2.at[0], r2.at[other, src], t2_send.at[0], t2_recv.at[other, src], partner).wait_recv()

    heads = []
    for h in range(2):
        cells = [r2[h, i].astype(F32) for i in range(n)]
        ms = [t[:, HEAD:HEAD + 1] + t[:, HEAD + 1:HEAD + 2] + t[:, HEAD + 2:HEAD + 3] for t in cells]
        ds = [t[:, HEAD + 3:HEAD + 4] + t[:, HEAD + 4:HEAD + 5] + t[:, HEAD + 5:HEAD + 6] for t in cells]
        ms.append(own_st[h * 16:(h + 1) * 16, 0:1])
        ds.append(own_st[h * 16:(h + 1) * 16, 1:2])
        accs = [t[:, :HEAD] for t in cells] + [own_acc[h * 16:(h + 1) * 16]]
        mx = functools.reduce(jnp.maximum, ms)
        num = jnp.zeros((16, HEAD), F32)
        dn = jnp.zeros((16, 1), F32)
        for m, dd, acc in zip(ms, ds, accs):
            w = jnp.exp(m - mx)
            num += acc * w
            dn += dd * w
        heads.append(num / dn)
    att = jnp.concatenate(
        [jnp.concatenate([a[0:8], a[8:16]], axis=1) for a in heads], axis=0
    ).astype(BF16)

    hw = wv.shape[1] // 2
    even = x + 1 - 2 * lax.rem(x, 2)
    odd = nx - 1 - x
    if nx == 1:
        for i in range(2):
            out_ref[0, i] = dot(att, wv[:, i * hw:(i + 1) * hw]).astype(BF16)
            out_ref[1, i] = jnp.zeros((16, hw), BF16)
    else:
        def trade(i, turn):
            src = ar.at[i] if turn == 0 else out_ref.at[0, i]
            dst = ar_rx.at[i] if turn == 0 else out_ref.at[1, i]
            to = even if (i + turn) % 2 == 0 else odd
            return remote(src, dst, ar_send.at[turn, i], ar_recv.at[turn, i], (to, b))

        for i in range(2):
            ar[i] = dot(att, wv[:, i * hw:(i + 1) * hw]).astype(BF16)
            start(trade(i, 0))
        for i in range(2):
            trade(i, 0).wait_recv()
            out_ref[0, i] = (ar[i].astype(F32) + ar_rx[i].astype(F32)).astype(BF16)
            if nx > 2:
                start(trade(i, 1))
            else:
                out_ref[1, i] = jnp.zeros((16, hw), BF16)
        for i in range(2):
            if nx > 2:
                trade(i, 1).wait_recv()
    for copy in pending:
        copy.wait_send()


def finish(sum_ref, hid_ref, gain_ref, score_ref, out_ref, sc_ref):
    reqs = hid_ref.shape[0]
    raw = hid_ref[...].astype(F32)
    total = jnp.concatenate(
        [sum_ref[0, i].astype(F32) + sum_ref[1, i].astype(F32) for i in range(2)], axis=1
    )
    hid = [(raw[:, i, :] + total[8 * i:8 * i + reqs]).astype(BF16).astype(F32) for i in range(2)]
    out_ref[...] = jnp.stack(hid, axis=1).astype(BF16)
    last = hid[1]
    normed = last * lax.rsqrt(jnp.mean(last * last, axis=1, keepdims=True) + 1e-06) * gain_ref[...]
    score = jnp.sum(normed * score_ref[...], axis=1, keepdims=True)
    tile = jnp.concatenate([jnp.broadcast_to(score, (reqs, 128)), jnp.zeros((128 - reqs, 128), F32)], axis=0)
    sc_ref[...] = jnp.transpose(tile)[0, :reqs]


def p1_of(y, z, h):
    return y + h * (z - y)


def body(n, nx, prefix_pool, slot_page, prompt_len, request_ids, tail_len, tail_cache, queries,
         new_kv, hidden, out_weight, norm_gain, score_weight):
    pages = prefix_pool.shape[1]
    reqs, width = hidden.shape[0], hidden.shape[2]
    chunk = n * 2 * reqs
    rows = pages * SAMPLES
    total = n * chunk
    vm = pl.BlockSpec(memory_space=pltpu.VMEM)
    hbm = pl.BlockSpec(memory_space=pl.ANY)
    dma = pltpu.SemaphoreType.DMA
    sums = pl.pallas_call(
        functools.partial(kernel, n, nx, reqs, pages),
        out_shape=pltpu.VMEM((2, 2, 16, width // 2), BF16),
        in_specs=[hbm] * 9,
        out_specs=vm,
        scratch_shapes=[
            pltpu.SMEM(slot_page.shape, jnp.int32),
            pltpu.SMEM(prompt_len.shape, jnp.int32),
            pltpu.SMEM(tail_len.shape, jnp.int32),
            pltpu.VMEM(request_ids.shape, jnp.int32),
            pltpu.VMEM(queries.shape, BF16),
            pltpu.VMEM(new_kv.shape[1:], BF16),
            pltpu.VMEM((2, 16, HEAD), BF16),
            pltpu.VMEM((2 * pages, PAGE, 2 * HEAD), BF16),
            pltpu.VMEM((reqs, 128, 2 * HEAD), BF16),
            pltpu.VMEM((2 * HEAD, width), BF16),
            pltpu.VMEM((2 * n, 16, HEAD), BF16),
            pltpu.VMEM((n, chunk, 512), BF16),
            pltpu.VMEM((n, 2 * rows, chunk), BF16),
            pltpu.VMEM((total, 2 * rows), BF16),
            pltpu.VMEM((2 * rows, 512), F32),
            pltpu.VMEM((2 * rows, 512), BF16),
            pltpu.VMEM((24, 2 * rows), BF16),
            pltpu.VMEM((2, pages, 128), F32),
            pltpu.VMEM((2, pages, 128), F32),
            pltpu.VMEM((7, chunk, 512), BF16),
            pltpu.VMEM((7, 8, 128), F32),
            pltpu.VMEM((2, chunk, 512), BF16),
            pltpu.VMEM((2, chunk // 2, 512), BF16),
            pltpu.VMEM((2, 2, chunk, 512), BF16),
            pltpu.VMEM((2, 4, 8, 128), F32),
            pltpu.VMEM((2 * n, 16, HEAD + 128), BF16),
            pltpu.VMEM((2, n, 16, HEAD + 128), BF16),
            pltpu.VMEM((32, HEAD), F32),
            pltpu.VMEM((32, 128), F32),
            pltpu.VMEM((2, 16, width // 2), BF16),
            pltpu.VMEM((2, 16, width // 2), BF16),
            dma((9,)), dma((2 * n,)), dma((2 * n,)),
            dma((2, 4, 2)), dma((2, 4, 2)),
            dma((2,)), dma((2,)),
            dma((2, 4)), dma((2, 4)), dma((2, 4)), dma((2, 4)),
            dma((2 * n,)), dma((2, n)), dma((2, 2)), dma((2, 2)),
        ],
        compiler_params=pltpu.CompilerParams(collective_id=0, has_side_effects=True),
    )(
        slot_page, prompt_len, tail_len, request_ids, queries, new_kv[0],
        prefix_pool[0], tail_cache[0], out_weight,
    )
    return pl.pallas_call(
        finish,
        out_shape=(jax.ShapeDtypeStruct(hidden.shape, BF16), jax.ShapeDtypeStruct((reqs,), F32)),
        in_specs=[vm] * 4,
        out_specs=(vm, vm),
    )(pltpu.with_memory_space_constraint(sums, pltpu.VMEM), hidden, norm_gain.reshape(1, -1), score_weight.reshape(1, -1))


def solution(mesh):
    nx = mesh.shape["kv"]
    n = int(round((mesh.shape["blk"] // 2) ** 0.5))
    in_specs = (
        P("kv", "blk", None, None),
        P("blk"),
        P(),
        P(),
        P("blk"),
        P("kv", "blk", None, None),
        P("blk", None, "kv"),
        P("kv", "blk", None, None),
        P("blk", None, None),
        P("kv", None),
        P(),
        P(),
    )
    out_specs = (P("blk", None, None), P("blk"))
    return jax.shard_map(
        functools.partial(body, n, nx), mesh=mesh, in_specs=in_specs, out_specs=out_specs, check_vma=False
    )
```

```python
import functools

import jax
import jax.numpy as jnp
from jax import lax
from jax.experimental import pallas as pl
from jax.experimental.pallas import tpu as pltpu
from jax.sharding import PartitionSpec as P

MESH = pl.DeviceIdType.MESH
SAMPLES = 16
HEAD = 256
PAGE = 64
NEG = -1e30
F32 = jnp.float32
BF16 = jnp.bfloat16


def iota(shape, dim):
    return lax.broadcasted_iota(jnp.int32, shape, dim)


def dot(a, b, ca=1, cb=0):
    return lax.dot_general(a, b, (((ca,), (cb,)), ((), ())), preferred_element_type=F32)


def floor_div(a, c):
    return jnp.floor((a.astype(F32) + 0.5) * (1.0 / c))


def split3(x):
    a = x.astype(BF16).astype(F32)
    b = (x - a).astype(BF16).astype(F32)
    return a, b, x - a - b


def kernel(
    n, nx, reqs, pages,
    slot_hbm, plen_hbm, tlen_hbm, ids_hbm, q_hbm, nk_hbm, pool_hbm, tail_hbm, w_hbm,
    hid_hbm, gain_hbm, score_hbm,
    out_ref, hid_out, gain_out, score_out,
    slot_ref, plen_ref, tlen_ref, ids_ref, q_in, nk_ref,
    q_ref, poolv, tailv, wv, s1, agm, gm, gt, pick, accm, stats, info_tx, info_rx,
    tx_acc, tx_ml, a3_acc, a4_acc, b_acc, rx_ml, t2, r2, own_acc, own_st, ar, ar_rx,
    local_sem, s1_send, s1_recv, ag_send, ag_recv,
    cx_send, cx_recv, rs_send, rs_recv, rm_send, rm_recv,
    t2_send, t2_recv, ar_send, ar_recv,
):
    chunk = n * 2 * reqs
    half = chunk // 2
    rows = pages * SAMPLES
    prompts = plen_ref.shape[0]
    scale = HEAD ** (-0.5)
    x = lax.axis_index("kv")
    b = lax.axis_index("blk")
    k = lax.rem(b, 2)
    y = lax.rem(lax.div(b, 2), n)
    z = lax.div(b, 2 * n)
    p1 = y + k * (z - y)
    p2 = z + k * (y - z)
    other = 1 - k

    def at(zz, yy, kk):
        return (x, (zz * n + yy) * 2 + kk)

    def ring1(pos, h, kk):
        if h == 0:
            return at(z, pos, kk)
        return at(pos, y, kk)

    def mine1(pos, kk):
        return at(z + k * (pos - z), pos + k * (y - pos), kk)

    def mine2(d):
        pos = lax.rem(p2 + (d + n), n)
        return at(pos + k * (z - pos), y + k * (pos - y), k)

    def near(d):
        return lax.rem(p2 + (d + n), n)

    partner = at(z, y, other)

    def remote(src, dst, send, recv, to):
        return pltpu.make_async_remote_copy(
            src_ref=src, dst_ref=dst, send_sem=send, recv_sem=recv, device_id=to, device_id_type=MESH
        )

    pending = []

    def start(copy):
        copy.start()
        pending.append(copy)

    barrier = pltpu.get_barrier_semaphore()

    def greet(to):
        pl.semaphore_signal(barrier, inc=1, device_id=to, device_id_type=MESH)

    for d in [i for j in range(1, n // 2 + 1) for i in ((j, n - j) if 2 * j != n else (j,))]:
        for kk in range(2):
            greet(at(z, lax.rem(y + d, n), kk))
            greet(at(lax.rem(z + d, n), y, kk))
    greet(partner)
    if nx > 1:
        greet((x + 1 - 2 * lax.rem(x, 2), b))
    if nx > 2:
        greet((nx - 1 - x, b))

    loads = [
        pltpu.make_async_copy(src, dst, local_sem.at[i])
        for i, (src, dst) in enumerate([
            (q_hbm, q_in), (plen_hbm, plen_ref), (slot_hbm, slot_ref), (ids_hbm, ids_ref),
            (pool_hbm, poolv.at[pl.ds(0, pages)]), (tlen_hbm, tlen_ref), (nk_hbm, nk_ref),
            (tail_hbm, tailv), (w_hbm, wv),
            (hid_hbm, hid_out), (gain_hbm, gain_out), (score_hbm, score_out),
        ])
    ]
    for load in loads:
        load.start()
    loads[0].wait()

    raw = q_in[...].astype(F32)
    gap = jnp.zeros((8 - reqs, HEAD), F32)
    for i in range(2):
        q_ref[i] = jnp.concatenate(
            [raw[:, i, 0:HEAD], gap, raw[:, i, HEAD:2 * HEAD], gap], axis=0
        ).astype(BF16)
    s1[p1 * 2 + k] = q_ref[k]

    pl.semaphore_wait(barrier, 1 + 4 * (n - 1) + min(nx - 1, 2))

    def first(h, d):
        mypos = (y, z)[h]
        pos = lax.rem(mypos + d, n)
        slot = mypos * 2 + k
        return remote(
            q_ref.at[h], s1.at[slot], s1_send.at[h * n + d], s1_recv.at[slot], ring1(pos, h, h)
        )

    order = [d for i in range(n // 2, 0, -1) for d in ((i, n - i) if 2 * i != n else (i,))]
    for d in order:
        for h in range(2):
            start(first(h, d))
    slot = p1_of(y, z, other) * 2 + k
    start(remote(q_ref.at[other], s1.at[slot], s1_send.at[other * n], s1_recv.at[slot], partner))

    swap = remote(pool_hbm, poolv.at[pl.ds(pages, pages)], cx_send.at[0], cx_recv.at[0], partner)
    start(swap)

    loads[1].wait()
    loads[2].wait()
    lane = iota((1, 128), 1)
    lens = jnp.zeros((1, 128), jnp.int32)
    for p in range(prompts):
        lens = jnp.where(lane == p, plen_ref[p], lens)
    need = lax.shift_right_logical(lens + (PAGE - 1), 6).astype(F32)
    grid_r, grid_c = iota((128, 128), 0), iota((128, 128), 1)
    need_t = jnp.transpose(jnp.broadcast_to(need, (128, 128)))
    ends = jnp.sum(jnp.where(grid_r <= grid_c, need_t, 0.0), axis=0, keepdims=True)
    starts = ends - need
    page_r = iota((pages, 128), 0)
    slots = jnp.zeros((pages, 128), jnp.int32)
    for j in range(pages):
        slots = jnp.where(page_r == j, slot_ref[j], slots)
    slots = slots.astype(F32)
    plane = iota((pages, 128), 1)
    owner = jnp.sum(
        jnp.where((plane < prompts) & (slots >= ends), 1.0, 0.0), axis=1, keepdims=True
    )
    used = owner < prompts
    owner = jnp.minimum(owner, prompts - 1.0)
    mine = plane.astype(F32) == owner
    begin = jnp.sum(jnp.where(mine, starts, 0.0), axis=1, keepdims=True)
    length = jnp.sum(jnp.where(mine, lens.astype(F32), 0.0), axis=1, keepdims=True)
    live = jnp.where(used, length - (slots - begin) * PAGE, 0.0)
    info_tx[0] = owner * SAMPLES + jnp.zeros_like(slots)
    info_tx[1] = live + jnp.zeros_like(slots)
    info = remote(info_tx, info_rx, cx_send.at[1], cx_recv.at[1], partner)
    start(info)

    pr, pc = iota((chunk, 2 * n * 16), 0), iota((chunk, 2 * n * 16), 1).astype(F32)
    cell = floor_div(pr, reqs)
    want = cell * 16.0 + (pr.astype(F32) - cell * reqs)
    for d in range(n):
        for kk in range(2):
            slot = lax.rem(p1 + d, n) * 2 + lax.rem(k + kk, 2)
            if d or kk:
                remote(q_ref.at[0], s1.at[slot], s1_send.at[0], s1_recv.at[slot], partner).wait_recv()
    s1v = s1[...].reshape(2 * n * 16, HEAD)
    packed = [
        dot(jnp.where(pc == want + c * 8.0, 1.0, 0.0).astype(BF16), s1v) for c in range(2)
    ]
    agm[p2] = jnp.concatenate(packed, axis=1).astype(BF16)

    def part(src, piece):
        return agm.at[src, pl.ds(piece * half, half)]

    def second(src, s, hop, kind, piece):
        return remote(
            part(src, piece), part(src, piece), ag_send.at[s, kind, piece], ag_recv.at[s, kind, piece],
            mine2((1, -1)[s] * hop),
        )

    def arrived(s, kind, piece):
        src = near(-(1, -1)[s] * (kind + 1))
        second(src, s, 1, kind, piece).wait_recv()
        return src

    for i in range(2):
        for s in range(2):
            start(second(p2, s, 2, 1, i ^ s))
    for i in range(2):
        for s in range(2):
            start(second(p2, s, 1, 0, i ^ s))

    total = n * chunk
    loads[3].wait()
    ids = ids_ref[...].reshape(1, total)
    grid_u = iota((n * n, total), 0).astype(F32)
    grid_e = iota((n * n, total), 1)
    on = floor_div(grid_e, 2 * reqs) == grid_u
    e_in = iota((total, 128), 0)
    e_mod = e_in.astype(F32) - floor_div(e_in, 2 * reqs) * (2 * reqs)
    l_in = iota((1, 128), 1)
    l_div = floor_div(l_in, 2 * reqs)
    l_mod = l_in.astype(F32) - l_div * (2 * reqs)
    spread_e = jnp.where(e_mod == l_mod, 1.0, 0.0).astype(BF16)
    hi = jnp.where(on, lax.shift_right_logical(ids, 5).astype(F32), 0.0).astype(BF16)
    lo = jnp.where(on, (ids & 31).astype(F32), 0.0).astype(BF16)
    table = dot(hi, spread_e) * 32.0 + dot(lo, spread_e)
    nat = jnp.concatenate(
        [
            jnp.sum(
                jnp.where(iota((n, 128), 0).astype(F32) == l_div, table[i * n:(i + 1) * n], 0.0),
                axis=0, keepdims=True,
            )
            for i in range(n)
        ],
        axis=0,
    )
    perm = jnp.zeros((n, 128), F32)
    for i in range(n):
        perm = jnp.where(l_div == float(i), table[i * n:(i + 1) * n], perm)
    ids_m = jnp.where(k == 0, nat, perm)
    info.wait_recv()
    pair = 2 * pages
    sample = (iota((2 * rows, 128), 0) & (SAMPLES - 1)).astype(F32)

    def per_row(i):
        v = jnp.concatenate([info_tx[i], info_rx[i]], axis=0)
        return jnp.broadcast_to(v[:, None, :], (pair, SAMPLES, 128)).reshape(2 * rows, 128)

    target = per_row(0) + sample
    live_c = per_row(1)
    for p in range(n):
        gm[p] = jnp.where(target[:, :chunk] == ids_m[p:p + 1, :chunk], 1.0, 0.0).astype(BF16)

    for i in range(2):
        for s in range(2):
            piece = i ^ s
            src = arrived(s, 1, piece)
            if i == 0:
                start(second(src, s, 2, 3, piece))
            start(second(src, s, 1, 2, piece))
    pick[...] = dot(gm[p2], agm[p2])

    def take(d):
        src = near(d)
        pick[...] += dot(gm[src], agm[src])

    for s in range(2):
        take((-2, 2)[s])
    target_row = jnp.concatenate(
        [jnp.transpose(target[i * 128:(i + 1) * 128])[0:8] for i in range(2 * rows // 128)], axis=1
    )
    live_row = jnp.concatenate(
        [jnp.transpose(live_c[i * 128:(i + 1) * 128])[0:1] for i in range(2 * rows // 128)], axis=1
    )
    both_t = jnp.concatenate([target_row[0:4, :rows], target_row[0:4, rows:]], axis=0)
    swap_t = jnp.concatenate([target_row[0:4, rows:], target_row[0:4, :rows]], axis=0)
    lane8 = iota((8, rows), 1)
    lower = iota((8, rows), 0) >= 4
    lead = jnp.where(lower & (swap_t == both_t), 0.0, 1.0)
    for d in range(1, pages):
        same = pltpu.roll(both_t, d * SAMPLES, 1) == both_t
        cross = pltpu.roll(swap_t, d * SAMPLES, 1) == both_t
        lead = jnp.where((same & (lane8 >= d * SAMPLES)) | (cross & lower), 0.0, lead)
    ids_t = jnp.transpose(jnp.concatenate([ids_m, jnp.zeros((128 - n, 128), F32)], axis=0))
    for p in range(n):
        gt[pl.ds(p * chunk, chunk), :] = jnp.where(
            ids_t[:chunk, p:p + 1] == target_row[0:1], 1.0, 0.0
        ).astype(BF16)
    for i in range(2):
        for s in range(2):
            arrived(s, 0, i ^ s)
    for s in range(2):
        take((-1, 1)[s])
    for i in range(2):
        for s in range(2):
            arrived(s, 2, i ^ s)
    for s in range(2):
        take((-3, 3)[s])
    for s in range(2):
        arrived(s, 3, s)
    take(4)

    loads[4].wait()
    swap.wait_recv()
    blocks = pair // 8
    scores, peaks = [], []
    page_l = lax.shift_right_logical(iota((PAGE, 256), 1) & 127, 4)
    for blk in range(blocks):
        keys = poolv[blk * 8:(blk + 1) * 8].reshape(8 * PAGE, 2 * HEAD)[:, :HEAD]
        sl = slice(blk * 128, (blk + 1) * 128)
        qb = jnp.concatenate([pick[sl, :HEAD], pick[sl, HEAD:]], axis=0).astype(BF16)
        full = dot(keys, qb, 1, 1)
        s = jnp.zeros((PAGE, 256), F32)
        for j in range(8):
            s = jnp.where(page_l == j, full[j * PAGE:(j + 1) * PAGE], s)
        lv = jnp.concatenate([live_row[:, sl]] * 2, axis=1)
        alive = iota((PAGE, 256), 0).astype(F32) < lv
        s = jnp.where(alive, s * scale, NEG)
        scores.append((s, alive))
        m = jnp.max(s, axis=0, keepdims=True)
        peaks.append(jnp.concatenate([m[:, :128], m[:, 128:]], axis=0))
    hb = blocks // 2
    low, high = jnp.concatenate(peaks[:hb], axis=1), jnp.concatenate(peaks[hb:], axis=1)

    both_m = jnp.concatenate([low, low, high, high], axis=0)
    swap_m = jnp.concatenate([high, high, low, low], axis=0)
    top = jnp.where(swap_t == both_t, jnp.maximum(both_m, swap_m), both_m)
    for d in range(1, pages):
        same = pltpu.roll(both_t, d * SAMPLES, 1) == both_t
        cross = pltpu.roll(swap_t, d * SAMPLES, 1) == both_t
        top = jnp.where(same, jnp.maximum(top, pltpu.roll(both_m, d * SAMPLES, 1)), top)
        top = jnp.where(cross, jnp.maximum(top, pltpu.roll(swap_m, d * SAMPLES, 1)), top)

    dens = []
    page_r8 = lax.shift_right_logical(iota((256, 8 * PAGE), 0) & 127, 4)
    own_page = page_r8 == lax.shift_right_logical(iota((256, 8 * PAGE), 1), 6)
    for blk in range(blocks):
        s, alive = scores[blk]
        base = 4 * (blk // hb)
        tb = top[base:base + 2, (blk % hb) * 128:(blk % hb + 1) * 128]
        tb = jnp.concatenate([tb[0:1], tb[1:2]], axis=1)
        w = jnp.where(alive, jnp.exp(s - tb), 0.0)
        dsum = jnp.sum(w, axis=0, keepdims=True)
        dens.append(jnp.concatenate([dsum[:, :128], dsum[:, 128:]], axis=0))
        wt = jnp.transpose(w)
        wt = jnp.concatenate([wt, wt], axis=1)
        wide = jnp.where(own_page, jnp.concatenate([wt] * 4, axis=1), 0.0).astype(BF16)
        values = poolv[blk * 8:(blk + 1) * 8].reshape(8 * PAGE, 2 * HEAD)[:, HEAD:]
        acc = dot(wide, values).astype(BF16)
        accm[blk * 128:(blk + 1) * 128, :HEAD] = acc[:128]
        accm[blk * 128:(blk + 1) * 128, HEAD:] = acc[128:]
    st = jnp.concatenate(
        [
            jnp.concatenate([jnp.where(lead[0:2] > 0.5, top[0:2], 0.0),
                             jnp.where(lead[4:6] > 0.5, top[4:6], 0.0)], axis=1),
            jnp.concatenate(dens, axis=1),
            jnp.concatenate([lead[0:1], lead[4:5]], axis=1),
            jnp.zeros((3, 2 * rows), F32),
        ],
        axis=0,
    )
    stats[...] = jnp.concatenate(split3(st), axis=0).astype(BF16)

    sub8 = iota((8, 128), 0)

    def sums(d):
        g = gt[pl.ds(pl.multiple_of(near(d) * chunk, chunk), chunk), :]
        acc = dot(g, accm[...])
        ml = dot(stats[...], g, 1, 1)
        ml = ml[0:8] + ml[8:16] + ml[16:24]
        ml = jnp.concatenate([ml, jnp.zeros((8, 128 - chunk), F32)], axis=1)
        return acc, jnp.where((sub8 < 2) & (ml[4:5] < 0.5), NEG, ml)

    def ring(s, kind, src, dst, hop):
        to = mine2((1, -1)[s] * hop)
        return (
            remote(src[0], dst, rs_send.at[s, kind], rs_recv.at[s, kind], to),
            remote(src[1], rx_ml.at[s, kind], rm_send.at[s, kind], rm_recv.at[s, kind], to),
        )

    def landed(s, kind, dst):
        for copy in ring(s, kind, (dst, rx_ml.at[s, kind]), dst, 1):
            copy.wait_recv()

    def store(i, d):
        acc, ml = sums(d)
        tx_acc[i] = acc.astype(BF16)
        tx_ml[i] = ml

    store(2, 4)
    for s in range(2):
        for copy in ring(s, 1, (tx_acc.at[2, pl.ds(s * half, half)], tx_ml.at[2]), a4_acc.at[s], 2):
            start(copy)
    for s in range(2):
        store(s, (3, -3)[s])
        for copy in ring(s, 0, (tx_acc.at[s], tx_ml.at[s]), a3_acc.at[s], 1):
            start(copy)
    for s in range(2):
        store(3 + s, (1, -1)[s])
        for copy in ring(s, 2, (tx_acc.at[3 + s], tx_ml.at[3 + s]), b_acc.at[s, 0], 1):
            start(copy)

    def weigh(mls):
        out = []
        for c in range(2):
            mx = functools.reduce(jnp.maximum, [m[c:c + 1] for m in mls])
            w = [jnp.exp(m[c:c + 1] - mx) for m in mls]
            dn = functools.reduce(jnp.add, [a * m[2 + c:3 + c] for a, m in zip(w, mls)])
            out.append((w, mx, dn))
        return out

    def columns(items):
        return jnp.transpose(
            jnp.concatenate(items + [jnp.zeros((128 - len(items), 128), F32)], axis=0)
        )

    lane128 = iota((8, 128), 1)
    for s in range(2):
        acc, ml = sums((2, -2)[s])
        landed(s, 0, a3_acc.at[s])
        landed(s, 1, a4_acc.at[s])
        inside = (lane128 < half) if s == 0 else (lane128 >= half)
        ml4 = jnp.where((sub8 < 2) & jnp.logical_not(inside), NEG, rx_ml[s, 1])
        mls = [ml, rx_ml[s, 0], ml4]
        st = weigh(mls)
        cols = columns(st[0][0] + st[1][0])
        outs = []
        for c in range(2):
            sl = slice(c * HEAD, (c + 1) * HEAD)
            a3 = a3_acc[s, :, sl].astype(F32)
            a4 = a4_acc[s, :, sl].astype(F32)
            v = acc[:, sl] * cols[:chunk, 3 * c:3 * c + 1] + a3 * cols[:chunk, 3 * c + 1:3 * c + 2]
            add = a4 * cols[s * half:(s + 1) * half, 3 * c + 2:3 * c + 3]
            if s == 0:
                v = jnp.concatenate([v[:half] + add, v[half:]], axis=0)
            else:
                v = jnp.concatenate([v[:half], v[half:] + add], axis=0)
            outs.append(v)
        tx_acc[5 + s] = jnp.concatenate(outs, axis=1).astype(BF16)
        tx_ml[5 + s] = jnp.concatenate(
            [st[0][1], st[1][1], st[0][2], st[1][2], jnp.zeros((4, 128), F32)], axis=0
        )
        for copy in ring(s, 3, (tx_acc.at[5 + s], tx_ml.at[5 + s]), b_acc.at[s, 1], 2):
            start(copy)
    home_acc, home_ml = sums(0)

    loads[5].wait()
    loads[6].wait()
    loads[7].wait()
    qown = jnp.concatenate([q_ref[0], q_ref[1]], axis=0)
    tails = tailv[...].reshape(reqs * 128, 2 * HEAD)
    row32 = iota((32, 128), 0) & 7
    ts, tl = [], []
    for r in range(reqs):
        ok = (row32 == r) & (iota((32, 128), 1) < tlen_ref[r])
        tl.append(ok)
        ts.append(jnp.where(ok, dot(qown, tails[r * 128:(r + 1) * 128, :HEAD], 1, 1) * scale, NEG))
    fresh = nk_ref[...].astype(F32)
    pad = jnp.zeros((8 - reqs, 2 * HEAD), F32)
    news = jnp.concatenate([fresh[:, 0, :], pad, fresh[:, 1, :], pad], axis=0).astype(BF16)
    nrow, ncol = iota((32, 16), 0), iota((32, 16), 1)
    nlive = ((nrow & 7) == (ncol & 7)) & (lax.shift_right_logical(ncol, 3) <= lax.shift_right_logical(nrow, 4))
    ns = jnp.where(nlive, dot(qown, news[:, :HEAD], 1, 1) * scale, NEG)
    peak = jnp.max(ns, axis=1, keepdims=True)
    peak = jnp.maximum(peak, jnp.max(functools.reduce(jnp.maximum, ts), axis=1, keepdims=True))
    nw = jnp.where(nlive, jnp.exp(ns - peak), 0.0)
    tw = [jnp.where(ok, jnp.exp(t - peak), 0.0) for t, ok in zip(ts, tl)]
    own_den = jnp.sum(nw, axis=1, keepdims=True)
    own_den += jnp.sum(functools.reduce(jnp.add, tw), axis=1, keepdims=True)
    own_acc[...] = dot(nw.astype(BF16), news[:, HEAD:]) + dot(
        jnp.concatenate(tw, axis=1).astype(BF16), tails[:, HEAD:]
    )
    own_st[...] = jnp.where(iota((32, 128), 1) == 0, peak, own_den)

    for s in range(2):
        landed(s, 2, b_acc.at[s, 0])
    for s in range(2):
        landed(s, 3, b_acc.at[s, 1])
    st = weigh([home_ml] + [rx_ml[s, kind] for s in range(2) for kind in (2, 3)])
    cols = columns(st[0][0] + st[1][0] + [st[0][1], st[1][1], st[0][2], st[1][2]])[:chunk]
    lane_c = iota((chunk, 128), 1)
    t2v = jnp.zeros((2 * n * 16, HEAD + 128), F32)
    sr, sc = iota((2 * n * 16, chunk), 0), iota((2 * n * 16, chunk), 1)
    for c in range(2):
        sl = slice(c * HEAD, (c + 1) * HEAD)
        acc = home_acc[:, sl] * cols[:, 5 * c:5 * c + 1]
        for i in range(4):
            acc += b_acc[i // 2, i % 2, :, sl].astype(F32) * cols[:, 5 * c + 1 + i:5 * c + 2 + i]
        parts = split3(cols[:, 10 + c:11 + c]) + split3(cols[:, 12 + c:13 + c])
        tile = jnp.zeros((chunk, 128), F32)
        for i, col in enumerate(parts):
            tile = jnp.where(lane_c == i, col, tile)
        rowsrc = jnp.concatenate([acc, tile], axis=1).astype(BF16)
        inner = (sr & 15) - c * 8
        pick_rows = (inner >= 0) & (inner < reqs) & (lax.shift_right_logical(sr, 4) * reqs + inner == sc)
        t2v += dot(jnp.where(pick_rows, 1.0, 0.0).astype(BF16), rowsrc)
    t2[...] = t2v.astype(BF16).reshape(2 * n, 16, HEAD + 128)

    def home(pos, kk):
        return remote(
            t2.at[pos * 2 + kk], r2.at[k, p1], t2_send.at[pos * 2 + kk], t2_recv.at[k, p1],
            mine1(pos, kk),
        )

    for d in order:
        pos = lax.rem(p1 + d, n)
        for kk in range(2):
            start(home(pos, kk))
    start(home(p1, other))
    r2[k, p1] = t2[p1 * 2 + k]
    loads[8].wait()
    for d in range(1, n):
        for h in range(2):
            src = lax.rem((y, z)[h] + d, n)
            remote(t2.at[0], r2.at[h, src], t2_send.at[0], t2_recv.at[h, src], partner).wait_recv()
    src = p1_of(y, z, other)
    remote(t2.at[0], r2.at[other, src], t2_send.at[0], t2_recv.at[other, src], partner).wait_recv()

    heads = []
    for h in range(2):
        cells = [r2[h, i].astype(F32) for i in range(n)]
        ms = [t[:, HEAD:HEAD + 1] + t[:, HEAD + 1:HEAD + 2] + t[:, HEAD + 2:HEAD + 3] for t in cells]
        ds = [t[:, HEAD + 3:HEAD + 4] + t[:, HEAD + 4:HEAD + 5] + t[:, HEAD + 5:HEAD + 6] for t in cells]
        ms.append(own_st[h * 16:(h + 1) * 16, 0:1])
        ds.append(own_st[h * 16:(h + 1) * 16, 1:2])
        accs = [t[:, :HEAD] for t in cells] + [own_acc[h * 16:(h + 1) * 16]]
        mx = functools.reduce(jnp.maximum, ms)
        num = jnp.zeros((16, HEAD), F32)
        dn = jnp.zeros((16, 1), F32)
        for m, dd, acc in zip(ms, ds, accs):
            w = jnp.exp(m - mx)
            num += acc * w
            dn += dd * w
        heads.append(num / dn)
    att = jnp.concatenate(
        [jnp.concatenate([a[0:8], a[8:16]], axis=1) for a in heads], axis=0
    ).astype(BF16)

    hw = wv.shape[1] // 2
    even = x + 1 - 2 * lax.rem(x, 2)
    odd = nx - 1 - x
    if nx == 1:
        for i in range(2):
            out_ref[0, i] = dot(att, wv[:, i * hw:(i + 1) * hw]).astype(BF16)
            out_ref[1, i] = jnp.zeros((16, hw), BF16)
    else:
        def trade(i, turn):
            src = ar.at[i] if turn == 0 else out_ref.at[0, i]
            dst = ar_rx.at[i] if turn == 0 else out_ref.at[1, i]
            to = even if (i + turn) % 2 == 0 else odd
            return remote(src, dst, ar_send.at[turn, i], ar_recv.at[turn, i], (to, b))

        for i in range(2):
            ar[i] = dot(att, wv[:, i * hw:(i + 1) * hw]).astype(BF16)
            start(trade(i, 0))
        for i in range(2):
            trade(i, 0).wait_recv()
            out_ref[0, i] = (ar[i].astype(F32) + ar_rx[i].astype(F32)).astype(BF16)
            if nx > 2:
                start(trade(i, 1))
            else:
                out_ref[1, i] = jnp.zeros((16, hw), BF16)
        for i in range(2):
            if nx > 2:
                trade(i, 1).wait_recv()
    for load in loads[9:]:
        load.wait()
    for copy in pending:
        copy.wait_send()


def finish(sum_ref, hid_ref, gain_ref, score_ref, out_ref, sc_ref):
    reqs = hid_ref.shape[0]
    raw = hid_ref[...].astype(F32)
    total = jnp.concatenate(
        [sum_ref[0, i].astype(F32) + sum_ref[1, i].astype(F32) for i in range(2)], axis=1
    )
    hid = [(raw[:, i, :] + total[8 * i:8 * i + reqs]).astype(BF16).astype(F32) for i in range(2)]
    out_ref[...] = jnp.stack(hid, axis=1).astype(BF16)
    last = hid[1]
    normed = last * lax.rsqrt(jnp.mean(last * last, axis=1, keepdims=True) + 1e-06) * gain_ref[...]
    score = jnp.sum(normed * score_ref[...], axis=1, keepdims=True)
    tile = jnp.concatenate([jnp.broadcast_to(score, (reqs, 128)), jnp.zeros((128 - reqs, 128), F32)], axis=0)
    sc_ref[...] = jnp.transpose(tile)[0, :reqs]


def p1_of(y, z, h):
    return y + h * (z - y)


def body(n, nx, prefix_pool, slot_page, prompt_len, request_ids, tail_len, tail_cache, queries,
         new_kv, hidden, out_weight, norm_gain, score_weight):
    pages = prefix_pool.shape[1]
    reqs, width = hidden.shape[0], hidden.shape[2]
    chunk = n * 2 * reqs
    rows = pages * SAMPLES
    total = n * chunk
    vm = pl.BlockSpec(memory_space=pltpu.VMEM)
    hbm = pl.BlockSpec(memory_space=pl.ANY)
    dma = pltpu.SemaphoreType.DMA
    sums = pl.pallas_call(
        functools.partial(kernel, n, nx, reqs, pages),
        out_shape=(
            pltpu.VMEM((2, 2, 16, width // 2), BF16),
            pltpu.VMEM(hidden.shape, BF16),
            pltpu.VMEM((1, width), F32),
            pltpu.VMEM((1, width), F32),
        ),
        in_specs=[hbm] * 12,
        out_specs=(vm,) * 4,
        scratch_shapes=[
            pltpu.SMEM(slot_page.shape, jnp.int32),
            pltpu.SMEM(prompt_len.shape, jnp.int32),
            pltpu.SMEM(tail_len.shape, jnp.int32),
            pltpu.VMEM(request_ids.shape, jnp.int32),
            pltpu.VMEM(queries.shape, BF16),
            pltpu.VMEM(new_kv.shape[1:], BF16),
            pltpu.VMEM((2, 16, HEAD), BF16),
            pltpu.VMEM((2 * pages, PAGE, 2 * HEAD), BF16),
            pltpu.VMEM((reqs, 128, 2 * HEAD), BF16),
            pltpu.VMEM((2 * HEAD, width), BF16),
            pltpu.VMEM((2 * n, 16, HEAD), BF16),
            pltpu.VMEM((n, chunk, 512), BF16),
            pltpu.VMEM((n, 2 * rows, chunk), BF16),
            pltpu.VMEM((total, 2 * rows), BF16),
            pltpu.VMEM((2 * rows, 512), F32),
            pltpu.VMEM((2 * rows, 512), BF16),
            pltpu.VMEM((24, 2 * rows), BF16),
            pltpu.VMEM((2, pages, 128), F32),
            pltpu.VMEM((2, pages, 128), F32),
            pltpu.VMEM((7, chunk, 512), BF16),
            pltpu.VMEM((7, 8, 128), F32),
            pltpu.VMEM((2, chunk, 512), BF16),
            pltpu.VMEM((2, chunk // 2, 512), BF16),
            pltpu.VMEM((2, 2, chunk, 512), BF16),
            pltpu.VMEM((2, 4, 8, 128), F32),
            pltpu.VMEM((2 * n, 16, HEAD + 128), BF16),
            pltpu.VMEM((2, n, 16, HEAD + 128), BF16),
            pltpu.VMEM((32, HEAD), F32),
            pltpu.VMEM((32, 128), F32),
            pltpu.VMEM((2, 16, width // 2), BF16),
            pltpu.VMEM((2, 16, width // 2), BF16),
            dma((12,)), dma((2 * n,)), dma((2 * n,)),
            dma((2, 4, 2)), dma((2, 4, 2)),
            dma((2,)), dma((2,)),
            dma((2, 4)), dma((2, 4)), dma((2, 4)), dma((2, 4)),
            dma((2 * n,)), dma((2, n)), dma((2, 2)), dma((2, 2)),
        ],
        compiler_params=pltpu.CompilerParams(collective_id=0, has_side_effects=True),
    )(
        slot_page, prompt_len, tail_len, request_ids, queries, new_kv[0],
        prefix_pool[0], tail_cache[0], out_weight, hidden, norm_gain.reshape(1, -1),
        score_weight.reshape(1, -1),
    )
    return pl.pallas_call(
        finish,
        out_shape=(jax.ShapeDtypeStruct(hidden.shape, BF16), jax.ShapeDtypeStruct((reqs,), F32)),
        in_specs=[vm] * 4,
        out_specs=(vm, vm),
    )(*(pltpu.with_memory_space_constraint(a, pltpu.VMEM) for a in sums))


def solution(mesh):
    nx = mesh.shape["kv"]
    n = int(round((mesh.shape["blk"] // 2) ** 0.5))
    in_specs = (
        P("kv", "blk", None, None),
        P("blk"),
        P(),
        P(),
        P("blk"),
        P("kv", "blk", None, None),
        P("blk", None, "kv"),
        P("kv", "blk", None, None),
        P("blk", None, None),
        P("kv", None),
        P(),
        P(),
    )
    out_specs = (P("blk", None, None), P("blk"))
    return jax.shard_map(
        functools.partial(body, n, nx), mesh=mesh, in_specs=in_specs, out_specs=out_specs, check_vma=False
    )
```

```python
import functools

import jax
import jax.numpy as jnp
from jax import lax
from jax.experimental import pallas as pl
from jax.experimental.pallas import tpu as pltpu
from jax.sharding import PartitionSpec as P

MESH = pl.DeviceIdType.MESH
SAMPLES = 16
HEAD = 256
PAGE = 64
NEG = -1e30
F32 = jnp.float32
BF16 = jnp.bfloat16


def iota(shape, dim):
    return lax.broadcasted_iota(jnp.int32, shape, dim)


def dot(a, b, ca=1, cb=0):
    return lax.dot_general(a, b, (((ca,), (cb,)), ((), ())), preferred_element_type=F32)


def floor_div(a, c):
    return jnp.floor((a.astype(F32) + 0.5) * (1.0 / c))


def split3(x):
    a = x.astype(BF16).astype(F32)
    b = (x - a).astype(BF16).astype(F32)
    return a, b, x - a - b


def kernel(
    n, nx, reqs, pages,
    slot_hbm, plen_hbm, tlen_hbm, ids_hbm, q_hbm, nk_hbm, pool_hbm, tail_hbm, w_hbm,
    hid_hbm, gain_hbm, score_hbm,
    out_ref, hid_out, gain_out, score_out,
    slot_ref, plen_ref, tlen_ref, ids_ref, q_in, nk_ref,
    q_ref, poolv, tailv, wv, s1, agm, gm, gt, pick, accm, stats, info_tx, info_rx,
    tx_acc, tx_ml, a3_acc, a4_acc, b_acc, rx_ml, t2, r2, own_acc, own_st, ar, ar_rx,
    local_sem, s1_send, s1_recv, ag_send, ag_recv,
    cx_send, cx_recv, rs_send, rs_recv, rm_send, rm_recv,
    t2_send, t2_recv, ar_send, ar_recv,
):
    chunk = n * 2 * reqs
    half = chunk // 2
    rows = pages * SAMPLES
    prompts = plen_ref.shape[0]
    scale = HEAD ** (-0.5)
    x = lax.axis_index("kv")
    b = lax.axis_index("blk")
    k = lax.rem(b, 2)
    y = lax.rem(lax.div(b, 2), n)
    z = lax.div(b, 2 * n)
    p1 = y + k * (z - y)
    p2 = z + k * (y - z)
    other = 1 - k

    def at(zz, yy, kk):
        return (x, (zz * n + yy) * 2 + kk)

    def ring1(pos, h, kk):
        if h == 0:
            return at(z, pos, kk)
        return at(pos, y, kk)

    def mine1(pos, kk):
        return at(z + k * (pos - z), pos + k * (y - pos), kk)

    def mine2(d):
        pos = lax.rem(p2 + (d + n), n)
        return at(pos + k * (z - pos), y + k * (pos - y), k)

    def near(d):
        return lax.rem(p2 + (d + n), n)

    partner = at(z, y, other)

    def remote(src, dst, send, recv, to):
        return pltpu.make_async_remote_copy(
            src_ref=src, dst_ref=dst, send_sem=send, recv_sem=recv, device_id=to, device_id_type=MESH
        )

    pending = []

    def start(copy):
        copy.start()
        pending.append(copy)

    barrier = pltpu.get_barrier_semaphore()

    def greet(to):
        pl.semaphore_signal(barrier, inc=1, device_id=to, device_id_type=MESH)

    for d in [i for j in range(1, n // 2 + 1) for i in ((j, n - j) if 2 * j != n else (j,))]:
        for kk in range(2):
            greet(at(z, lax.rem(y + d, n), kk))
            greet(at(lax.rem(z + d, n), y, kk))
    greet(partner)
    if nx > 1:
        greet((x + 1 - 2 * lax.rem(x, 2), b))
    if nx > 2:
        greet((nx - 1 - x, b))

    loads = [
        pltpu.make_async_copy(src, dst, local_sem.at[i])
        for i, (src, dst) in enumerate([
            (q_hbm, q_in), (plen_hbm, plen_ref), (slot_hbm, slot_ref), (ids_hbm, ids_ref),
            (pool_hbm, poolv.at[pl.ds(0, pages)]), (tlen_hbm, tlen_ref), (nk_hbm, nk_ref),
            (tail_hbm, tailv), (w_hbm, wv),
            (hid_hbm, hid_out), (gain_hbm, gain_out), (score_hbm, score_out),
        ])
    ]
    for load in loads:
        load.start()
    loads[0].wait()

    raw = q_in[...].astype(F32)
    gap = jnp.zeros((8 - reqs, HEAD), F32)
    for i in range(2):
        q_ref[i] = jnp.concatenate(
            [raw[:, i, 0:HEAD], gap, raw[:, i, HEAD:2 * HEAD], gap], axis=0
        ).astype(BF16)
    s1[p1 * 2 + k] = q_ref[k]

    pl.semaphore_wait(barrier, 1 + 4 * (n - 1) + min(nx - 1, 2))

    def first(h, d):
        mypos = (y, z)[h]
        pos = lax.rem(mypos + d, n)
        slot = mypos * 2 + k
        return remote(
            q_ref.at[h], s1.at[slot], s1_send.at[h * n + d], s1_recv.at[slot], ring1(pos, h, h)
        )

    order = [d for i in range(n // 2, 0, -1) for d in ((i, n - i) if 2 * i != n else (i,))]
    for d in order:
        for h in range(2):
            start(first(h, d))
    slot = p1_of(y, z, other) * 2 + k
    start(remote(q_ref.at[other], s1.at[slot], s1_send.at[other * n], s1_recv.at[slot], partner))

    swap = remote(pool_hbm, poolv.at[pl.ds(pages, pages)], cx_send.at[0], cx_recv.at[0], partner)
    start(swap)

    loads[1].wait()
    loads[2].wait()
    lane = iota((1, 128), 1)
    lens = jnp.zeros((1, 128), jnp.int32)
    for p in range(prompts):
        lens = jnp.where(lane == p, plen_ref[p], lens)
    need = lax.shift_right_logical(lens + (PAGE - 1), 6).astype(F32)
    grid_r, grid_c = iota((128, 128), 0), iota((128, 128), 1)
    need_t = jnp.transpose(jnp.broadcast_to(need, (128, 128)))
    ends = jnp.sum(jnp.where(grid_r <= grid_c, need_t, 0.0), axis=0, keepdims=True)
    starts = ends - need
    page_r = iota((pages, 128), 0)
    slots = jnp.zeros((pages, 128), jnp.int32)
    for j in range(pages):
        slots = jnp.where(page_r == j, slot_ref[j], slots)
    slots = slots.astype(F32)
    plane = iota((pages, 128), 1)
    owner = jnp.sum(
        jnp.where((plane < prompts) & (slots >= ends), 1.0, 0.0), axis=1, keepdims=True
    )
    used = owner < prompts
    owner = jnp.minimum(owner, prompts - 1.0)
    mine = plane.astype(F32) == owner
    begin = jnp.sum(jnp.where(mine, starts, 0.0), axis=1, keepdims=True)
    length = jnp.sum(jnp.where(mine, lens.astype(F32), 0.0), axis=1, keepdims=True)
    live = jnp.where(used, length - (slots - begin) * PAGE, 0.0)
    info_tx[0] = owner * SAMPLES + jnp.zeros_like(slots)
    info_tx[1] = live + jnp.zeros_like(slots)
    info = remote(info_tx, info_rx, cx_send.at[1], cx_recv.at[1], partner)
    start(info)

    pr, pc = iota((chunk, 2 * n * 16), 0), iota((chunk, 2 * n * 16), 1).astype(F32)
    cell = floor_div(pr, reqs)
    want = cell * 16.0 + (pr.astype(F32) - cell * reqs)
    for d in range(n):
        for kk in range(2):
            slot = lax.rem(p1 + d, n) * 2 + lax.rem(k + kk, 2)
            if d or kk:
                remote(q_ref.at[0], s1.at[slot], s1_send.at[0], s1_recv.at[slot], partner).wait_recv()
    s1v = s1[...].reshape(2 * n * 16, HEAD)
    packed = [
        dot(jnp.where(pc == want + c * 8.0, 1.0, 0.0).astype(BF16), s1v) for c in range(2)
    ]
    agm[p2] = jnp.concatenate(packed, axis=1).astype(BF16)

    def part(src, piece):
        return agm.at[src, pl.ds(piece * half, half)]

    def second(src, s, hop, kind, piece):
        return remote(
            part(src, piece), part(src, piece), ag_send.at[s, kind, piece], ag_recv.at[s, kind, piece],
            mine2((1, -1)[s] * hop),
        )

    def arrived(s, kind, piece):
        src = near(-(1, -1)[s] * (kind + 1))
        second(src, s, 1, kind, piece).wait_recv()
        return src

    for i in range(2):
        for s in range(2):
            start(second(p2, s, 2, 1, i ^ s))
    for i in range(2):
        for s in range(2):
            start(second(p2, s, 1, 0, i ^ s))

    total = n * chunk
    loads[3].wait()
    ids = ids_ref[...].reshape(1, total)
    grid_u = iota((n * n, total), 0).astype(F32)
    grid_e = iota((n * n, total), 1)
    on = floor_div(grid_e, 2 * reqs) == grid_u
    e_in = iota((total, 128), 0)
    e_mod = e_in.astype(F32) - floor_div(e_in, 2 * reqs) * (2 * reqs)
    l_in = iota((1, 128), 1)
    l_div = floor_div(l_in, 2 * reqs)
    l_mod = l_in.astype(F32) - l_div * (2 * reqs)
    spread_e = jnp.where(e_mod == l_mod, 1.0, 0.0).astype(BF16)
    hi = jnp.where(on, lax.shift_right_logical(ids, 5).astype(F32), 0.0).astype(BF16)
    lo = jnp.where(on, (ids & 31).astype(F32), 0.0).astype(BF16)
    table = dot(hi, spread_e) * 32.0 + dot(lo, spread_e)
    nat = jnp.concatenate(
        [
            jnp.sum(
                jnp.where(iota((n, 128), 0).astype(F32) == l_div, table[i * n:(i + 1) * n], 0.0),
                axis=0, keepdims=True,
            )
            for i in range(n)
        ],
        axis=0,
    )
    perm = jnp.zeros((n, 128), F32)
    for i in range(n):
        perm = jnp.where(l_div == float(i), table[i * n:(i + 1) * n], perm)
    ids_m = jnp.where(k == 0, nat, perm)
    info.wait_recv()
    pair = 2 * pages
    sample = (iota((2 * rows, 128), 0) & (SAMPLES - 1)).astype(F32)

    def per_row(i):
        v = jnp.concatenate([info_tx[i], info_rx[i]], axis=0)
        return jnp.broadcast_to(v[:, None, :], (pair, SAMPLES, 128)).reshape(2 * rows, 128)

    target = per_row(0) + sample
    live_c = per_row(1)
    for p in range(n):
        gm[p] = jnp.where(target[:, :chunk] == ids_m[p:p + 1, :chunk], 1.0, 0.0).astype(BF16)

    for i in range(2):
        for s in range(2):
            piece = i ^ s
            src = arrived(s, 1, piece)
            if i == 0:
                start(second(src, s, 2, 3, piece))
            start(second(src, s, 1, 2, piece))
    pick[...] = dot(gm[p2], agm[p2])

    def take(d):
        src = near(d)
        pick[...] += dot(gm[src], agm[src])

    for s in range(2):
        take((-2, 2)[s])
    target_row = jnp.concatenate(
        [jnp.transpose(target[i * 128:(i + 1) * 128])[0:8] for i in range(2 * rows // 128)], axis=1
    )
    live_row = jnp.concatenate(
        [jnp.transpose(live_c[i * 128:(i + 1) * 128])[0:1] for i in range(2 * rows // 128)], axis=1
    )
    both_t = jnp.concatenate([target_row[0:4, :rows], target_row[0:4, rows:]], axis=0)
    swap_t = jnp.concatenate([target_row[0:4, rows:], target_row[0:4, :rows]], axis=0)
    lane8 = iota((8, rows), 1)
    lower = iota((8, rows), 0) >= 4
    lead = jnp.where(lower & (swap_t == both_t), 0.0, 1.0)
    for d in range(1, pages):
        same = pltpu.roll(both_t, d * SAMPLES, 1) == both_t
        cross = pltpu.roll(swap_t, d * SAMPLES, 1) == both_t
        lead = jnp.where((same & (lane8 >= d * SAMPLES)) | (cross & lower), 0.0, lead)
    ids_t = jnp.transpose(jnp.concatenate([ids_m, jnp.zeros((128 - n, 128), F32)], axis=0))
    for p in range(n):
        gt[pl.ds(p * chunk, chunk), :] = jnp.where(
            ids_t[:chunk, p:p + 1] == target_row[0:1], 1.0, 0.0
        ).astype(BF16)
    for i in range(2):
        for s in range(2):
            arrived(s, 0, i ^ s)
    for s in range(2):
        take((-1, 1)[s])
    for i in range(2):
        for s in range(2):
            arrived(s, 2, i ^ s)
    for s in range(2):
        take((-3, 3)[s])
    for s in range(2):
        arrived(s, 3, s)
    take(4)

    loads[4].wait()
    swap.wait_recv()
    blocks = pair // 8
    scores, peaks = [], []
    page_l = lax.shift_right_logical(iota((PAGE, 256), 1) & 127, 4)
    for blk in range(blocks):
        keys = poolv[blk * 8:(blk + 1) * 8].reshape(8 * PAGE, 2 * HEAD)[:, :HEAD]
        sl = slice(blk * 128, (blk + 1) * 128)
        qb = jnp.concatenate([pick[sl, :HEAD], pick[sl, HEAD:]], axis=0).astype(BF16)
        full = dot(keys, qb, 1, 1)
        s = jnp.zeros((PAGE, 256), F32)
        for j in range(8):
            s = jnp.where(page_l == j, full[j * PAGE:(j + 1) * PAGE], s)
        lv = jnp.concatenate([live_row[:, sl]] * 2, axis=1)
        alive = iota((PAGE, 256), 0).astype(F32) < lv
        s = jnp.where(alive, s * scale, NEG)
        scores.append((s, alive))
        m = jnp.max(s, axis=0, keepdims=True)
        peaks.append(jnp.concatenate([m[:, :128], m[:, 128:]], axis=0))
    hb = blocks // 2
    low, high = jnp.concatenate(peaks[:hb], axis=1), jnp.concatenate(peaks[hb:], axis=1)

    both_m = jnp.concatenate([low, low, high, high], axis=0)
    swap_m = jnp.concatenate([high, high, low, low], axis=0)
    top = jnp.where(swap_t == both_t, jnp.maximum(both_m, swap_m), both_m)
    for d in range(1, pages):
        same = pltpu.roll(both_t, d * SAMPLES, 1) == both_t
        cross = pltpu.roll(swap_t, d * SAMPLES, 1) == both_t
        top = jnp.where(same, jnp.maximum(top, pltpu.roll(both_m, d * SAMPLES, 1)), top)
        top = jnp.where(cross, jnp.maximum(top, pltpu.roll(swap_m, d * SAMPLES, 1)), top)

    dens = []
    page_r8 = lax.shift_right_logical(iota((256, 8 * PAGE), 0) & 127, 4)
    own_page = page_r8 == lax.shift_right_logical(iota((256, 8 * PAGE), 1), 6)
    for blk in range(blocks):
        s, alive = scores[blk]
        base = 4 * (blk // hb)
        tb = top[base:base + 2, (blk % hb) * 128:(blk % hb + 1) * 128]
        tb = jnp.concatenate([tb[0:1], tb[1:2]], axis=1)
        w = jnp.where(alive, jnp.exp(s - tb), 0.0)
        dsum = jnp.sum(w, axis=0, keepdims=True)
        dens.append(jnp.concatenate([dsum[:, :128], dsum[:, 128:]], axis=0))
        wt = jnp.transpose(w)
        wt = jnp.concatenate([wt, wt], axis=1)
        wide = jnp.where(own_page, jnp.concatenate([wt] * 4, axis=1), 0.0).astype(BF16)
        values = poolv[blk * 8:(blk + 1) * 8].reshape(8 * PAGE, 2 * HEAD)[:, HEAD:]
        acc = dot(wide, values).astype(BF16)
        accm[blk * 128:(blk + 1) * 128, :HEAD] = acc[:128]
        accm[blk * 128:(blk + 1) * 128, HEAD:] = acc[128:]
    st = jnp.concatenate(
        [
            jnp.concatenate([jnp.where(lead[0:2] > 0.5, top[0:2], 0.0),
                             jnp.where(lead[4:6] > 0.5, top[4:6], 0.0)], axis=1),
            jnp.concatenate(dens, axis=1),
            jnp.concatenate([lead[0:1], lead[4:5]], axis=1),
            jnp.zeros((3, 2 * rows), F32),
        ],
        axis=0,
    )
    stats[...] = jnp.concatenate(split3(st), axis=0).astype(BF16)

    sub8 = iota((8, 128), 0)

    def sums(d):
        g = gt[pl.ds(pl.multiple_of(near(d) * chunk, chunk), chunk), :]
        acc = dot(g, accm[...])
        ml = dot(stats[...], g, 1, 1)
        ml = ml[0:8] + ml[8:16] + ml[16:24]
        ml = jnp.concatenate([ml, jnp.zeros((8, 128 - chunk), F32)], axis=1)
        return acc, jnp.where((sub8 < 2) & (ml[4:5] < 0.5), NEG, ml)

    def ring(s, kind, src, dst, hop):
        to = mine2((1, -1)[s] * hop)
        return (
            remote(src[0], dst, rs_send.at[s, kind], rs_recv.at[s, kind], to),
            remote(src[1], rx_ml.at[s, kind], rm_send.at[s, kind], rm_recv.at[s, kind], to),
        )

    def landed(s, kind, dst):
        for copy in ring(s, kind, (dst, rx_ml.at[s, kind]), dst, 1):
            copy.wait_recv()

    def store(i, d):
        acc, ml = sums(d)
        tx_acc[i] = acc.astype(BF16)
        tx_ml[i] = ml

    store(2, 4)
    for s in range(2):
        for copy in ring(s, 1, (tx_acc.at[2, pl.ds(s * half, half)], tx_ml.at[2]), a4_acc.at[s], 2):
            start(copy)
    for s in range(2):
        store(s, (3, -3)[s])
        for copy in ring(s, 0, (tx_acc.at[s], tx_ml.at[s]), a3_acc.at[s], 1):
            start(copy)

    def weigh(mls):
        out = []
        for c in range(2):
            mx = functools.reduce(jnp.maximum, [m[c:c + 1] for m in mls])
            w = [jnp.exp(m[c:c + 1] - mx) for m in mls]
            dn = functools.reduce(jnp.add, [a * m[2 + c:3 + c] for a, m in zip(w, mls)])
            out.append((w, mx, dn))
        return out

    def columns(items):
        return jnp.transpose(
            jnp.concatenate(items + [jnp.zeros((128 - len(items), 128), F32)], axis=0)
        )

    lane128 = iota((8, 128), 1)
    for s in range(2):
        acc, ml = sums((2, -2)[s])
        landed(s, 0, a3_acc.at[s])
        landed(s, 1, a4_acc.at[s])
        inside = (lane128 < half) if s == 0 else (lane128 >= half)
        ml4 = jnp.where((sub8 < 2) & jnp.logical_not(inside), NEG, rx_ml[s, 1])
        mls = [ml, rx_ml[s, 0], ml4]
        st = weigh(mls)
        cols = columns(st[0][0] + st[1][0])
        outs = []
        for c in range(2):
            sl = slice(c * HEAD, (c + 1) * HEAD)
            a3 = a3_acc[s, :, sl].astype(F32)
            a4 = a4_acc[s, :, sl].astype(F32)
            v = acc[:, sl] * cols[:chunk, 3 * c:3 * c + 1] + a3 * cols[:chunk, 3 * c + 1:3 * c + 2]
            add = a4 * cols[s * half:(s + 1) * half, 3 * c + 2:3 * c + 3]
            if s == 0:
                v = jnp.concatenate([v[:half] + add, v[half:]], axis=0)
            else:
                v = jnp.concatenate([v[:half], v[half:] + add], axis=0)
            outs.append(v)
        tx_acc[5 + s] = jnp.concatenate(outs, axis=1).astype(BF16)
        tx_ml[5 + s] = jnp.concatenate(
            [st[0][1], st[1][1], st[0][2], st[1][2], jnp.zeros((4, 128), F32)], axis=0
        )
        for copy in ring(s, 3, (tx_acc.at[5 + s], tx_ml.at[5 + s]), b_acc.at[s, 1], 2):
            start(copy)
    for s in range(2):
        store(3 + s, (1, -1)[s])
        for copy in ring(s, 2, (tx_acc.at[3 + s], tx_ml.at[3 + s]), b_acc.at[s, 0], 1):
            start(copy)
    home_acc, home_ml = sums(0)

    loads[5].wait()
    loads[6].wait()
    loads[7].wait()
    qown = jnp.concatenate([q_ref[0], q_ref[1]], axis=0)
    tails = tailv[...].reshape(reqs * 128, 2 * HEAD)
    row32 = iota((32, 128), 0) & 7
    ts, tl = [], []
    for r in range(reqs):
        ok = (row32 == r) & (iota((32, 128), 1) < tlen_ref[r])
        tl.append(ok)
        ts.append(jnp.where(ok, dot(qown, tails[r * 128:(r + 1) * 128, :HEAD], 1, 1) * scale, NEG))
    fresh = nk_ref[...].astype(F32)
    pad = jnp.zeros((8 - reqs, 2 * HEAD), F32)
    news = jnp.concatenate([fresh[:, 0, :], pad, fresh[:, 1, :], pad], axis=0).astype(BF16)
    nrow, ncol = iota((32, 16), 0), iota((32, 16), 1)
    nlive = ((nrow & 7) == (ncol & 7)) & (lax.shift_right_logical(ncol, 3) <= lax.shift_right_logical(nrow, 4))
    ns = jnp.where(nlive, dot(qown, news[:, :HEAD], 1, 1) * scale, NEG)
    peak = jnp.max(ns, axis=1, keepdims=True)
    peak = jnp.maximum(peak, jnp.max(functools.reduce(jnp.maximum, ts), axis=1, keepdims=True))
    nw = jnp.where(nlive, jnp.exp(ns - peak), 0.0)
    tw = [jnp.where(ok, jnp.exp(t - peak), 0.0) for t, ok in zip(ts, tl)]
    own_den = jnp.sum(nw, axis=1, keepdims=True)
    own_den += jnp.sum(functools.reduce(jnp.add, tw), axis=1, keepdims=True)
    own_acc[...] = dot(nw.astype(BF16), news[:, HEAD:]) + dot(
        jnp.concatenate(tw, axis=1).astype(BF16), tails[:, HEAD:]
    )
    own_st[...] = jnp.where(iota((32, 128), 1) == 0, peak, own_den)

    for s in range(2):
        landed(s, 2, b_acc.at[s, 0])
    for s in range(2):
        landed(s, 3, b_acc.at[s, 1])
    st = weigh([home_ml] + [rx_ml[s, kind] for s in range(2) for kind in (2, 3)])
    cols = columns(st[0][0] + st[1][0] + [st[0][1], st[1][1], st[0][2], st[1][2]])[:chunk]
    lane_c = iota((chunk, 128), 1)
    t2v = jnp.zeros((2 * n * 16, HEAD + 128), F32)
    sr, sc = iota((2 * n * 16, chunk), 0), iota((2 * n * 16, chunk), 1)
    for c in range(2):
        sl = slice(c * HEAD, (c + 1) * HEAD)
        acc = home_acc[:, sl] * cols[:, 5 * c:5 * c + 1]
        for i in range(4):
            acc += b_acc[i // 2, i % 2, :, sl].astype(F32) * cols[:, 5 * c + 1 + i:5 * c + 2 + i]
        parts = split3(cols[:, 10 + c:11 + c]) + split3(cols[:, 12 + c:13 + c])
        tile = jnp.zeros((chunk, 128), F32)
        for i, col in enumerate(parts):
            tile = jnp.where(lane_c == i, col, tile)
        rowsrc = jnp.concatenate([acc, tile], axis=1).astype(BF16)
        inner = (sr & 15) - c * 8
        pick_rows = (inner >= 0) & (inner < reqs) & (lax.shift_right_logical(sr, 4) * reqs + inner == sc)
        t2v += dot(jnp.where(pick_rows, 1.0, 0.0).astype(BF16), rowsrc)
    t2[...] = t2v.astype(BF16).reshape(2 * n, 16, HEAD + 128)

    def home(pos, kk):
        return remote(
            t2.at[pos * 2 + kk], r2.at[k, p1], t2_send.at[pos * 2 + kk], t2_recv.at[k, p1],
            mine1(pos, kk),
        )

    for d in order:
        pos = lax.rem(p1 + d, n)
        for kk in range(2):
            start(home(pos, kk))
    start(home(p1, other))
    r2[k, p1] = t2[p1 * 2 + k]
    loads[8].wait()
    for d in range(1, n):
        for h in range(2):
            src = lax.rem((y, z)[h] + d, n)
            remote(t2.at[0], r2.at[h, src], t2_send.at[0], t2_recv.at[h, src], partner).wait_recv()
    src = p1_of(y, z, other)
    remote(t2.at[0], r2.at[other, src], t2_send.at[0], t2_recv.at[other, src], partner).wait_recv()

    heads = []
    for h in range(2):
        cells = [r2[h, i].astype(F32) for i in range(n)]
        ms = [t[:, HEAD:HEAD + 1] + t[:, HEAD + 1:HEAD + 2] + t[:, HEAD + 2:HEAD + 3] for t in cells]
        ds = [t[:, HEAD + 3:HEAD + 4] + t[:, HEAD + 4:HEAD + 5] + t[:, HEAD + 5:HEAD + 6] for t in cells]
        ms.append(own_st[h * 16:(h + 1) * 16, 0:1])
        ds.append(own_st[h * 16:(h + 1) * 16, 1:2])
        accs = [t[:, :HEAD] for t in cells] + [own_acc[h * 16:(h + 1) * 16]]
        mx = functools.reduce(jnp.maximum, ms)
        num = jnp.zeros((16, HEAD), F32)
        dn = jnp.zeros((16, 1), F32)
        for m, dd, acc in zip(ms, ds, accs):
            w = jnp.exp(m - mx)
            num += acc * w
            dn += dd * w
        heads.append(num / dn)
    att = jnp.concatenate(
        [jnp.concatenate([a[0:8], a[8:16]], axis=1) for a in heads], axis=0
    ).astype(BF16)

    hw = wv.shape[1] // 2
    even = x + 1 - 2 * lax.rem(x, 2)
    odd = nx - 1 - x
    if nx == 1:
        for i in range(2):
            out_ref[0, i] = dot(att, wv[:, i * hw:(i + 1) * hw]).astype(BF16)
            out_ref[1, i] = jnp.zeros((16, hw), BF16)
    else:
        def trade(i, turn):
            src = ar.at[i] if turn == 0 else out_ref.at[0, i]
            dst = ar_rx.at[i] if turn == 0 else out_ref.at[1, i]
            to = even if (i + turn) % 2 == 0 else odd
            return remote(src, dst, ar_send.at[turn, i], ar_recv.at[turn, i], (to, b))

        for i in range(2):
            ar[i] = dot(att, wv[:, i * hw:(i + 1) * hw]).astype(BF16)
            start(trade(i, 0))
        for i in range(2):
            trade(i, 0).wait_recv()
            out_ref[0, i] = (ar[i].astype(F32) + ar_rx[i].astype(F32)).astype(BF16)
            if nx > 2:
                start(trade(i, 1))
            else:
                out_ref[1, i] = jnp.zeros((16, hw), BF16)
        for i in range(2):
            if nx > 2:
                trade(i, 1).wait_recv()
    for load in loads[9:]:
        load.wait()
    for copy in pending:
        copy.wait_send()


def finish(sum_ref, hid_ref, gain_ref, score_ref, out_ref, sc_ref):
    reqs = hid_ref.shape[0]
    raw = hid_ref[...].astype(F32)
    total = jnp.concatenate(
        [sum_ref[0, i].astype(F32) + sum_ref[1, i].astype(F32) for i in range(2)], axis=1
    )
    hid = [(raw[:, i, :] + total[8 * i:8 * i + reqs]).astype(BF16).astype(F32) for i in range(2)]
    out_ref[...] = jnp.stack(hid, axis=1).astype(BF16)
    last = hid[1]
    normed = last * lax.rsqrt(jnp.mean(last * last, axis=1, keepdims=True) + 1e-06) * gain_ref[...]
    score = jnp.sum(normed * score_ref[...], axis=1, keepdims=True)
    tile = jnp.concatenate([jnp.broadcast_to(score, (reqs, 128)), jnp.zeros((128 - reqs, 128), F32)], axis=0)
    sc_ref[...] = jnp.transpose(tile)[0, :reqs]


def p1_of(y, z, h):
    return y + h * (z - y)


def body(n, nx, prefix_pool, slot_page, prompt_len, request_ids, tail_len, tail_cache, queries,
         new_kv, hidden, out_weight, norm_gain, score_weight):
    pages = prefix_pool.shape[1]
    reqs, width = hidden.shape[0], hidden.shape[2]
    chunk = n * 2 * reqs
    rows = pages * SAMPLES
    total = n * chunk
    vm = pl.BlockSpec(memory_space=pltpu.VMEM)
    hbm = pl.BlockSpec(memory_space=pl.ANY)
    dma = pltpu.SemaphoreType.DMA
    sums = pl.pallas_call(
        functools.partial(kernel, n, nx, reqs, pages),
        out_shape=(
            pltpu.VMEM((2, 2, 16, width // 2), BF16),
            pltpu.VMEM(hidden.shape, BF16),
            pltpu.VMEM((1, width), F32),
            pltpu.VMEM((1, width), F32),
        ),
        in_specs=[hbm] * 12,
        out_specs=(vm,) * 4,
        scratch_shapes=[
            pltpu.SMEM(slot_page.shape, jnp.int32),
            pltpu.SMEM(prompt_len.shape, jnp.int32),
            pltpu.SMEM(tail_len.shape, jnp.int32),
            pltpu.VMEM(request_ids.shape, jnp.int32),
            pltpu.VMEM(queries.shape, BF16),
            pltpu.VMEM(new_kv.shape[1:], BF16),
            pltpu.VMEM((2, 16, HEAD), BF16),
            pltpu.VMEM((2 * pages, PAGE, 2 * HEAD), BF16),
            pltpu.VMEM((reqs, 128, 2 * HEAD), BF16),
            pltpu.VMEM((2 * HEAD, width), BF16),
            pltpu.VMEM((2 * n, 16, HEAD), BF16),
            pltpu.VMEM((n, chunk, 512), BF16),
            pltpu.VMEM((n, 2 * rows, chunk), BF16),
            pltpu.VMEM((total, 2 * rows), BF16),
            pltpu.VMEM((2 * rows, 512), F32),
            pltpu.VMEM((2 * rows, 512), BF16),
            pltpu.VMEM((24, 2 * rows), BF16),
            pltpu.VMEM((2, pages, 128), F32),
            pltpu.VMEM((2, pages, 128), F32),
            pltpu.VMEM((7, chunk, 512), BF16),
            pltpu.VMEM((7, 8, 128), F32),
            pltpu.VMEM((2, chunk, 512), BF16),
            pltpu.VMEM((2, chunk // 2, 512), BF16),
            pltpu.VMEM((2, 2, chunk, 512), BF16),
            pltpu.VMEM((2, 4, 8, 128), F32),
            pltpu.VMEM((2 * n, 16, HEAD + 128), BF16),
            pltpu.VMEM((2, n, 16, HEAD + 128), BF16),
            pltpu.VMEM((32, HEAD), F32),
            pltpu.VMEM((32, 128), F32),
            pltpu.VMEM((2, 16, width // 2), BF16),
            pltpu.VMEM((2, 16, width // 2), BF16),
            dma((12,)), dma((2 * n,)), dma((2 * n,)),
            dma((2, 4, 2)), dma((2, 4, 2)),
            dma((2,)), dma((2,)),
            dma((2, 4)), dma((2, 4)), dma((2, 4)), dma((2, 4)),
            dma((2 * n,)), dma((2, n)), dma((2, 2)), dma((2, 2)),
        ],
        compiler_params=pltpu.CompilerParams(collective_id=0, has_side_effects=True),
    )(
        slot_page, prompt_len, tail_len, request_ids, queries, new_kv[0],
        prefix_pool[0], tail_cache[0], out_weight, hidden, norm_gain.reshape(1, -1),
        score_weight.reshape(1, -1),
    )
    return pl.pallas_call(
        finish,
        out_shape=(jax.ShapeDtypeStruct(hidden.shape, BF16), jax.ShapeDtypeStruct((reqs,), F32)),
        in_specs=[vm] * 4,
        out_specs=(vm, vm),
    )(*(pltpu.with_memory_space_constraint(a, pltpu.VMEM) for a in sums))


def solution(mesh):
    nx = mesh.shape["kv"]
    n = int(round((mesh.shape["blk"] // 2) ** 0.5))
    in_specs = (
        P("kv", "blk", None, None),
        P("blk"),
        P(),
        P(),
        P("blk"),
        P("kv", "blk", None, None),
        P("blk", None, "kv"),
        P("kv", "blk", None, None),
        P("blk", None, None),
        P("kv", None),
        P(),
        P(),
    )
    out_specs = (P("blk", None, None), P("blk"))
    return jax.shard_map(
        functools.partial(body, n, nx), mesh=mesh, in_specs=in_specs, out_specs=out_specs, check_vma=False
    )
```

```python
import functools

import jax
import jax.numpy as jnp
from jax import lax
from jax.experimental import pallas as pl
from jax.experimental.pallas import tpu as pltpu
from jax.sharding import PartitionSpec as P

MESH = pl.DeviceIdType.MESH
SAMPLES = 16
HEAD = 256
PAGE = 64
NEG = -1e30
F32 = jnp.float32
BF16 = jnp.bfloat16


def iota(shape, dim):
    return lax.broadcasted_iota(jnp.int32, shape, dim)


def dot(a, b, ca=1, cb=0):
    return lax.dot_general(a, b, (((ca,), (cb,)), ((), ())), preferred_element_type=F32)


def floor_div(a, c):
    return jnp.floor((a.astype(F32) + 0.5) * (1.0 / c))


def split3(x):
    a = x.astype(BF16).astype(F32)
    b = (x - a).astype(BF16).astype(F32)
    return a, b, x - a - b


def kernel(
    n, nx, reqs, pages,
    slot_hbm, plen_hbm, tlen_hbm, ids_hbm, q_hbm, nk_hbm, pool_hbm, tail_hbm, w_hbm,
    hid_hbm, gain_hbm, score_hbm,
    out_ref, hid_out, gain_out, score_out,
    slot_ref, plen_ref, tlen_ref, ids_ref, q_in, nk_ref,
    q_ref, poolv, tailv, wv, s1, agm, gm, gt, pick, accm, stats, info_tx, info_rx,
    tx_acc, tx_ml, a3_acc, a4_acc, b_acc, rx_ml, t2, r2, own_acc, own_st, ar, ar_rx,
    local_sem, s1_send, s1_recv, ag_send, ag_recv,
    cx_send, cx_recv, rs_send, rs_recv, rm_send, rm_recv,
    t2_send, t2_recv, ar_send, ar_recv,
):
    chunk = n * 2 * reqs
    half = chunk // 2
    rows = pages * SAMPLES
    prompts = plen_ref.shape[0]
    scale = HEAD ** (-0.5)
    x = lax.axis_index("kv")
    b = lax.axis_index("blk")
    k = lax.rem(b, 2)
    y = lax.rem(lax.div(b, 2), n)
    z = lax.div(b, 2 * n)
    p1 = y + k * (z - y)
    p2 = z + k * (y - z)
    other = 1 - k

    def at(zz, yy, kk):
        return (x, (zz * n + yy) * 2 + kk)

    def ring1(pos, h, kk):
        if h == 0:
            return at(z, pos, kk)
        return at(pos, y, kk)

    def mine1(pos, kk):
        return at(z + k * (pos - z), pos + k * (y - pos), kk)

    def mine2(d):
        pos = lax.rem(p2 + (d + n), n)
        return at(pos + k * (z - pos), y + k * (pos - y), k)

    def near(d):
        return lax.rem(p2 + (d + n), n)

    partner = at(z, y, other)

    def remote(src, dst, send, recv, to):
        return pltpu.make_async_remote_copy(
            src_ref=src, dst_ref=dst, send_sem=send, recv_sem=recv, device_id=to, device_id_type=MESH
        )

    pending = []

    def start(copy):
        copy.start()
        pending.append(copy)

    barrier = pltpu.get_barrier_semaphore()

    def greet(to):
        pl.semaphore_signal(barrier, inc=1, device_id=to, device_id_type=MESH)

    for d in [i for j in range(1, n // 2 + 1) for i in ((j, n - j) if 2 * j != n else (j,))]:
        for kk in range(2):
            greet(at(z, lax.rem(y + d, n), kk))
            greet(at(lax.rem(z + d, n), y, kk))
    greet(partner)
    if nx > 1:
        greet((x + 1 - 2 * lax.rem(x, 2), b))
    if nx > 2:
        greet((nx - 1 - x, b))

    loads = [
        pltpu.make_async_copy(src, dst, local_sem.at[i])
        for i, (src, dst) in enumerate([
            (q_hbm, q_in), (plen_hbm, plen_ref), (slot_hbm, slot_ref), (ids_hbm, ids_ref),
            (pool_hbm, poolv.at[pl.ds(0, pages)]), (tlen_hbm, tlen_ref), (nk_hbm, nk_ref),
            (tail_hbm, tailv), (w_hbm, wv),
            (hid_hbm, hid_out), (gain_hbm, gain_out), (score_hbm, score_out),
        ])
    ]
    for load in loads:
        load.start()
    loads[0].wait()

    raw = q_in[...].astype(F32)
    gap = jnp.zeros((8 - reqs, HEAD), F32)
    for i in range(2):
        q_ref[i] = jnp.concatenate(
            [raw[:, i, 0:HEAD], gap, raw[:, i, HEAD:2 * HEAD], gap], axis=0
        ).astype(BF16)
    s1[p1 * 2 + k] = q_ref[k]

    pl.semaphore_wait(barrier, 1 + 4 * (n - 1) + min(nx - 1, 2))

    def first(h, d):
        mypos = (y, z)[h]
        pos = lax.rem(mypos + d, n)
        slot = mypos * 2 + k
        return remote(
            q_ref.at[h], s1.at[slot], s1_send.at[h * n + d], s1_recv.at[slot], ring1(pos, h, h)
        )

    order = [d for i in range(n // 2, 0, -1) for d in ((i, n - i) if 2 * i != n else (i,))]
    for d in order:
        for h in range(2):
            start(first(h, d))
    slot = p1_of(y, z, other) * 2 + k
    start(remote(q_ref.at[other], s1.at[slot], s1_send.at[other * n], s1_recv.at[slot], partner))

    swap = remote(pool_hbm, poolv.at[pl.ds(pages, pages)], cx_send.at[0], cx_recv.at[0], partner)
    start(swap)

    loads[1].wait()
    loads[2].wait()
    lane = iota((1, 128), 1)
    lens = jnp.zeros((1, 128), jnp.int32)
    for p in range(prompts):
        lens = jnp.where(lane == p, plen_ref[p], lens)
    need = lax.shift_right_logical(lens + (PAGE - 1), 6).astype(F32)
    grid_r, grid_c = iota((128, 128), 0), iota((128, 128), 1)
    need_t = jnp.transpose(jnp.broadcast_to(need, (128, 128)))
    ends = jnp.sum(jnp.where(grid_r <= grid_c, need_t, 0.0), axis=0, keepdims=True)
    starts = ends - need
    page_r = iota((pages, 128), 0)
    slots = jnp.zeros((pages, 128), jnp.int32)
    for j in range(pages):
        slots = jnp.where(page_r == j, slot_ref[j], slots)
    slots = slots.astype(F32)
    plane = iota((pages, 128), 1)
    owner = jnp.sum(
        jnp.where((plane < prompts) & (slots >= ends), 1.0, 0.0), axis=1, keepdims=True
    )
    used = owner < prompts
    owner = jnp.minimum(owner, prompts - 1.0)
    mine = plane.astype(F32) == owner
    begin = jnp.sum(jnp.where(mine, starts, 0.0), axis=1, keepdims=True)
    length = jnp.sum(jnp.where(mine, lens.astype(F32), 0.0), axis=1, keepdims=True)
    live = jnp.where(used, length - (slots - begin) * PAGE, 0.0)
    info_tx[0] = owner * SAMPLES + jnp.zeros_like(slots)
    info_tx[1] = live + jnp.zeros_like(slots)
    info = remote(info_tx, info_rx, cx_send.at[1], cx_recv.at[1], partner)
    start(info)

    pr, pc = iota((chunk, 2 * n * 16), 0), iota((chunk, 2 * n * 16), 1).astype(F32)
    cell = floor_div(pr, reqs)
    want = cell * 16.0 + (pr.astype(F32) - cell * reqs)
    for d in range(n):
        for kk in range(2):
            slot = lax.rem(p1 + d, n) * 2 + lax.rem(k + kk, 2)
            if d or kk:
                remote(q_ref.at[0], s1.at[slot], s1_send.at[0], s1_recv.at[slot], partner).wait_recv()
    s1v = s1[...].reshape(2 * n * 16, HEAD)
    packed = [
        dot(jnp.where(pc == want + c * 8.0, 1.0, 0.0).astype(BF16), s1v) for c in range(2)
    ]
    agm[p2] = jnp.concatenate(packed, axis=1).astype(BF16)

    def part(src, piece):
        return agm.at[src, pl.ds(piece * half, half)]

    def second(src, s, hop, kind, piece):
        return remote(
            part(src, piece), part(src, piece), ag_send.at[s, kind, piece], ag_recv.at[s, kind, piece],
            mine2((1, -1)[s] * hop),
        )

    def arrived(s, kind, piece):
        src = near(-(1, -1)[s] * (kind + 1))
        second(src, s, 1, kind, piece).wait_recv()
        return src

    for i in range(2):
        for s in range(2):
            start(second(p2, s, 2, 1, i ^ s))
    for i in range(2):
        for s in range(2):
            start(second(p2, s, 1, 0, i ^ s))

    total = n * chunk
    loads[3].wait()
    ids = ids_ref[...].reshape(1, total)
    grid_u = iota((n * n, total), 0).astype(F32)
    grid_e = iota((n * n, total), 1)
    on = floor_div(grid_e, 2 * reqs) == grid_u
    e_in = iota((total, 128), 0)
    e_mod = e_in.astype(F32) - floor_div(e_in, 2 * reqs) * (2 * reqs)
    l_in = iota((1, 128), 1)
    l_div = floor_div(l_in, 2 * reqs)
    l_mod = l_in.astype(F32) - l_div * (2 * reqs)
    spread_e = jnp.where(e_mod == l_mod, 1.0, 0.0).astype(BF16)
    hi = jnp.where(on, lax.shift_right_logical(ids, 5).astype(F32), 0.0).astype(BF16)
    lo = jnp.where(on, (ids & 31).astype(F32), 0.0).astype(BF16)
    table = dot(hi, spread_e) * 32.0 + dot(lo, spread_e)
    nat = jnp.concatenate(
        [
            jnp.sum(
                jnp.where(iota((n, 128), 0).astype(F32) == l_div, table[i * n:(i + 1) * n], 0.0),
                axis=0, keepdims=True,
            )
            for i in range(n)
        ],
        axis=0,
    )
    perm = jnp.zeros((n, 128), F32)
    for i in range(n):
        perm = jnp.where(l_div == float(i), table[i * n:(i + 1) * n], perm)
    ids_m = jnp.where(k == 0, nat, perm)
    info.wait_recv()
    pair = 2 * pages
    sample = (iota((2 * rows, 128), 0) & (SAMPLES - 1)).astype(F32)

    def per_row(i):
        v = jnp.concatenate([info_tx[i], info_rx[i]], axis=0)
        return jnp.broadcast_to(v[:, None, :], (pair, SAMPLES, 128)).reshape(2 * rows, 128)

    target = per_row(0) + sample
    live_c = per_row(1)
    for p in range(n):
        gm[p] = jnp.where(target[:, :chunk] == ids_m[p:p + 1, :chunk], 1.0, 0.0).astype(BF16)

    for i in range(2):
        for s in range(2):
            piece = i ^ s
            src = arrived(s, 1, piece)
            if i == 0:
                start(second(src, s, 2, 3, piece))
            start(second(src, s, 1, 2, piece))
    pick[...] = dot(gm[p2], agm[p2])

    def take(d):
        src = near(d)
        pick[...] += dot(gm[src], agm[src])

    for s in range(2):
        take((-2, 2)[s])
    target_row = jnp.concatenate(
        [jnp.transpose(target[i * 128:(i + 1) * 128])[0:8] for i in range(2 * rows // 128)], axis=1
    )
    live_row = jnp.concatenate(
        [jnp.transpose(live_c[i * 128:(i + 1) * 128])[0:1] for i in range(2 * rows // 128)], axis=1
    )
    both_t = jnp.concatenate([target_row[0:4, :rows], target_row[0:4, rows:]], axis=0)
    swap_t = jnp.concatenate([target_row[0:4, rows:], target_row[0:4, :rows]], axis=0)
    lane8 = iota((8, rows), 1)
    lower = iota((8, rows), 0) >= 4
    lead = jnp.where(lower & (swap_t == both_t), 0.0, 1.0)
    for d in range(1, pages):
        same = pltpu.roll(both_t, d * SAMPLES, 1) == both_t
        cross = pltpu.roll(swap_t, d * SAMPLES, 1) == both_t
        lead = jnp.where((same & (lane8 >= d * SAMPLES)) | (cross & lower), 0.0, lead)
    ids_t = jnp.transpose(jnp.concatenate([ids_m, jnp.zeros((128 - n, 128), F32)], axis=0))
    for p in range(n):
        gt[pl.ds(p * chunk, chunk), :] = jnp.where(
            ids_t[:chunk, p:p + 1] == target_row[0:1], 1.0, 0.0
        ).astype(BF16)
    for i in range(2):
        for s in range(2):
            arrived(s, 0, i ^ s)
    for s in range(2):
        take((-1, 1)[s])
    for i in range(2):
        for s in range(2):
            arrived(s, 2, i ^ s)
    for s in range(2):
        take((-3, 3)[s])
    for s in range(2):
        arrived(s, 3, s)
    take(4)

    loads[4].wait()
    swap.wait_recv()
    blocks = pair // 8
    scores, peaks = [], []
    page_l = lax.shift_right_logical(iota((PAGE, 256), 1) & 127, 4)
    for blk in range(blocks):
        keys = poolv[blk * 8:(blk + 1) * 8].reshape(8 * PAGE, 2 * HEAD)[:, :HEAD]
        sl = slice(blk * 128, (blk + 1) * 128)
        qb = jnp.concatenate([pick[sl, :HEAD], pick[sl, HEAD:]], axis=0).astype(BF16)
        full = dot(keys, qb, 1, 1)
        s = jnp.zeros((PAGE, 256), F32)
        for j in range(8):
            s = jnp.where(page_l == j, full[j * PAGE:(j + 1) * PAGE], s)
        lv = jnp.concatenate([live_row[:, sl]] * 2, axis=1)
        alive = iota((PAGE, 256), 0).astype(F32) < lv
        s = jnp.where(alive, s * scale, NEG)
        scores.append((s, alive))
        m = jnp.max(s, axis=0, keepdims=True)
        peaks.append(jnp.concatenate([m[:, :128], m[:, 128:]], axis=0))
    hb = blocks // 2
    low, high = jnp.concatenate(peaks[:hb], axis=1), jnp.concatenate(peaks[hb:], axis=1)

    both_m = jnp.concatenate([low, low, high, high], axis=0)
    swap_m = jnp.concatenate([high, high, low, low], axis=0)
    top = jnp.where(swap_t == both_t, jnp.maximum(both_m, swap_m), both_m)
    for d in range(1, pages):
        same = pltpu.roll(both_t, d * SAMPLES, 1) == both_t
        cross = pltpu.roll(swap_t, d * SAMPLES, 1) == both_t
        top = jnp.where(same, jnp.maximum(top, pltpu.roll(both_m, d * SAMPLES, 1)), top)
        top = jnp.where(cross, jnp.maximum(top, pltpu.roll(swap_m, d * SAMPLES, 1)), top)

    dens = []
    page_r8 = lax.shift_right_logical(iota((256, 8 * PAGE), 0) & 127, 4)
    own_page = page_r8 == lax.shift_right_logical(iota((256, 8 * PAGE), 1), 6)
    for blk in range(blocks):
        s, alive = scores[blk]
        base = 4 * (blk // hb)
        tb = top[base:base + 2, (blk % hb) * 128:(blk % hb + 1) * 128]
        tb = jnp.concatenate([tb[0:1], tb[1:2]], axis=1)
        w = jnp.where(alive, jnp.exp(s - tb), 0.0)
        dsum = jnp.sum(w, axis=0, keepdims=True)
        dens.append(jnp.concatenate([dsum[:, :128], dsum[:, 128:]], axis=0))
        wt = jnp.transpose(w)
        wt = jnp.concatenate([wt, wt], axis=1)
        wide = jnp.where(own_page, jnp.concatenate([wt] * 4, axis=1), 0.0).astype(BF16)
        values = poolv[blk * 8:(blk + 1) * 8].reshape(8 * PAGE, 2 * HEAD)[:, HEAD:]
        acc = dot(wide, values).astype(BF16)
        accm[blk * 128:(blk + 1) * 128, :HEAD] = acc[:128]
        accm[blk * 128:(blk + 1) * 128, HEAD:] = acc[128:]
    st = jnp.concatenate(
        [
            jnp.concatenate([jnp.where(lead[0:2] > 0.5, top[0:2], 0.0),
                             jnp.where(lead[4:6] > 0.5, top[4:6], 0.0)], axis=1),
            jnp.concatenate(dens, axis=1),
            jnp.concatenate([lead[0:1], lead[4:5]], axis=1),
            jnp.zeros((3, 2 * rows), F32),
        ],
        axis=0,
    )
    stats[...] = jnp.concatenate(split3(st), axis=0).astype(BF16)

    sub8 = iota((8, 128), 0)

    def sums(d):
        g = gt[pl.ds(pl.multiple_of(near(d) * chunk, chunk), chunk), :]
        acc = dot(g, accm[...])
        ml = dot(stats[...], g, 1, 1)
        ml = ml[0:8] + ml[8:16] + ml[16:24]
        ml = jnp.concatenate([ml, jnp.zeros((8, 128 - chunk), F32)], axis=1)
        return acc, jnp.where((sub8 < 2) & (ml[4:5] < 0.5), NEG, ml)

    def ring(s, kind, src, dst, hop):
        to = mine2((1, -1)[s] * hop)
        return (
            remote(src[0], dst, rs_send.at[s, kind], rs_recv.at[s, kind], to),
            remote(src[1], rx_ml.at[s, kind], rm_send.at[s, kind], rm_recv.at[s, kind], to),
        )

    def landed(s, kind, dst):
        for copy in ring(s, kind, (dst, rx_ml.at[s, kind]), dst, 1):
            copy.wait_recv()

    def store(i, d):
        acc, ml = sums(d)
        tx_acc[i] = acc.astype(BF16)
        tx_ml[i] = ml

    store(2, 4)
    for s in range(2):
        for copy in ring(s, 1, (tx_acc.at[2, pl.ds(s * half, half)], tx_ml.at[2]), a4_acc.at[s], 2):
            start(copy)
    for s in range(2):
        store(s, (3, -3)[s])
        for copy in ring(s, 0, (tx_acc.at[s], tx_ml.at[s]), a3_acc.at[s], 1):
            start(copy)
    for s in range(2):
        store(3 + s, (1, -1)[s])
        for copy in ring(s, 2, (tx_acc.at[3 + s], tx_ml.at[3 + s]), b_acc.at[s, 0], 1):
            start(copy)

    def weigh(mls):
        out = []
        for c in range(2):
            mx = functools.reduce(jnp.maximum, [m[c:c + 1] for m in mls])
            w = [jnp.exp(m[c:c + 1] - mx) for m in mls]
            dn = functools.reduce(jnp.add, [a * m[2 + c:3 + c] for a, m in zip(w, mls)])
            out.append((w, mx, dn))
        return out

    def columns(items):
        return jnp.transpose(
            jnp.concatenate(items + [jnp.zeros((128 - len(items), 128), F32)], axis=0)
        )

    lane128 = iota((8, 128), 1)
    own2 = [sums(2), sums(-2)]
    for s in range(2):
        acc, ml = own2[s]
        landed(s, 0, a3_acc.at[s])
        landed(s, 1, a4_acc.at[s])
        inside = (lane128 < half) if s == 0 else (lane128 >= half)
        ml4 = jnp.where((sub8 < 2) & jnp.logical_not(inside), NEG, rx_ml[s, 1])
        mls = [ml, rx_ml[s, 0], ml4]
        st = weigh(mls)
        cols = columns(st[0][0] + st[1][0])
        outs = []
        for c in range(2):
            sl = slice(c * HEAD, (c + 1) * HEAD)
            a3 = a3_acc[s, :, sl].astype(F32)
            a4 = a4_acc[s, :, sl].astype(F32)
            v = acc[:, sl] * cols[:chunk, 3 * c:3 * c + 1] + a3 * cols[:chunk, 3 * c + 1:3 * c + 2]
            add = a4 * cols[s * half:(s + 1) * half, 3 * c + 2:3 * c + 3]
            if s == 0:
                v = jnp.concatenate([v[:half] + add, v[half:]], axis=0)
            else:
                v = jnp.concatenate([v[:half], v[half:] + add], axis=0)
            outs.append(v)
        tx_acc[5 + s] = jnp.concatenate(outs, axis=1).astype(BF16)
        tx_ml[5 + s] = jnp.concatenate(
            [st[0][1], st[1][1], st[0][2], st[1][2], jnp.zeros((4, 128), F32)], axis=0
        )
        for copy in ring(s, 3, (tx_acc.at[5 + s], tx_ml.at[5 + s]), b_acc.at[s, 1], 2):
            start(copy)
    home_acc, home_ml = sums(0)

    loads[5].wait()
    loads[6].wait()
    loads[7].wait()
    qown = jnp.concatenate([q_ref[0], q_ref[1]], axis=0)
    tails = tailv[...].reshape(reqs * 128, 2 * HEAD)
    row32 = iota((32, 128), 0) & 7
    ts, tl = [], []
    for r in range(reqs):
        ok = (row32 == r) & (iota((32, 128), 1) < tlen_ref[r])
        tl.append(ok)
        ts.append(jnp.where(ok, dot(qown, tails[r * 128:(r + 1) * 128, :HEAD], 1, 1) * scale, NEG))
    fresh = nk_ref[...].astype(F32)
    pad = jnp.zeros((8 - reqs, 2 * HEAD), F32)
    news = jnp.concatenate([fresh[:, 0, :], pad, fresh[:, 1, :], pad], axis=0).astype(BF16)
    nrow, ncol = iota((32, 16), 0), iota((32, 16), 1)
    nlive = ((nrow & 7) == (ncol & 7)) & (lax.shift_right_logical(ncol, 3) <= lax.shift_right_logical(nrow, 4))
    ns = jnp.where(nlive, dot(qown, news[:, :HEAD], 1, 1) * scale, NEG)
    peak = jnp.max(ns, axis=1, keepdims=True)
    peak = jnp.maximum(peak, jnp.max(functools.reduce(jnp.maximum, ts), axis=1, keepdims=True))
    nw = jnp.where(nlive, jnp.exp(ns - peak), 0.0)
    tw = [jnp.where(ok, jnp.exp(t - peak), 0.0) for t, ok in zip(ts, tl)]
    own_den = jnp.sum(nw, axis=1, keepdims=True)
    own_den += jnp.sum(functools.reduce(jnp.add, tw), axis=1, keepdims=True)
    own_acc[...] = dot(nw.astype(BF16), news[:, HEAD:]) + dot(
        jnp.concatenate(tw, axis=1).astype(BF16), tails[:, HEAD:]
    )
    own_st[...] = jnp.where(iota((32, 128), 1) == 0, peak, own_den)

    for s in range(2):
        landed(s, 2, b_acc.at[s, 0])
    for s in range(2):
        landed(s, 3, b_acc.at[s, 1])
    st = weigh([home_ml] + [rx_ml[s, kind] for s in range(2) for kind in (2, 3)])
    cols = columns(st[0][0] + st[1][0] + [st[0][1], st[1][1], st[0][2], st[1][2]])[:chunk]
    lane_c = iota((chunk, 128), 1)
    t2v = jnp.zeros((2 * n * 16, HEAD + 128), F32)
    sr, sc = iota((2 * n * 16, chunk), 0), iota((2 * n * 16, chunk), 1)
    for c in range(2):
        sl = slice(c * HEAD, (c + 1) * HEAD)
        acc = home_acc[:, sl] * cols[:, 5 * c:5 * c + 1]
        for i in range(4):
            acc += b_acc[i // 2, i % 2, :, sl].astype(F32) * cols[:, 5 * c + 1 + i:5 * c + 2 + i]
        parts = split3(cols[:, 10 + c:11 + c]) + split3(cols[:, 12 + c:13 + c])
        tile = jnp.zeros((chunk, 128), F32)
        for i, col in enumerate(parts):
            tile = jnp.where(lane_c == i, col, tile)
        rowsrc = jnp.concatenate([acc, tile], axis=1).astype(BF16)
        inner = (sr & 15) - c * 8
        pick_rows = (inner >= 0) & (inner < reqs) & (lax.shift_right_logical(sr, 4) * reqs + inner == sc)
        t2v += dot(jnp.where(pick_rows, 1.0, 0.0).astype(BF16), rowsrc)
    t2[...] = t2v.astype(BF16).reshape(2 * n, 16, HEAD + 128)

    def home(pos, kk):
        return remote(
            t2.at[pos * 2 + kk], r2.at[k, p1], t2_send.at[pos * 2 + kk], t2_recv.at[k, p1],
            mine1(pos, kk),
        )

    for d in order:
        pos = lax.rem(p1 + d, n)
        for kk in range(2):
            start(home(pos, kk))
    start(home(p1, other))
    r2[k, p1] = t2[p1 * 2 + k]
    loads[8].wait()
    for d in range(1, n):
        for h in range(2):
            src = lax.rem((y, z)[h] + d, n)
            remote(t2.at[0], r2.at[h, src], t2_send.at[0], t2_recv.at[h, src], partner).wait_recv()
    src = p1_of(y, z, other)
    remote(t2.at[0], r2.at[other, src], t2_send.at[0], t2_recv.at[other, src], partner).wait_recv()

    heads = []
    for h in range(2):
        cells = [r2[h, i].astype(F32) for i in range(n)]
        ms = [t[:, HEAD:HEAD + 1] + t[:, HEAD + 1:HEAD + 2] + t[:, HEAD + 2:HEAD + 3] for t in cells]
        ds = [t[:, HEAD + 3:HEAD + 4] + t[:, HEAD + 4:HEAD + 5] + t[:, HEAD + 5:HEAD + 6] for t in cells]
        ms.append(own_st[h * 16:(h + 1) * 16, 0:1])
        ds.append(own_st[h * 16:(h + 1) * 16, 1:2])
        accs = [t[:, :HEAD] for t in cells] + [own_acc[h * 16:(h + 1) * 16]]
        mx = functools.reduce(jnp.maximum, ms)
        num = jnp.zeros((16, HEAD), F32)
        dn = jnp.zeros((16, 1), F32)
        for m, dd, acc in zip(ms, ds, accs):
            w = jnp.exp(m - mx)
            num += acc * w
            dn += dd * w
        heads.append(num / dn)
    att = jnp.concatenate(
        [jnp.concatenate([a[0:8], a[8:16]], axis=1) for a in heads], axis=0
    ).astype(BF16)

    hw = wv.shape[1] // 2
    even = x + 1 - 2 * lax.rem(x, 2)
    odd = nx - 1 - x
    if nx == 1:
        for i in range(2):
            out_ref[0, i] = dot(att, wv[:, i * hw:(i + 1) * hw]).astype(BF16)
            out_ref[1, i] = jnp.zeros((16, hw), BF16)
    else:
        def trade(i, turn):
            src = ar.at[i] if turn == 0 else out_ref.at[0, i]
            dst = ar_rx.at[i] if turn == 0 else out_ref.at[1, i]
            to = even if (i + turn) % 2 == 0 else odd
            return remote(src, dst, ar_send.at[turn, i], ar_recv.at[turn, i], (to, b))

        for i in range(2):
            ar[i] = dot(att, wv[:, i * hw:(i + 1) * hw]).astype(BF16)
            start(trade(i, 0))
        for i in range(2):
            trade(i, 0).wait_recv()
            out_ref[0, i] = (ar[i].astype(F32) + ar_rx[i].astype(F32)).astype(BF16)
            if nx > 2:
                start(trade(i, 1))
            else:
                out_ref[1, i] = jnp.zeros((16, hw), BF16)
        for i in range(2):
            if nx > 2:
                trade(i, 1).wait_recv()
    for load in loads[9:]:
        load.wait()
    for copy in pending:
        copy.wait_send()


def finish(sum_ref, hid_ref, gain_ref, score_ref, out_ref, sc_ref):
    reqs = hid_ref.shape[0]
    raw = hid_ref[...].astype(F32)
    total = jnp.concatenate(
        [sum_ref[0, i].astype(F32) + sum_ref[1, i].astype(F32) for i in range(2)], axis=1
    )
    hid = [(raw[:, i, :] + total[8 * i:8 * i + reqs]).astype(BF16).astype(F32) for i in range(2)]
    out_ref[...] = jnp.stack(hid, axis=1).astype(BF16)
    last = hid[1]
    normed = last * lax.rsqrt(jnp.mean(last * last, axis=1, keepdims=True) + 1e-06) * gain_ref[...]
    score = jnp.sum(normed * score_ref[...], axis=1, keepdims=True)
    tile = jnp.concatenate([jnp.broadcast_to(score, (reqs, 128)), jnp.zeros((128 - reqs, 128), F32)], axis=0)
    sc_ref[...] = jnp.transpose(tile)[0, :reqs]


def p1_of(y, z, h):
    return y + h * (z - y)


def body(n, nx, prefix_pool, slot_page, prompt_len, request_ids, tail_len, tail_cache, queries,
         new_kv, hidden, out_weight, norm_gain, score_weight):
    pages = prefix_pool.shape[1]
    reqs, width = hidden.shape[0], hidden.shape[2]
    chunk = n * 2 * reqs
    rows = pages * SAMPLES
    total = n * chunk
    vm = pl.BlockSpec(memory_space=pltpu.VMEM)
    hbm = pl.BlockSpec(memory_space=pl.ANY)
    dma = pltpu.SemaphoreType.DMA
    sums = pl.pallas_call(
        functools.partial(kernel, n, nx, reqs, pages),
        out_shape=(
            pltpu.VMEM((2, 2, 16, width // 2), BF16),
            pltpu.VMEM(hidden.shape, BF16),
            pltpu.VMEM((1, width), F32),
            pltpu.VMEM((1, width), F32),
        ),
        in_specs=[hbm] * 12,
        out_specs=(vm,) * 4,
        scratch_shapes=[
            pltpu.SMEM(slot_page.shape, jnp.int32),
            pltpu.SMEM(prompt_len.shape, jnp.int32),
            pltpu.SMEM(tail_len.shape, jnp.int32),
            pltpu.VMEM(request_ids.shape, jnp.int32),
            pltpu.VMEM(queries.shape, BF16),
            pltpu.VMEM(new_kv.shape[1:], BF16),
            pltpu.VMEM((2, 16, HEAD), BF16),
            pltpu.VMEM((2 * pages, PAGE, 2 * HEAD), BF16),
            pltpu.VMEM((reqs, 128, 2 * HEAD), BF16),
            pltpu.VMEM((2 * HEAD, width), BF16),
            pltpu.VMEM((2 * n, 16, HEAD), BF16),
            pltpu.VMEM((n, chunk, 512), BF16),
            pltpu.VMEM((n, 2 * rows, chunk), BF16),
            pltpu.VMEM((total, 2 * rows), BF16),
            pltpu.VMEM((2 * rows, 512), F32),
            pltpu.VMEM((2 * rows, 512), BF16),
            pltpu.VMEM((24, 2 * rows), BF16),
            pltpu.VMEM((2, pages, 128), F32),
            pltpu.VMEM((2, pages, 128), F32),
            pltpu.VMEM((7, chunk, 512), BF16),
            pltpu.VMEM((7, 8, 128), F32),
            pltpu.VMEM((2, chunk, 512), BF16),
            pltpu.VMEM((2, chunk // 2, 512), BF16),
            pltpu.VMEM((2, 2, chunk, 512), BF16),
            pltpu.VMEM((2, 4, 8, 128), F32),
            pltpu.VMEM((2 * n, 16, HEAD + 128), BF16),
            pltpu.VMEM((2, n, 16, HEAD + 128), BF16),
            pltpu.VMEM((32, HEAD), F32),
            pltpu.VMEM((32, 128), F32),
            pltpu.VMEM((2, 16, width // 2), BF16),
            pltpu.VMEM((2, 16, width // 2), BF16),
            dma((12,)), dma((2 * n,)), dma((2 * n,)),
            dma((2, 4, 2)), dma((2, 4, 2)),
            dma((2,)), dma((2,)),
            dma((2, 4)), dma((2, 4)), dma((2, 4)), dma((2, 4)),
            dma((2 * n,)), dma((2, n)), dma((2, 2)), dma((2, 2)),
        ],
        compiler_params=pltpu.CompilerParams(collective_id=0, has_side_effects=True),
    )(
        slot_page, prompt_len, tail_len, request_ids, queries, new_kv[0],
        prefix_pool[0], tail_cache[0], out_weight, hidden, norm_gain.reshape(1, -1),
        score_weight.reshape(1, -1),
    )
    return pl.pallas_call(
        finish,
        out_shape=(jax.ShapeDtypeStruct(hidden.shape, BF16), jax.ShapeDtypeStruct((reqs,), F32)),
        in_specs=[vm] * 4,
        out_specs=(vm, vm),
    )(*(pltpu.with_memory_space_constraint(a, pltpu.VMEM) for a in sums))


def solution(mesh):
    nx = mesh.shape["kv"]
    n = int(round((mesh.shape["blk"] // 2) ** 0.5))
    in_specs = (
        P("kv", "blk", None, None),
        P("blk"),
        P(),
        P(),
        P("blk"),
        P("kv", "blk", None, None),
        P("blk", None, "kv"),
        P("kv", "blk", None, None),
        P("blk", None, None),
        P("kv", None),
        P(),
        P(),
    )
    out_specs = (P("blk", None, None), P("blk"))
    return jax.shard_map(
        functools.partial(body, n, nx), mesh=mesh, in_specs=in_specs, out_specs=out_specs, check_vma=False
    )
```
